32 devices in a mesh: dp: 16 (over z, y, core), tensor: 2 (over x).
Axes of the slice: x: 2, y: 2, z: 4, core: 2. Of those that a mesh axis runs over, the one named last changes fastest.
Arguments:
- tokens: bfloat16 [8192, 896], P('dp'), may hold values from -6 to 6
- out_grad: bfloat16 [8192, 896], P('dp'), may hold values from -6 to 6
- doc_lengths: int32 [16, 8], P('dp'), may hold values from 0 to 512, as said below
- q_weight: bfloat16 [896, 896], P(None, 'tensor'), may hold values from -0.1875 to 0.1875
- k_weight: bfloat16 [896, 128], P(None, 'tensor'), may hold values from -0.1875 to 0.1875
- v_weight: bfloat16 [896, 128], P(None, 'tensor'), may hold values from -0.1875 to 0.1875
- q_bias: bfloat16 [14, 64], P('tensor'), may hold values from -3 to 3
- k_bias: bfloat16 [2, 64], P('tensor'), may hold values from -3 to 3
- v_bias: bfloat16 [2, 64], P('tensor'), may hold values from -3 to 3
- o_weight: bfloat16 [896, 896], P('tensor'), may hold values from -1 to 1
- attn_gain: bfloat16 [896], replicated, may hold values from 0.099609375 to 1.8984375
- ffn_gain: bfloat16 [896], replicated, may hold values from 0.099609375 to 1.8984375
- gate_weight: bfloat16 [896, 4864], P(None, 'tensor'), may hold values from -0.1875 to 0.1875
- up_weight: bfloat16 [896, 4864], P(None, 'tensor'), may hold values from -0.1875 to 0.1875
- down_weight: bfloat16 [4864, 896], P('tensor'), may hold values from -0.078125 to 0.078125
Outputs:
- layer_out: bfloat16 [8192, 896], P('dp')
- tokens_grad: bfloat16 [8192, 896], P('dp')
- q_weight_grad: float32 [896, 896], P('dp', 'tensor')
- k_weight_grad: float32 [896, 128], P('dp', 'tensor')
- v_weight_grad: float32 [896, 128], P('dp', 'tensor')
- q_bias_grad: float32 [14, 64], P('tensor', 'dp')
- k_bias_grad: float32 [2, 64], P('tensor')
- v_bias_grad: float32 [2, 64], P('tensor', 'dp')
- o_weight_grad: float32 [896, 896], P('tensor', 'dp')
- attn_gain_grad: float32 [896], P('dp')
- ffn_gain_grad: float32 [896], P('dp')
- gate_weight_grad: float32 [896, 4864], P('dp', 'tensor')
- up_weight_grad: float32 [896, 4864], P('dp', 'tensor')
- down_weight_grad: float32 [4864, 896], P('tensor', 'dp')
The draws below stay inside these ranges and needn't reach their ends.
Inputs may be any that keep to these rules, and one draw needn't show every extreme that they name: `doc_lengths`: each row lists the sequences of one token buffer, zeros after the last; a row's sum is at most 512, every nonzero entry is 200 or more, the first entry is nonzero, and in every draw some buffer holds one sequence of exactly 512 tokens.
All inputs are finite; a program needn't handle non-finite values.
Results may differ from the reference program's by a relative error of at most 0.024.
Values sent between devices are 32-bit elements; how exact they have to be, the bound alone decides.
No kernel may reach another device: no remote copies, remote signals or barrier semaphores. Data moves between devices by JAX's collectives and lax.ppermute only.
A program may use at most 192 MiB of HBM per device.

```python
import math
import jax
import jax.numpy as jnp
from jax import lax

D = 896
HQ = 14
KVH = 2
HD = 64
FF = 4864
TOK_DEV = 512
MIN_LEN = 200
SLOTS = 8
TOKENS = 8192
N_DP = 16


def draw_doc_lengths(key, part):
    key_size, key_shift, key_full = jax.random.split(key, 3)
    spread_raw = jax.random.randint(key_size, (N_DP, SLOTS), 0, TOK_DEV - MIN_LEN + 1)
    shifts = jax.random.randint(key_shift, (N_DP, SLOTS), 0, 4)
    doc_sizes = MIN_LEN + spread_raw // jnp.left_shift(jnp.ones_like(shifts), shifts)
    doc_ends = jnp.cumsum(doc_sizes, axis=1)
    doc_sizes = jnp.where(doc_ends <= TOK_DEV, doc_sizes, 0)
    chosen = jax.random.randint(key_full, (), 0, N_DP)
    full_row = jnp.where(jnp.arange(SLOTS) == 0, TOK_DEV, 0)
    doc_sizes = jnp.where((jnp.arange(N_DP) == chosen)[:, None], full_row[None, :], doc_sizes)
    return doc_sizes.astype(jnp.int32)


def spiked(array, own_key, source, target, blocks, factor):
    def block_of(axis_at):
        return (jnp.arange(array.shape[axis_at]) // (array.shape[axis_at] // blocks)).reshape((-1,) + (1,) * (array.ndim - 1 - axis_at))

    first = jax.random.permutation(own_key, blocks)[block_of(target)]
    far = (block_of(target) + blocks // 2) % blocks
    return jnp.where((block_of(source) == first) | (block_of(source) == far), factor * array, array)


def block_levels(rng, shape, shards, low, top_value):
    factor_of = 1.0
    for position, blocks in shards:
        draws = jax.random.uniform(jax.random.fold_in(jax.random.fold_in(rng, 6), position), (blocks,), jnp.float32, low / len(shards), top_value / len(shards))
        factor_of = factor_of * jnp.repeat(jnp.exp(draws), shape[position] // blocks).reshape((-1,) + (1,) * (len(shape) - 1 - position))
    return factor_of


def gaussian(stream_key, extent, scale, limit, cuts=(), kind=jnp.bfloat16):
    level = block_levels(stream_key, extent, cuts, -0.22, 0.18) if cuts else 1.0
    values = jax.random.normal(stream_key, extent, jnp.float32) * scale * level
    return jnp.minimum(jnp.maximum(values, -limit), limit).astype(kind)


def gaussian_with(stream_key, extent, scale, bound, cuts, heavy, held_as=jnp.bfloat16):
    entries = scale * jax.random.normal(stream_key, extent, jnp.float32)
    if cuts:
        entries = entries * block_levels(stream_key, extent, cuts, -0.22, 0.18)
    return jnp.clip(spiked(entries, jax.random.fold_in(stream_key, 3), *heavy), -bound, bound).astype(held_as)


def setup_inputs(seed: int = 0) -> dict:
    arg_keys = jax.random.split(jax.random.key(seed), 16)
    return {
        "tokens": gaussian_with(arg_keys[0], (TOKENS, D), 1.0, 6.0, ((0, 16),), (0, 1, 16, 2.0)),
        "out_grad": gaussian_with(arg_keys[1], (TOKENS, D), 1.0, 6.0, ((0, 16),), (0, 1, 16, 2.0)),
        "doc_lengths": draw_doc_lengths(jax.random.fold_in(arg_keys[15], 71), 0),
        "q_weight": gaussian(arg_keys[3], (D, HQ * HD), D ** -0.5, 0.1875, ((1, 2),)),
        "k_weight": gaussian(arg_keys[4], (D, KVH * HD), D ** -0.5, 0.1875, ((1, 2),)),
        "v_weight": gaussian(arg_keys[5], (D, KVH * HD), D ** -0.5, 0.1875, ((1, 2),)),
        "q_bias": gaussian(arg_keys[6], (HQ, HD), 0.5, 3.0, ((0, 2),)),
        "k_bias": gaussian(arg_keys[7], (KVH, HD), 0.5, 3.0, ((0, 2),)),
        "v_bias": gaussian(arg_keys[8], (KVH, HD), 0.5, 3.0, ((0, 2),)),
        "o_weight": gaussian(arg_keys[9], (HQ * HD, D), (HQ * HD // 32) ** -0.5, 1.0, ((0, 2),)),
        "attn_gain": jnp.clip(1.0 + 0.18 * jax.random.normal(arg_keys[10], (D,), jnp.float32), 0.099609375, 1.8984375).astype(jnp.bfloat16),
        "ffn_gain": jnp.clip(1.0 + 0.18 * jax.random.normal(arg_keys[11], (D,), jnp.float32), 0.099609375, 1.8984375).astype(jnp.bfloat16),
        "gate_weight": gaussian(arg_keys[12], (D, FF), D ** -0.5, 0.1875, ((1, 2),)),
        "up_weight": gaussian(arg_keys[13], (D, FF), D ** -0.5, 0.1875, ((1, 2),)),
        "down_weight": gaussian(arg_keys[14], (FF, D), FF ** -0.5, 0.078125, ((0, 2),)),
    }


@jax.custom_vjp
def low(v):
    return lax.optimization_barrier(v.astype(jnp.bfloat16)).astype(jnp.float32)

@jax.custom_vjp
def low_back(v):
    return v

def low_keep(v):
    return (low(v), None)

def low_pass(kept, grad):
    return (grad,)

def back_keep(v):
    return (v, None)

def back_low(kept, grad):
    return (low(grad),)
low.defvjp(low_keep, low_pass)
low_back.defvjp(back_keep, back_low)
norm_eps = 1e-06
rope_base = 1000000.0

def layout(lengths, row_total):
    doc_ends = jnp.cumsum(lengths).astype(jnp.int32)
    places = jnp.arange(row_total, dtype=jnp.int32)
    passed = (places[:, None] >= doc_ends[None, :]).astype(jnp.int32)
    segment = lax.optimization_barrier(jnp.sum(passed, axis=1)).astype(jnp.int32)
    begins = lax.optimization_barrier(jnp.sum(passed * lengths[None, :], axis=1)).astype(jnp.int32)
    alive = places < doc_ends[-1]
    return (segment, places - begins, alive)

def rotary(positions, width):
    half_width = width // 2
    inv_freq = jnp.exp(jnp.arange(half_width, dtype=jnp.float32) * (-2.0 * math.log(rope_base) / width))
    angles = positions.astype(jnp.float32)[:, None] * inv_freq[None, :]
    return (jnp.cos(angles), jnp.sin(angles))

def rotate_pairs(heads_in, cosine, sine_table):
    half_width = heads_in.shape[-1] // 2
    front_half = heads_in[..., :half_width]
    back_half = heads_in[..., half_width:]
    cos_rows = cosine[:, None, :]
    sin_rows = sine_table[:, None, :]
    return jnp.concatenate([front_half * cos_rows - back_half * sin_rows, back_half * cos_rows + front_half * sin_rows], axis=-1)

def norm_rows(values_in, gain):
    factor = lax.rsqrt(lax.optimization_barrier(jnp.mean(values_in * values_in, axis=-1, keepdims=True)) + norm_eps)
    return values_in * factor * gain

def block_forward(weights, inputs, segment, cosine, sine_table, alive):
    q_weight, k_weight, v_weight, q_bias, k_bias, v_bias, o_weight, attn_gain, ffn_gain, gate_weight, up_weight, down_weight = weights
    row_total = inputs.shape[0]
    exact_mode = lax.Precision.HIGHEST
    normed = low(norm_rows(inputs, attn_gain))
    query_pre = low_back(jnp.dot(normed, q_weight, precision=exact_mode) + q_bias.reshape(-1))
    key_pre = low_back(jnp.dot(normed, k_weight, precision=exact_mode) + k_bias.reshape(-1))
    values = low(low_back(jnp.dot(normed, v_weight, precision=exact_mode) + v_bias.reshape(-1)))
    queries = low(rotate_pairs(query_pre.reshape(row_total, HQ, HD), cosine, sine_table))
    key_rows = low(rotate_pairs(key_pre.reshape(row_total, KVH, HD), cosine, sine_table))
    value_rows = values.reshape(row_total, KVH, HD)
    grouped = queries.reshape(row_total, KVH, HQ // KVH, HD)
    block_rows = min(512, row_total)
    places = jnp.arange(row_total, dtype=jnp.int32)
    score_scale = HD ** (-0.5)

    def attend(start_row):
        query_rows = lax.dynamic_slice_in_dim(grouped, start_row, block_rows, 0)
        seg_rows = lax.dynamic_slice_in_dim(segment, start_row, block_rows, 0)
        row_places = start_row + jnp.arange(block_rows, dtype=jnp.int32)
        scores = low_back(jnp.einsum('qkgd,skd->kgqs', query_rows, key_rows, precision=exact_mode) * score_scale)
        allowed = (seg_rows[:, None] == segment[None, :]) & (row_places[:, None] >= places[None, :])
        scores = jnp.where(allowed, scores, -1e+30)
        attn_probs = jax.nn.softmax(scores, axis=-1)
        return jnp.einsum('kgqs,skd->qkgd', low(attn_probs), value_rows, precision=exact_mode)
    block_starts = jnp.arange(0, row_total, block_rows, dtype=jnp.int32)
    mixed_heads = lax.map(jax.checkpoint(attend), block_starts).reshape(row_total, HQ * HD)
    mixed_heads = low(low_back(mixed_heads))
    residual = inputs + low_back(jnp.dot(mixed_heads, o_weight, precision=exact_mode))
    normed_two = low(norm_rows(residual, ffn_gain))
    gate_act = low_back(jnp.dot(normed_two, gate_weight, precision=exact_mode))
    up_act = low_back(jnp.dot(normed_two, up_weight, precision=exact_mode))
    hidden_act = low(jax.nn.silu(gate_act) * up_act)
    block_out = residual + low_back(jnp.dot(hidden_act, down_weight, precision=exact_mode))
    return jnp.where(alive[:, None], block_out, inputs)

def reference(tokens, out_grad, doc_lengths, q_weight, k_weight, v_weight, q_bias, k_bias, v_bias, o_weight, attn_gain, ffn_gain, gate_weight, up_weight, down_weight):
    params = tuple((weight_arr.astype(jnp.float32) for weight_arr in (q_weight, k_weight, v_weight, q_bias, k_bias, v_bias, o_weight, attn_gain, ffn_gain, gate_weight, up_weight, down_weight)))
    token_blocks = tokens.reshape(N_DP, TOK_DEV, D)
    grad_blocks = out_grad.reshape(N_DP, TOK_DEV, D)

    def one_device(totals, inputs):
        token_rows, grad_rows, lengths = inputs
        segment, positions, alive = layout(lengths.astype(jnp.int32), TOK_DEV)
        cosine, sine_table = rotary(positions, HD)

        def forward(start_rows, *weights):
            return block_forward(weights, start_rows, segment, cosine, sine_table, alive)
        result, pullback = jax.vjp(forward, token_rows.astype(jnp.float32), *params)
        grads = pullback(grad_rows.astype(jnp.float32))
        totals = tuple((running + addend for running, addend in zip(totals, grads[1:])))
        return (totals, (result.astype(jnp.bfloat16), grads[0].astype(jnp.bfloat16)))
    zero_grads = tuple((jnp.zeros(weight_arr.shape, jnp.float32) for weight_arr in params))
    totals, (results, token_grads) = lax.scan(one_device, zero_grads, (token_blocks, grad_blocks, doc_lengths))
    return (results.reshape(TOKENS, D), token_grads.reshape(TOKENS, D), totals[0], totals[1], totals[2], totals[3], totals[4], totals[5], totals[6], totals[7], totals[8], totals[9], totals[10], totals[11])
```

```python
import math

import jax
import jax.numpy as jnp
from jax import lax
from jax.sharding import PartitionSpec as P

HD = 64


norm_eps = 1e-06
rope_base = 1000000.0


def layout(lengths, row_total):
    doc_ends = jnp.cumsum(lengths)
    places = jnp.arange(row_total, dtype=jnp.int32)
    passed = (places[:, None] >= doc_ends[None, :]).astype(jnp.int32)
    segment = jnp.sum(passed, axis=1)
    begins = jnp.sum(passed * lengths[None, :], axis=1)
    alive = places < doc_ends[-1]
    return (segment, places - begins, alive)


def rotary(positions, width):
    half_width = width // 2
    inv_freq = jnp.exp(
        jnp.arange(half_width, dtype=jnp.float32) * (-2.0 * math.log(rope_base) / width)
    )
    angles = positions.astype(jnp.float32)[:, None] * inv_freq[None, :]
    return (jnp.cos(angles), jnp.sin(angles))


def rotate_pairs(heads_in, cosine, sine_table):
    half_width = heads_in.shape[-1] // 2
    front_half = heads_in[..., :half_width]
    back_half = heads_in[..., half_width:]
    cos_rows = cosine[:, None, :]
    sin_rows = sine_table[:, None, :]
    return jnp.concatenate(
        [
            front_half * cos_rows - back_half * sin_rows,
            back_half * cos_rows + front_half * sin_rows,
        ],
        axis=-1,
    )


def norm_back(inputs, factor, gain, upstream):
    scaled = upstream * gain
    return factor * scaled - inputs * factor**3 * jnp.mean(scaled * inputs, axis=-1, keepdims=True)


def swap_tensor(rows):
    size = lax.axis_size("tensor")
    return lax.ppermute(rows, "tensor", [(i, i ^ 1) for i in range(size)])


def swap_dp(rows, bit):
    size = lax.axis_size("dp")
    return lax.ppermute(rows, "dp", [(i, i ^ (1 << bit)) for i in range(size)])


def dest_columns(width, order):
    steps = len(order)
    blocks = 1 << steps
    block = width // blocks
    own = lax.axis_index("dp")
    places = jnp.arange(width, dtype=jnp.int32)
    spot = places // block
    flip = jnp.zeros_like(spot)
    for j, bit in enumerate(order):
        flip = flip + (((spot >> (steps - 1 - j)) & 1) << bit)
    source = (own ^ flip) * block + places % block
    chosen = (jnp.arange(width, dtype=jnp.int32)[:, None] == source[None, :]).astype(jnp.bfloat16)
    return chosen[:, : width // 2], chosen[:, width // 2 :]


def pick(rows, chosen):
    return jnp.dot(rows, chosen, preferred_element_type=jnp.float32).astype(jnp.bfloat16)


def scatter_sum(kept_rows, sent_rows, features, order):
    sent = jnp.einsum("td,tf->df", sent_rows, features, preferred_element_type=jnp.float32)
    sent = swap_dp(sent, order[0])
    total = jnp.einsum("td,tf->df", kept_rows, features, preferred_element_type=jnp.float32) + sent
    for bit in order[1:]:
        half = total.shape[0] // 2
        total = total[:half] + swap_dp(total[half:], bit)
    return total


def on_device(
    tokens,
    out_grad,
    doc_lengths,
    q_weight,
    k_weight,
    v_weight,
    q_bias,
    k_bias,
    v_bias,
    o_weight,
    attn_gain,
    ffn_gain,
    gate_weight,
    up_weight,
    down_weight,
):
    row_total, width = tokens.shape
    local_heads = q_weight.shape[1] // HD
    local_kv = k_weight.shape[1] // HD
    group_size = local_heads // local_kv
    dp_size = lax.axis_size("dp")
    dp_bits = dp_size.bit_length() - 1
    ffn_order = tuple(range(dp_bits))
    attn_order = (0,) + tuple(range(2, dp_bits)) + (1,)
    own = lax.axis_index("dp")
    score_scale = HD ** (-0.5)
    segment, positions, alive = layout(doc_lengths[0], row_total)
    cosine, sine_table = rotary(positions, HD)
    alive_rows = alive.astype(jnp.float32)[:, None]
    places = jnp.arange(row_total, dtype=jnp.int32)
    inputs = tokens.astype(jnp.float32)
    gain_one = attn_gain.astype(jnp.float32)
    gain_two = ffn_gain.astype(jnp.float32)
    factor_one = lax.rsqrt(jnp.mean(inputs * inputs, axis=-1, keepdims=True) + norm_eps)
    normed = (inputs * factor_one * gain_one).astype(jnp.bfloat16)
    qkv_weight = jnp.concatenate([q_weight, k_weight, v_weight], axis=1)
    qkv_bias = jnp.concatenate([q_bias.reshape(-1), k_bias.reshape(-1), v_bias.reshape(-1)])
    qkv = jnp.dot(normed, qkv_weight, preferred_element_type=jnp.float32) + qkv_bias.astype(jnp.float32)
    q_width = local_heads * HD
    k_width = local_kv * HD
    value_rows = qkv[:, q_width + k_width :].astype(jnp.bfloat16).reshape(row_total, local_kv, HD)
    turned = rotate_pairs(
        qkv[:, : q_width + k_width].reshape(row_total, local_heads + local_kv, HD), cosine, sine_table
    ).astype(jnp.bfloat16)
    queries = turned[:, :local_heads].reshape(row_total, local_kv, group_size, HD)
    key_rows = turned[:, local_heads:]
    allowed = (segment[:, None] == segment[None, :]) & (places[:, None] >= places[None, :])
    scores = jnp.einsum("qkgd,skd->kgqs", queries, key_rows, preferred_element_type=jnp.float32) * score_scale
    scores = jnp.where(allowed, scores, -1e30)
    top_score = jnp.max(scores, axis=-1, keepdims=True)
    exp_scores = jnp.exp(scores - top_score)
    total_mass = jnp.sum(exp_scores, axis=-1, keepdims=True)
    attn_probs = exp_scores / total_mass
    low_probs = attn_probs.astype(jnp.bfloat16)
    mixed_heads = (
        jnp.einsum("kgqs,skd->qkgd", low_probs, value_rows, preferred_element_type=jnp.float32)
        .reshape(row_total, q_width)
        .astype(jnp.bfloat16)
    )
    attn_part = jnp.dot(mixed_heads, o_weight, preferred_element_type=jnp.float32)
    residual = inputs + (attn_part + swap_tensor(attn_part))
    factor_two = lax.rsqrt(jnp.mean(residual * residual, axis=-1, keepdims=True) + norm_eps)
    normed_two = (residual * factor_two * gain_two).astype(jnp.bfloat16)
    gate_act = jnp.dot(normed_two, gate_weight, preferred_element_type=jnp.float32)
    up_act = jnp.dot(normed_two, up_weight, preferred_element_type=jnp.float32)
    hidden_act = (jax.nn.silu(gate_act) * up_act).astype(jnp.bfloat16)
    upstream = out_grad.astype(jnp.float32)
    branch_grad = (upstream * alive_rows).astype(jnp.bfloat16)
    ffn_keep, ffn_send = dest_columns(width, ffn_order)
    attn_keep, attn_send = dest_columns(width, attn_order)
    down_grad = scatter_sum(pick(branch_grad, ffn_keep), pick(branch_grad, ffn_send), hidden_act, ffn_order)
    hidden_grad = jnp.einsum("td,fd->tf", branch_grad, down_weight, preferred_element_type=jnp.float32)
    sigmoid_gate = jax.nn.sigmoid(gate_act)
    gate_grad_rows = (
        hidden_grad * up_act * (sigmoid_gate * (1.0 + gate_act * (1.0 - sigmoid_gate)))
    ).astype(jnp.bfloat16)
    up_grad_rows = (hidden_grad * jax.nn.silu(gate_act)).astype(jnp.bfloat16)
    normed_two_part = jnp.einsum(
        "tf,df->td", gate_grad_rows, gate_weight, preferred_element_type=jnp.float32
    ) + jnp.einsum("tf,df->td", up_grad_rows, up_weight, preferred_element_type=jnp.float32)
    two_keep, two_send = pick(normed_two, ffn_keep), pick(normed_two, ffn_send)
    gate_grad = scatter_sum(two_keep, two_send, gate_grad_rows, ffn_order)
    up_grad = scatter_sum(two_keep, two_send, up_grad_rows, ffn_order)
    normed_two_grad = normed_two_part + swap_tensor(normed_two_part)
    ffn_gain_part = jnp.sum(normed_two_part * (residual * factor_two), axis=0)
    residual_grad = norm_back(residual, factor_two, gain_two, normed_two_grad)
    residual_grad = residual_grad + upstream * alive_rows
    residual_low = residual_grad.astype(jnp.bfloat16)
    o_grad = scatter_sum(pick(residual_low, attn_keep), pick(residual_low, attn_send), mixed_heads, attn_order)
    mixed_grad = (
        jnp.einsum("td,ad->ta", residual_low, o_weight, preferred_element_type=jnp.float32)
        .astype(jnp.bfloat16)
        .reshape(row_total, local_kv, group_size, HD)
    )
    value_acc = jnp.einsum("kgqs,qkgd->skd", low_probs, mixed_grad, preferred_element_type=jnp.float32)
    prob_grad = jnp.einsum("qkgd,skd->kgqs", mixed_grad, value_rows, preferred_element_type=jnp.float32)
    inner_sum = jnp.sum(attn_probs * prob_grad, axis=-1, keepdims=True)
    score_grad = (attn_probs * (prob_grad - inner_sum)).astype(jnp.bfloat16)
    query_acc = (
        jnp.einsum("kgqs,skd->qkgd", score_grad, key_rows, preferred_element_type=jnp.float32) * score_scale
    )
    key_acc = jnp.einsum("kgqs,qkgd->skd", score_grad, queries, preferred_element_type=jnp.float32) * score_scale
    turned_back = rotate_pairs(
        jnp.concatenate([query_acc.reshape(row_total, local_heads, HD), key_acc], axis=1), cosine, -sine_table
    )
    qkv_grad_rows = (
        jnp.concatenate([turned_back, value_acc], axis=1)
        .reshape(row_total, q_width + 2 * k_width)
        .astype(jnp.bfloat16)
    )
    normed_part = jnp.einsum("ta,da->td", qkv_grad_rows, qkv_weight, preferred_element_type=jnp.float32)
    qkv_grad = scatter_sum(pick(normed, attn_keep), pick(normed, attn_send), qkv_grad_rows, attn_order)
    attn_gain_part = jnp.sum(normed_part * (inputs * factor_one), axis=0)
    bias_part = jnp.sum(qkv_grad_rows.astype(jnp.float32), axis=0)
    normed_grad = normed_part + swap_tensor(normed_part)
    input_grad = norm_back(inputs, factor_one, gain_one, normed_grad)
    tokens_grad = (upstream * (1.0 - alive_rows) + residual_grad + input_grad).astype(jnp.bfloat16)
    gain_parts = jnp.concatenate([attn_gain_part, ffn_gain_part])
    gain_parts = gain_parts + swap_tensor(gain_parts)
    small = jnp.concatenate([gain_parts, bias_part])
    for bit in range(dp_bits):
        small = small + swap_dp(small, bit)
    gain_block = width // dp_size
    attn_gain_grad = lax.dynamic_slice_in_dim(small, own * gain_block, gain_block)
    ffn_gain_grad = lax.dynamic_slice_in_dim(small, width + own * gain_block, gain_block)
    bias_heads = small[2 * width :].reshape(local_heads + 2 * local_kv, HD)
    bias_block = HD // dp_size
    bias_own = lax.dynamic_slice_in_dim(bias_heads, own * bias_block, bias_block, axis=1)
    ffn_part = jnp.dot(hidden_act, down_weight, preferred_element_type=jnp.float32)
    block_out = residual + (ffn_part + swap_tensor(ffn_part))
    layer_out = jnp.where(alive[:, None], block_out, inputs).astype(jnp.bfloat16)
    return (
        layer_out,
        tokens_grad,
        qkv_grad[:, :q_width],
        qkv_grad[:, q_width : q_width + k_width],
        qkv_grad[:, q_width + k_width :],
        bias_own[:local_heads],
        bias_heads[local_heads : local_heads + local_kv],
        bias_own[local_heads + local_kv :],
        o_grad.T,
        attn_gain_grad,
        ffn_gain_grad,
        gate_grad,
        up_grad,
        down_grad.T,
    )


def solution(mesh):
    return jax.shard_map(
        on_device,
        mesh=mesh,
        in_specs=(
            P("dp", None),
            P("dp", None),
            P("dp", None),
            P(None, "tensor"),
            P(None, "tensor"),
            P(None, "tensor"),
            P("tensor", None),
            P("tensor", None),
            P("tensor", None),
            P("tensor", None),
            P(),
            P(),
            P(None, "tensor"),
            P(None, "tensor"),
            P("tensor", None),
        ),
        out_specs=(
            P("dp", None),
            P("dp", None),
            P("dp", "tensor"),
            P("dp", "tensor"),
            P("dp", "tensor"),
            P("tensor", "dp"),
            P("tensor", None),
            P("tensor", "dp"),
            P("tensor", "dp"),
            P("dp"),
            P("dp"),
            P("dp", "tensor"),
            P("dp", "tensor"),
            P("tensor", "dp"),
        ),
        check_vma=False,
    )
```

```python
import functools
import math

import jax
import jax.numpy as jnp
from jax import lax
from jax.experimental import pallas as pl
from jax.experimental.pallas import tpu as pltpu
from jax.sharding import PartitionSpec as P

HD = 64


norm_eps = 1e-06
rope_base = 1000000.0


def layout(lengths, row_total):
    doc_ends = jnp.cumsum(lengths)
    places = jnp.arange(row_total, dtype=jnp.int32)
    passed = (places[:, None] >= doc_ends[None, :]).astype(jnp.int32)
    segment = jnp.sum(passed, axis=1)
    begins = jnp.sum(passed * lengths[None, :], axis=1)
    alive = places < doc_ends[-1]
    return (segment, places - begins, alive)


def rotary(positions, width):
    half_width = width // 2
    inv_freq = jnp.exp(
        jnp.arange(half_width, dtype=jnp.float32) * (-2.0 * math.log(rope_base) / width)
    )
    angles = positions.astype(jnp.float32)[:, None] * inv_freq[None, :]
    return (jnp.cos(angles), jnp.sin(angles))


def rotate_pairs(heads_in, cosine, sine_table):
    half_width = heads_in.shape[-1] // 2
    front_half = heads_in[..., :half_width]
    back_half = heads_in[..., half_width:]
    cos_rows = cosine[:, None, :]
    sin_rows = sine_table[:, None, :]
    return jnp.concatenate(
        [
            front_half * cos_rows - back_half * sin_rows,
            back_half * cos_rows + front_half * sin_rows,
        ],
        axis=-1,
    )


def norm_back(inputs, factor, gain, upstream):
    scaled = upstream * gain
    return factor * scaled - inputs * factor**3 * jnp.mean(scaled * inputs, axis=-1, keepdims=True)


def swap_tensor(rows):
    size = lax.axis_size("tensor")
    return lax.ppermute(rows, "tensor", [(i, i ^ 1) for i in range(size)])


def swap_dp(rows, bit):
    size = lax.axis_size("dp")
    return lax.ppermute(rows, "dp", [(i, i ^ (1 << bit)) for i in range(size)])


def after(value, *others):
    return lax.optimization_barrier((value, *others))[0]


def dest_columns(width, order, fixed=()):
    steps = len(order)
    block = width >> (steps + len(fixed))
    count = block << steps
    own = lax.axis_index("dp")
    places = jnp.arange(count, dtype=jnp.int32)
    spot = places // block
    flip = jnp.zeros_like(spot)
    for j, bit in enumerate(order):
        flip = flip + (((spot >> (steps - 1 - j)) & 1) << bit)
    source = (own ^ flip) * block + places % block
    chosen = (jnp.arange(width, dtype=jnp.int32)[:, None] == source[None, :]).astype(jnp.bfloat16)
    return chosen[:, : count // 2], chosen[:, count // 2 :]


def pick(rows, chosen):
    return jnp.dot(rows, chosen, preferred_element_type=jnp.float32).astype(jnp.bfloat16)


def outer(rows, features):
    return jnp.einsum("td,tf->df", rows, features, preferred_element_type=jnp.float32)


def fold(kept_rows, features, sent):
    kept_rows = after(kept_rows, sent)
    half = sent.shape[0] // 2
    keep = outer(kept_rows[:, :half], features) + sent[:half]
    send = outer(kept_rows[:, half:], features) + sent[half:]
    return keep, send


def finish(keep, send, order):
    for bit in order[:-1]:
        sent = swap_dp(send, bit)
        half = sent.shape[0] // 2
        send = keep[half:] + sent[half:]
        keep = keep[:half] + sent[:half]
    return keep + swap_dp(send, order[-1])


def scatter_sum(kept_rows, sent_rows, features, order):
    keep, send = fold(kept_rows, features, swap_dp(outer(sent_rows, features), order[0]))
    return finish(keep, send, order[1:])


IN_VMEM = pl.BlockSpec(memory_space=pltpu.VMEM)


def contract(left, right, left_dim, right_dim):
    return lax.dot_general(
        left, right, (((left_dim,), (right_dim,)), ((), ())), preferred_element_type=jnp.float32
    )


def over(total, size, step):
    count, rest = divmod(total, size)

    def turn(i, carry):
        step(pl.multiple_of(i * size, size), size)
        return carry

    lax.fori_loop(0, count, turn, 0)
    if rest:
        step(count * size, rest)


def ffn_kernel(two_ref, branch_ref, gate_ref, up_ref, down_ref, hidden_ref, gate_rows_ref, up_rows_ref, *own_refs):
    def forth(start, size):
        c = pl.ds(start, size)
        gate = contract(two_ref[...], gate_ref[:, c], 1, 0)
        up = contract(two_ref[...], up_ref[:, c], 1, 0)
        hidden_grad = contract(branch_ref[...], down_ref[c, :], 1, 1)
        sigmoid_gate = 0.5 * jnp.tanh(0.5 * gate) + 0.5
        silu_gate = gate * sigmoid_gate
        hidden_ref[:, c] = (silu_gate * up).astype(jnp.bfloat16)
        gate_rows_ref[:, c] = (hidden_grad * up * (sigmoid_gate + silu_gate * (1.0 - sigmoid_gate))).astype(jnp.bfloat16)
        up_rows_ref[:, c] = (hidden_grad * silu_gate).astype(jnp.bfloat16)

    def back(start, size):
        part_ref, ffn_ref = own_refs
        c = pl.ds(start, size)
        part_ref[:, c] = contract(gate_rows_ref[...], gate_ref[c, :], 1, 1) + contract(
            up_rows_ref[...], up_ref[c, :], 1, 1
        )
        ffn_ref[:, c] = contract(hidden_ref[...], down_ref[:, c], 1, 0)

    over(gate_ref.shape[1], 768, forth)
    if own_refs:
        over(gate_ref.shape[0], 256, back)


def ffn_rows(rows, branch, gate_weight, up_weight, down_weight, own):
    count, width = rows.shape
    wide = jax.ShapeDtypeStruct((count, gate_weight.shape[1]), jnp.bfloat16)
    total = jax.ShapeDtypeStruct((count, width), jnp.float32)
    return pl.pallas_call(
        ffn_kernel,
        in_specs=[IN_VMEM] * 5,
        out_specs=[IN_VMEM] * (5 if own else 3),
        out_shape=[wide] * 3 + [total] * (2 if own else 0),
        compiler_params=pltpu.CompilerParams(vmem_limit_bytes=40 * 2**20),
        name="ffn_own" if own else "ffn_pair",
    )(rows, branch, gate_weight, up_weight, down_weight)


def on_device(
    tokens,
    out_grad,
    doc_lengths,
    q_weight,
    k_weight,
    v_weight,
    q_bias,
    k_bias,
    v_bias,
    o_weight,
    attn_gain,
    ffn_gain,
    gate_weight,
    up_weight,
    down_weight,
):
    row_total, width = tokens.shape
    local_heads = q_weight.shape[1] // HD
    local_kv = k_weight.shape[1] // HD
    group_size = local_heads // local_kv
    dp_size = lax.axis_size("dp")
    dp_bits = dp_size.bit_length() - 1
    pair_bit = 2
    ffn_order = (0, 1) + tuple(range(3, dp_bits))
    attn_order = (0, pair_bit, 1) + tuple(range(3, dp_bits))
    own = lax.axis_index("dp")
    score_scale = HD ** (-0.5)
    segment, positions, alive = layout(doc_lengths[0], row_total)
    cosine, sine_table = rotary(positions, HD)
    alive_rows = alive.astype(jnp.float32)[:, None]
    places = jnp.arange(row_total, dtype=jnp.int32)
    unit = alive_rows[0, 0]
    o_half = o_weight.shape[0] // 2
    o_first = own & 1
    upstream = out_grad.astype(jnp.float32)
    branch_wide = upstream * alive_rows
    o_mine = lax.dynamic_slice_in_dim(o_weight, o_first * o_half, o_half).astype(jnp.float32)
    o_same = swap_tensor(o_mine)
    pair_branch = (swap_dp(branch_wide, pair_bit) * unit).astype(jnp.bfloat16)
    o_cross = swap_dp(o_same, 0) * unit
    o_same = o_same * unit
    o_low = jnp.where(o_first == 0, o_same, o_cross).astype(jnp.bfloat16)
    o_high = jnp.where(o_first == 0, o_cross, o_same).astype(jnp.bfloat16)
    branch_grad = branch_wide.astype(jnp.bfloat16)
    inputs = tokens.astype(jnp.float32)
    gain_one = attn_gain.astype(jnp.float32)
    gain_two = ffn_gain.astype(jnp.float32)
    factor_one = lax.rsqrt(jnp.mean(inputs * inputs, axis=-1, keepdims=True) + norm_eps)
    normed = (inputs * factor_one * gain_one).astype(jnp.bfloat16)
    qkv_weight = jnp.concatenate([q_weight, k_weight, v_weight], axis=1)
    qkv_bias = jnp.concatenate([q_bias.reshape(-1), k_bias.reshape(-1), v_bias.reshape(-1)])
    qkv = jnp.dot(normed, qkv_weight, preferred_element_type=jnp.float32) + qkv_bias.astype(jnp.float32)
    q_width = local_heads * HD
    k_width = local_kv * HD
    value_rows = qkv[:, q_width + k_width :].astype(jnp.bfloat16).reshape(row_total, local_kv, HD)
    turned = rotate_pairs(
        qkv[:, : q_width + k_width].reshape(row_total, local_heads + local_kv, HD), cosine, sine_table
    ).astype(jnp.bfloat16)
    queries = turned[:, :local_heads].reshape(row_total, local_kv, group_size, HD)
    key_rows = turned[:, local_heads:]
    allowed = (segment[:, None] == segment[None, :]) & (places[:, None] >= places[None, :])
    scores = jnp.einsum("qkgd,skd->kgqs", queries, key_rows, preferred_element_type=jnp.float32) * score_scale
    scores = jnp.where(allowed, scores, -1e30)
    top_score = jnp.max(scores, axis=-1, keepdims=True)
    exp_scores = jnp.exp(scores - top_score)
    total_mass = jnp.sum(exp_scores, axis=-1, keepdims=True)
    attn_probs = exp_scores / total_mass
    low_probs = attn_probs.astype(jnp.bfloat16)
    mixed_heads = (
        jnp.einsum("kgqs,skd->qkgd", low_probs, value_rows, preferred_element_type=jnp.float32)
        .reshape(row_total, q_width)
        .astype(jnp.bfloat16)
    )
    mixed_other = (swap_tensor(mixed_heads.astype(jnp.float32)) * unit).astype(jnp.bfloat16)
    residual = inputs + (
        jnp.dot(mixed_heads, o_weight, preferred_element_type=jnp.float32)
        + jnp.dot(
            mixed_other, jnp.concatenate([o_low, o_high]), preferred_element_type=jnp.float32
        )
    )
    factor_two = lax.rsqrt(jnp.mean(residual * residual, axis=-1, keepdims=True) + norm_eps)
    normed_two = (residual * factor_two * gain_two).astype(jnp.bfloat16)
    pair_two = (swap_dp(normed_two.astype(jnp.float32), pair_bit) * unit).astype(jnp.bfloat16)

    hidden_act, gate_grad_rows, up_grad_rows, normed_two_part, ffn_part = ffn_rows(
        normed_two, branch_grad, gate_weight, up_weight, down_weight, True
    )
    two_from_x = swap_tensor(normed_two_part)
    ffn_gain_part = jnp.sum(normed_two_part * (residual * factor_two), axis=0)

    pair_hidden, pair_gate_rows, pair_up_rows = ffn_rows(
        pair_two, pair_branch, gate_weight, up_weight, down_weight, False
    )
    ffn_keep, ffn_send = dest_columns(width, ffn_order, (pair_bit,))
    attn_keep, attn_send = dest_columns(width, attn_order)
    both_branch = jnp.concatenate([branch_grad, pair_branch])
    both_two = jnp.concatenate([normed_two, pair_two])
    both_hidden = jnp.concatenate([hidden_act, pair_hidden])
    both_gate = jnp.concatenate([gate_grad_rows, pair_gate_rows])
    both_up = jnp.concatenate([up_grad_rows, pair_up_rows])
    branch_keep, branch_send = pick(both_branch, ffn_keep), pick(both_branch, ffn_send)
    two_keep, two_send = pick(both_two, ffn_keep), pick(both_two, ffn_send)
    down_sent = swap_dp(outer(branch_send, both_hidden), 0)
    gate_sent = swap_dp(outer(two_send, both_gate), 0)
    up_sent = swap_dp(outer(two_send, both_up), 0)
    down_parts = fold(branch_keep, both_hidden, down_sent)
    gate_parts = fold(after(two_keep, *down_parts), both_gate, gate_sent)
    up_parts = fold(after(two_keep, *gate_parts), both_up, up_sent)
    down_grad = finish(*down_parts, ffn_order[1:])
    gate_grad = finish(*gate_parts, ffn_order[1:])
    up_grad = finish(*up_parts, ffn_order[1:])
    two_from_x = after(two_from_x, *up_parts)
    normed_two_grad = normed_two_part + two_from_x
    residual_grad = norm_back(residual, factor_two, gain_two, normed_two_grad)
    residual_grad = residual_grad + upstream * alive_rows
    residual_low = residual_grad.astype(jnp.bfloat16)
    o_grad = scatter_sum(pick(residual_low, attn_keep), pick(residual_low, attn_send), mixed_heads, attn_order)
    mixed_grad = (
        jnp.einsum("td,ad->ta", residual_low, o_weight, preferred_element_type=jnp.float32)
        .astype(jnp.bfloat16)
        .reshape(row_total, local_kv, group_size, HD)
    )
    value_acc = jnp.einsum("kgqs,qkgd->skd", low_probs, mixed_grad, preferred_element_type=jnp.float32)
    prob_grad = jnp.einsum("qkgd,skd->kgqs", mixed_grad, value_rows, preferred_element_type=jnp.float32)
    inner_sum = jnp.sum(attn_probs * prob_grad, axis=-1, keepdims=True)
    score_grad = (attn_probs * (prob_grad - inner_sum)).astype(jnp.bfloat16)
    query_acc = (
        jnp.einsum("kgqs,skd->qkgd", score_grad, key_rows, preferred_element_type=jnp.float32) * score_scale
    )
    key_acc = jnp.einsum("kgqs,qkgd->skd", score_grad, queries, preferred_element_type=jnp.float32) * score_scale
    turned_back = rotate_pairs(
        jnp.concatenate([query_acc.reshape(row_total, local_heads, HD), key_acc], axis=1), cosine, -sine_table
    )
    qkv_grad_rows = (
        jnp.concatenate([turned_back, value_acc], axis=1)
        .reshape(row_total, q_width + 2 * k_width)
        .astype(jnp.bfloat16)
    )
    normed_part = jnp.einsum("ta,da->td", qkv_grad_rows, qkv_weight, preferred_element_type=jnp.float32)
    qkv_grad = scatter_sum(pick(normed, attn_keep), pick(normed, attn_send), qkv_grad_rows, attn_order)
    attn_gain_part = jnp.sum(normed_part * (inputs * factor_one), axis=0)
    bias_part = jnp.sum(qkv_grad_rows.astype(jnp.float32), axis=0)
    normed_grad = normed_part + swap_tensor(normed_part)
    input_grad = norm_back(inputs, factor_one, gain_one, normed_grad)
    tokens_grad = (upstream * (1.0 - alive_rows) + residual_grad + input_grad).astype(jnp.bfloat16)
    gain_parts = jnp.concatenate([attn_gain_part, ffn_gain_part])
    gain_parts = gain_parts + swap_tensor(gain_parts)
    small = jnp.concatenate([gain_parts, bias_part])
    for bit in range(dp_bits):
        small = small + swap_dp(small, bit)
    gain_block = width // dp_size
    attn_gain_grad = lax.dynamic_slice_in_dim(small, own * gain_block, gain_block)
    ffn_gain_grad = lax.dynamic_slice_in_dim(small, width + own * gain_block, gain_block)
    bias_heads = small[2 * width :].reshape(local_heads + 2 * local_kv, HD)
    bias_block = HD // dp_size
    bias_own = lax.dynamic_slice_in_dim(bias_heads, own * bias_block, bias_block, axis=1)
    ffn_part = after(ffn_part, two_from_x)
    block_out = residual + (ffn_part + swap_tensor(ffn_part))
    layer_out = jnp.where(alive[:, None], block_out, inputs).astype(jnp.bfloat16)
    return (
        layer_out,
        tokens_grad,
        qkv_grad[:, :q_width],
        qkv_grad[:, q_width : q_width + k_width],
        qkv_grad[:, q_width + k_width :],
        bias_own[:local_heads],
        bias_heads[local_heads : local_heads + local_kv],
        bias_own[local_heads + local_kv :],
        o_grad.T,
        attn_gain_grad,
        ffn_gain_grad,
        gate_grad,
        up_grad,
        down_grad.T,
    )


def solution(mesh):
    return jax.shard_map(
        on_device,
        mesh=mesh,
        in_specs=(
            P("dp", None),
            P("dp", None),
            P("dp", None),
            P(None, "tensor"),
            P(None, "tensor"),
            P(None, "tensor"),
            P("tensor", None),
            P("tensor", None),
            P("tensor", None),
            P("tensor", None),
            P(),
            P(),
            P(None, "tensor"),
            P(None, "tensor"),
            P("tensor", None),
        ),
        out_specs=(
            P("dp", None),
            P("dp", None),
            P("dp", "tensor"),
            P("dp", "tensor"),
            P("dp", "tensor"),
            P("tensor", "dp"),
            P("tensor", None),
            P("tensor", "dp"),
            P("tensor", "dp"),
            P("dp"),
            P("dp"),
            P("dp", "tensor"),
            P("dp", "tensor"),
            P("tensor", "dp"),
        ),
        check_vma=False,
    )
```

```python
import functools
import math

import jax
import jax.numpy as jnp
from jax import lax
from jax.experimental import pallas as pl
from jax.experimental.pallas import tpu as pltpu
from jax.sharding import PartitionSpec as P

HD = 64


norm_eps = 1e-06
rope_base = 1000000.0


def layout(lengths, row_total):
    doc_ends = jnp.cumsum(lengths)
    places = jnp.arange(row_total, dtype=jnp.int32)
    passed = (places[:, None] >= doc_ends[None, :]).astype(jnp.int32)
    begins = jnp.sum(passed * lengths[None, :], axis=1)
    alive = places < doc_ends[-1]
    return (places - begins, alive)


def rotary(positions, width):
    half_width = width // 2
    inv_freq = jnp.exp(
        jnp.arange(half_width, dtype=jnp.float32) * (-2.0 * math.log(rope_base) / width)
    )
    angles = inv_freq[:, None] * positions.astype(jnp.float32)[None, :]
    return (jnp.cos(angles), jnp.sin(angles))


def norm_back(inputs, factor, gain, upstream):
    scaled = upstream * gain
    return factor * scaled - inputs * factor**3 * jnp.mean(scaled * inputs, axis=-1, keepdims=True)


def swap_tensor(rows):
    size = lax.axis_size("tensor")
    return lax.ppermute(rows, "tensor", [(i, i ^ 1) for i in range(size)])


def swap_dp(rows, bit):
    size = lax.axis_size("dp")
    return lax.ppermute(rows, "dp", [(i, i ^ (1 << bit)) for i in range(size)])


def after(value, *others):
    return lax.optimization_barrier((value, *others))[0]


def dest_columns(width, order, fixed=(), extra=0):
    steps = len(order)
    block = width >> (steps + len(fixed))
    whole = block + extra
    count = whole << steps
    own = lax.axis_index("dp")
    places = jnp.arange(count, dtype=jnp.int32)
    spot = places // whole
    flip = jnp.zeros_like(spot)
    for j, bit in enumerate(order):
        flip = flip + (((spot >> (steps - 1 - j)) & 1) << bit)
    within = places % whole
    source = jnp.where(within < block, (own ^ flip) * block + within, -1)
    chosen = (source[:, None] == jnp.arange(width, dtype=jnp.int32)[None, :]).astype(jnp.bfloat16)
    return chosen[: count // 2], chosen[count // 2 :]


def finish(keep, send, order):
    for bit in order[:-1]:
        sent = swap_dp(send, bit)
        half = sent.shape[0] // 2
        send = keep[half:] + sent[half:]
        keep = keep[:half] + sent[:half]
    return keep + swap_dp(send, order[-1])


def close(keep, sent, order):
    return finish(*step_on(keep, sent), order) if order else keep + sent


def step_on(keep, sent):
    half = sent.shape[0] // 2
    return keep[:half] + sent[:half], keep[half:] + sent[half:]


IN_VMEM = pl.BlockSpec(memory_space=pltpu.VMEM)
LIMIT = 16
EXTRA = 8


def contract(left, right, left_dim, right_dim):
    return lax.dot_general(
        left, right, (((left_dim,), (right_dim,)), ((), ())), preferred_element_type=jnp.float32
    )


def over(total, size, step):
    count, rest = divmod(total, size)

    def turn(i, carry):
        step(pl.multiple_of(i * size, size), size)
        return carry

    lax.fori_loop(0, count, turn, 0)
    if rest:
        step(count * size, rest)


def call(kernel, name, shapes, *operands, scratch=()):
    return pl.pallas_call(
        kernel,
        in_specs=[IN_VMEM] * len(operands),
        out_specs=[IN_VMEM] * len(shapes),
        out_shape=[jax.ShapeDtypeStruct(shape, dtype) for shape, dtype in shapes],
        compiler_params=pltpu.CompilerParams(vmem_limit_bytes=LIMIT * 2**20),
        cost_estimate=pl.CostEstimate(flops=1000, bytes_accessed=1000, transcendentals=0),
        scratch_shapes=[pltpu.VMEM(shape, dtype) for shape, dtype in scratch],
        name=name,
    )(*operands)


def turn(pairs, cosine, sine_table):
    half = pairs.shape[0] // 2
    front, back = pairs[:half], pairs[half:]
    return jnp.concatenate([front * cosine - back * sine_table, back * cosine + front * sine_table], axis=0)


def blocks_of(begins_ref, row_total):
    size = row_total // 2
    for first in range(0, row_total, size):
        keys = first + size
        key_place = lax.broadcasted_iota(jnp.int32, (keys, size), 0)
        query_place = lax.broadcasted_iota(jnp.int32, (keys, size), 1) + first
        allowed = (key_place >= begins_ref[:, first:keys]) & (key_place <= query_place)
        yield slice(first, keys), keys, allowed


def attend_kernel(
    heads,
    tokens_ref,
    gain_ref,
    weight_ref,
    bias_ref,
    cosine_ref,
    sine_ref,
    begins_ref,
    normed_ref,
    turned_ref,
    mixed_ref,
    mixed_wide_ref,
    top_ref,
    mass_ref,
    pre_ref,
    mixed_across_ref,
):
    inputs = tokens_ref[...].astype(jnp.float32)
    factor = lax.rsqrt(jnp.mean(inputs * inputs, axis=-1, keepdims=True) + norm_eps)
    normed = (inputs * factor * gain_ref[...]).astype(jnp.bfloat16)
    normed_ref[...] = normed
    pre_ref[...] = contract(weight_ref[...], normed, 1, 1) + bias_ref[...]
    cosine, sine_table = cosine_ref[...], sine_ref[...]

    def rope(h, carry):
        r = pl.ds(pl.multiple_of(h * HD, HD), HD)
        turned_ref[r, :] = turn(pre_ref[r, :], cosine, sine_table).astype(jnp.bfloat16)
        return carry

    lax.fori_loop(0, heads + 1, rope, 0)
    value_rows = pre_ref[(heads + 1) * HD :, :].astype(jnp.bfloat16)
    turned_ref[(heads + 1) * HD :, :] = value_rows
    key_rows = turned_ref[heads * HD : (heads + 1) * HD, :].astype(jnp.float32).T.astype(jnp.bfloat16)
    blocks = list(blocks_of(begins_ref, inputs.shape[0]))

    def head(h, carry):
        r = pl.ds(pl.multiple_of(h * HD, HD), HD)
        for cols, keys, allowed in blocks:
            scores = contract(key_rows[:keys], turned_ref[r, cols], 1, 0) * HD ** (-0.5)
            scores = jnp.where(allowed, scores, -1e30)
            top = jnp.max(scores, axis=0, keepdims=True)
            exp_scores = jnp.exp(scores - top)
            mass = 1.0 / jnp.sum(exp_scores, axis=0, keepdims=True)
            low_probs = (exp_scores * mass).astype(jnp.bfloat16)
            mixed_across_ref[r, cols] = contract(value_rows[:, :keys], low_probs, 1, 0)
            top_ref[pl.ds(h, 1), cols] = top
            mass_ref[pl.ds(h, 1), cols] = mass
        return carry

    lax.fori_loop(0, heads, head, 0)
    mixed_wide_ref[...] = mixed_across_ref[: heads * HD, :].astype(jnp.bfloat16).astype(jnp.float32)
    mixed_ref[...] = mixed_across_ref[...].T[:, : heads * HD].astype(jnp.bfloat16)


def project_kernel(
    first_ref,
    tokens_ref,
    mixed_ref,
    other_ref,
    o_ref,
    same_ref,
    cross_ref,
    gain_ref,
    residual_ref,
    two_ref,
    low_ref,
    high_ref,
    o_other_ref,
):
    first = first_ref[...] == 0.0
    o_half = same_ref.shape[0]
    same, cross = same_ref[...], cross_ref[...]
    o_other_ref[:o_half, :] = jnp.where(first, same, cross).astype(jnp.bfloat16)
    o_other_ref[o_half:, :] = jnp.where(first, cross, same).astype(jnp.bfloat16)
    half = low_ref.shape[0]
    for rows, wide_ref in ((slice(0, half), low_ref), (slice(half, 2 * half), high_ref)):
        other = other_ref[:, rows].T.astype(jnp.bfloat16)
        residual = tokens_ref[rows, :].astype(jnp.float32) + (
            contract(mixed_ref[rows, :], o_ref[...], 1, 0) + contract(other, o_other_ref[...], 1, 0)
        )
        residual_ref[rows, :] = residual
        factor = lax.rsqrt(jnp.mean(residual * residual, axis=-1, keepdims=True) + norm_eps)
        two = (residual * factor * gain_ref[...]).astype(jnp.bfloat16)
        two_ref[rows, :] = two
        wide_ref[...] = two.astype(jnp.float32)


def norm_back_kernel(
    low_ref, high_ref, low_x_ref, high_x_ref, residual_ref, gain_ref, branch_ref, grad_ref, grad_low_ref, gain_grad_ref
):
    half = low_ref.shape[0]
    gain_grad = jnp.zeros(gain_grad_ref.shape, jnp.float32)
    for first, part_ref, x_ref in ((0, low_ref, low_x_ref), (half, high_ref, high_x_ref)):
        rows = slice(first, first + half)
        residual = residual_ref[rows, :]
        upstream = part_ref[...] + x_ref[...]
        factor = lax.rsqrt(jnp.mean(residual * residual, axis=-1, keepdims=True) + norm_eps)
        gain_grad += jnp.sum(upstream * (residual * factor), axis=0, keepdims=True)
        grad = norm_back(residual, factor, gain_ref[...], upstream) + branch_ref[rows, :].astype(jnp.float32)
        grad_ref[rows, :] = grad
        grad_low_ref[rows, :] = grad.astype(jnp.bfloat16)
    gain_grad_ref[...] = gain_grad


def tokens_back_kernel(tokens_ref, part_ref, other_ref, gain_ref, residual_ref, out_grad_ref, alive_ref, grad_ref):
    size = 128
    for first in range(0, tokens_ref.shape[0], size):
        rows = slice(first, first + size)
        inputs = tokens_ref[rows, :].astype(jnp.float32)
        factor = lax.rsqrt(jnp.mean(inputs * inputs, axis=-1, keepdims=True) + norm_eps)
        grad = norm_back(inputs, factor, gain_ref[...], part_ref[rows, :] + other_ref[rows, :])
        upstream = out_grad_ref[rows, :].astype(jnp.float32)
        total = upstream * (1.0 - alive_ref[rows, :]) + residual_ref[rows, :] + grad
        grad_ref[rows, :] = total.astype(jnp.bfloat16)


def attend_back_kernel(
    heads,
    residual_ref,
    o_ref,
    weight_ref,
    turned_ref,
    top_ref,
    mass_ref,
    cosine_ref,
    sine_ref,
    begins_ref,
    tokens_ref,
    rows_ref,
    part_ref,
    gain_grad_ref,
    mixed_ref,
    across_ref,
    key_ref,
    value_ref,
):
    mixed_ref[...] = contract(o_ref[...], residual_ref[...], 1, 1).astype(jnp.bfloat16)
    cosine, sine_table = cosine_ref[...], -sine_ref[...]
    k, v = heads * HD, (heads + 1) * HD
    keys_across = turned_ref[k:v, :]
    key_rows = keys_across.astype(jnp.float32).T.astype(jnp.bfloat16)
    value_rows = turned_ref[v:, :].astype(jnp.float32).T.astype(jnp.bfloat16)
    blocks = list(blocks_of(begins_ref, residual_ref.shape[0]))
    key_ref[...] = jnp.zeros(key_ref.shape, jnp.float32)
    value_ref[...] = jnp.zeros(value_ref.shape, jnp.float32)

    def head(h, carry):
        r = pl.ds(pl.multiple_of(h * HD, HD), HD)
        for cols, keys, allowed in blocks:
            query, grad = turned_ref[r, cols], mixed_ref[r, cols]
            scores = contract(key_rows[:keys], query, 1, 0) * HD ** (-0.5)
            scores = jnp.where(allowed, scores, -1e30)
            probs = jnp.exp(scores - top_ref[pl.ds(h, 1), cols]) * mass_ref[pl.ds(h, 1), cols]
            prob_grad = contract(value_rows[:keys], grad, 1, 0)
            inner_sum = jnp.sum(probs * prob_grad, axis=0, keepdims=True)
            score_grad = (probs * (prob_grad - inner_sum)).astype(jnp.bfloat16)
            query_grad = contract(keys_across[:, :keys], score_grad, 1, 0) * HD ** (-0.5)
            across_ref[r, cols] = turn(query_grad, cosine[:, cols], sine_table[:, cols])
            key_ref[:keys, :] += contract(score_grad, query, 1, 1)
            value_ref[:keys, :] += contract(probs.astype(jnp.bfloat16), grad, 1, 1)
        return carry

    lax.fori_loop(0, heads, head, 0)
    across_ref[k:v, :] = turn(key_ref[...].T * HD ** (-0.5), cosine, sine_table)
    across_ref[v : v + HD, :] = value_ref[...].T
    rows_ref[...] = across_ref[...].T[:, : v + HD].astype(jnp.bfloat16)

    def step(start, size):
        c = pl.ds(start, size)
        part = contract(rows_ref[...], weight_ref[:, c], 1, 0)
        part_ref[:, c] = part
        gain_grad_ref[:, c] = jnp.sum(part * (tokens_ref[:, c].astype(jnp.float32) * factor), axis=0, keepdims=True)

    inputs = tokens_ref[...].astype(jnp.float32)
    factor = lax.rsqrt(jnp.mean(inputs * inputs, axis=-1, keepdims=True) + norm_eps)
    over(part_ref.shape[1], 256, step)


def ffn_kernel(two_ref, branch_ref, gate_ref, up_ref, down_ref, hidden_ref, gate_rows_ref, up_rows_ref, *low_refs):
    if low_refs:
        for wide_ref, low_ref in zip((two_ref, branch_ref), low_refs):
            low_ref[...] = wide_ref[...].astype(jnp.bfloat16)
        two_ref, branch_ref = low_refs

    def step(start, size):
        c = pl.ds(start, size)
        gate = contract(two_ref[...], gate_ref[:, c], 1, 0)
        up = contract(two_ref[...], up_ref[:, c], 1, 0)
        hidden_grad = contract(branch_ref[...], down_ref[c, :], 1, 1)
        sigmoid_gate = 0.5 * jnp.tanh(0.5 * gate) + 0.5
        silu_gate = gate * sigmoid_gate
        hidden_ref[:, c] = (silu_gate * up).astype(jnp.bfloat16)
        gate_rows_ref[:, c] = (hidden_grad * up * (sigmoid_gate + silu_gate * (1.0 - sigmoid_gate))).astype(jnp.bfloat16)
        up_rows_ref[:, c] = (hidden_grad * silu_gate).astype(jnp.bfloat16)

    over(gate_ref.shape[1], 768, step)


def ffn_rows(rows, branch, gate_weight, up_weight, down_weight):
    wide = ((rows.shape[0], gate_weight.shape[1]), jnp.bfloat16)
    low = [(rows.shape, jnp.bfloat16)] * 2 if rows.dtype == jnp.float32 else []
    return call(ffn_kernel, "ffn_rows", [wide] * 3 + low, rows, branch, gate_weight, up_weight, down_weight)


def back_kernel(first, gate_rows_ref, up_rows_ref, gate_ref, up_ref, part_ref):
    count = part_ref.shape[0]
    rows = pl.ds(first, count)

    def step(start, size):
        c = pl.ds(start, size)
        part_ref[:, c] = contract(gate_rows_ref[rows, :], gate_ref[c, :], 1, 1) + contract(
            up_rows_ref[rows, :], up_ref[c, :], 1, 1
        )

    over(gate_ref.shape[0], 256, step)


def ffn_back(gate_rows, up_rows, gate_weight, up_weight, first, count):
    shape = ((count, gate_weight.shape[0]), jnp.float32)
    (part,) = call(
        functools.partial(back_kernel, first), "ffn_back", [shape], gate_rows, up_rows, gate_weight, up_weight
    )
    return part


def down_kernel(hidden_ref, down_ref, low_ref, high_ref):
    half = low_ref.shape[0]

    def step(start, size):
        c = pl.ds(start, size)
        low_ref[:, c] = contract(hidden_ref[:half, :], down_ref[:, c], 1, 0)
        high_ref[:, c] = contract(hidden_ref[half:, :], down_ref[:, c], 1, 0)

    over(down_ref.shape[1], 256, step)


def ffn_down(hidden, down_weight):
    shape = ((hidden.shape[0] // 2, down_weight.shape[1]), jnp.float32)
    return call(down_kernel, "ffn_down", [shape] * 2, hidden, down_weight)


def sums_kernel(pieces, chosen_ref, *refs):
    rows_refs, feature_refs, refs = refs[:pieces], refs[pieces : 2 * pieces], refs[2 * pieces :]
    picked = [contract(chosen_ref[...], r[...], 1, 1).astype(jnp.bfloat16) for r in rows_refs]

    def step(start, size):
        c = pl.ds(start, size)
        total = sum(contract(p, f[:, c], 1, 0) for p, f in zip(picked, feature_refs))
        if len(refs) == 1:
            refs[0][:, c] = total
        else:
            half = total.shape[0] // 2
            arrived_ref, keep_ref, send_ref = refs
            keep_ref[:, c] = total[:half] + arrived_ref[:half, c]
            send_ref[:, c] = total[half:] + arrived_ref[half:, c]

    over(feature_refs[0].shape[1], 640, step)


def outer_sums(chosen, rows, features):
    shape = ((chosen.shape[0], features[0].shape[1]), jnp.float32)
    kernel = functools.partial(sums_kernel, len(rows))
    return call(kernel, "outer_sums", [shape], chosen, *rows, *features)[0]


def outer_fold(chosen, rows, features, arrived):
    shape = ((chosen.shape[0] // 2, features[0].shape[1]), jnp.float32)
    kernel = functools.partial(sums_kernel, len(rows))
    return call(kernel, "outer_fold", [shape] * 2, chosen, *rows, *features, arrived)


def attn_sums_kernel(block, chosen_ref, gains_ref, normed_ref, residual_ref, qkv_ref, mixed_ref, *refs):
    count = chosen_ref.shape[0]
    chosen = chosen_ref[...]
    qkv_width = qkv_ref.shape[1]
    o_start = qkv_width + gains_ref.shape[1]
    ones_row = lax.broadcasted_iota(jnp.int32, (count, normed_ref.shape[0]), 0) % (block + EXTRA) == block
    picked = contract(chosen, normed_ref[...], 1, 1)
    picked = jnp.where(ones_row, 1.0, picked).astype(jnp.bfloat16)
    gains = jnp.dot(
        chosen.astype(jnp.float32), gains_ref[...], preferred_element_type=jnp.float32, precision=lax.Precision.HIGHEST
    )
    picked_residual = contract(chosen, residual_ref[...], 1, 1).astype(jnp.bfloat16)
    total = jnp.concatenate(
        [
            contract(picked, qkv_ref[...], 1, 0),
            gains,
            contract(picked_residual, mixed_ref[...], 1, 0),
            jnp.zeros((count, -mixed_ref.shape[1] % 128), jnp.float32),
        ],
        axis=1,
    )
    if len(refs) == 1:
        refs[0][...] = total
    else:
        arrived_ref, keep_ref, send_ref = refs
        half = count // 2
        keep_ref[...] = total[:half] + arrived_ref[:half, :]
        send_ref[...] = total[half:] + arrived_ref[half:, :]


def attn_sums(block, chosen, gains, normed, residual_low, qkv_rows, mixed, arrived=None):
    count = chosen.shape[0]
    features = qkv_rows.shape[1] + gains.shape[1] + -(-mixed.shape[1] // 128) * 128
    kernel = functools.partial(attn_sums_kernel, block)
    operands = (chosen, gains, normed, residual_low, qkv_rows, mixed)
    if arrived is None:
        return call(kernel, "attn_sums", [((count, features), jnp.float32)], *operands)[0]
    return call(kernel, "attn_fold", [((count // 2, features), jnp.float32)] * 2, *operands, arrived)


def on_device(
    tokens,
    out_grad,
    doc_lengths,
    q_weight,
    k_weight,
    v_weight,
    q_bias,
    k_bias,
    v_bias,
    o_weight,
    attn_gain,
    ffn_gain,
    gate_weight,
    up_weight,
    down_weight,
):
    row_total, width = tokens.shape
    local_heads = q_weight.shape[1] // HD
    local_kv = k_weight.shape[1] // HD
    dp_size = lax.axis_size("dp")
    dp_bits = dp_size.bit_length() - 1
    pair_bit = 2
    ffn_order = (0, 1) + tuple(range(3, dp_bits))
    attn_order = (0, pair_bit, 1) + tuple(range(3, dp_bits))
    own = lax.axis_index("dp")
    positions, alive = layout(doc_lengths[0], row_total)
    cosine, sine_table = rotary(positions, HD)
    alive_rows = alive.astype(jnp.float32)[:, None]
    places = jnp.arange(row_total, dtype=jnp.int32)
    o_half = o_weight.shape[0] // 2
    o_first = own & 1
    upstream = out_grad.astype(jnp.float32)
    branch_wide = upstream * alive_rows
    o_mine = lax.dynamic_slice_in_dim(o_weight, o_first * o_half, o_half).astype(jnp.float32)
    o_same = swap_tensor(o_mine)
    half_rows = row_total // 2
    pair_branch = swap_dp(branch_wide, pair_bit)
    ffn_keep, ffn_send = dest_columns(width, ffn_order, (pair_bit,))
    attn_keep, attn_send = dest_columns(width, attn_order, extra=EXTRA)
    branch_grad = branch_wide.astype(jnp.bfloat16)
    inputs = tokens.astype(jnp.float32)
    gain_one = attn_gain.astype(jnp.float32)
    gain_two = ffn_gain.astype(jnp.float32)
    qkv_across = jnp.concatenate([q_weight.T, k_weight.T, v_weight.T])
    qkv_bias = jnp.concatenate([q_bias.reshape(-1), k_bias.reshape(-1), v_bias.reshape(-1)]).astype(jnp.float32)
    q_width = local_heads * HD
    k_width = local_kv * HD
    qkv_width = q_width + 2 * k_width
    begins = (places - positions)[None, :]
    padded = -(-qkv_width // 128) * 128
    row_stats = ((-(-local_heads // 8) * 8, row_total), jnp.float32)
    normed, turned, mixed_heads, mixed_wide, top_score, mass = call(
        functools.partial(attend_kernel, local_heads),
        "attend",
        [
            ((row_total, width), jnp.bfloat16),
            ((qkv_width, row_total), jnp.bfloat16),
            ((row_total, q_width), jnp.bfloat16),
            ((q_width, row_total), jnp.float32),
            row_stats,
            row_stats,
        ],
        tokens,
        gain_one[None, :],
        qkv_across,
        qkv_bias[:, None],
        cosine,
        sine_table,
        begins,
        scratch=[((qkv_width, row_total), jnp.float32), ((-(-q_width // 128) * 128, row_total), jnp.float32)],
    )
    mixed_other = swap_tensor(mixed_wide)
    o_same = after(o_same, mixed_heads)
    o_cross = swap_dp(o_same, 0)
    residual, normed_two, low_wide, high_wide = call(
        project_kernel,
        "project",
        [
            ((row_total, width), jnp.float32),
            ((row_total, width), jnp.bfloat16),
            ((half_rows, width), jnp.float32),
            ((half_rows, width), jnp.float32),
        ],
        jnp.broadcast_to(o_first.astype(jnp.float32), (1, width)),
        tokens,
        mixed_heads,
        after(mixed_other, o_cross, ffn_keep, ffn_send, attn_keep, attn_send, branch_grad),
        o_weight,
        o_same,
        o_cross,
        gain_two[None, :],
        scratch=[((q_width, width), jnp.bfloat16)],
    )
    low_two = swap_dp(low_wide, pair_bit)
    high_two = swap_dp(high_wide, pair_bit)
    ffn_weights = (gate_weight, up_weight, down_weight)

    hidden_act, gate_grad_rows, up_grad_rows = ffn_rows(normed_two, branch_grad, *ffn_weights)
    low_part = ffn_back(after(gate_grad_rows, pair_branch), up_grad_rows, gate_weight, up_weight, 0, half_rows)
    low_from_x = swap_tensor(low_part)
    high_part = ffn_back(after(gate_grad_rows, low_part), up_grad_rows, gate_weight, up_weight, half_rows, half_rows)
    low_branch, high_branch = pair_branch[:half_rows], pair_branch[half_rows:]
    low_hidden, low_gate, low_up, low_two, low_branch = ffn_rows(after(low_two, high_part), low_branch, *ffn_weights)
    low_down, high_down = ffn_down(after(hidden_act, low_hidden), down_weight)
    high_from_x = swap_tensor(after(high_part, low_from_x))
    high_hidden, high_gate, high_up, high_two, high_branch = ffn_rows(
        after(high_two, low_down, low_from_x), high_branch, *ffn_weights
    )
    branch_rows = (branch_grad, low_branch, high_branch)
    two_rows = (normed_two, low_two, high_two)
    down_sums = outer_sums(ffn_send, branch_rows, (hidden_act, low_hidden, high_hidden))
    down_sent = swap_dp(down_sums, 0)
    gate_sums = outer_sums(after(ffn_send, down_sums), two_rows, (gate_grad_rows, low_gate, high_gate))
    gate_sent = swap_dp(gate_sums, 0)
    up_sums = outer_sums(after(ffn_send, gate_sums), two_rows, (up_grad_rows, low_up, high_up))
    up_sent = swap_dp(up_sums, 0)
    down_keep, down_send = outer_fold(
        after(ffn_keep, up_sums), branch_rows, (hidden_act, low_hidden, high_hidden), down_sent
    )
    gate_keep, gate_send = outer_fold(
        after(ffn_keep, down_send), two_rows, (gate_grad_rows, low_gate, high_gate), gate_sent
    )
    up_keep, up_send = outer_fold(after(ffn_keep, gate_send), two_rows, (up_grad_rows, low_up, high_up), up_sent)
    down_from_y, gate_from_y, up_from_y = (swap_dp(v, ffn_order[1]) for v in (down_send, gate_send, up_send))
    high_from_x = after(high_from_x, up_send)
    low_down_x = swap_tensor(after(low_down, high_from_x))
    wide, low = ((row_total, width), jnp.float32), ((row_total, width), jnp.bfloat16)
    gain_row = ((1, width), jnp.float32)
    residual_grad, residual_low, ffn_gain_sum = call(
        norm_back_kernel,
        "norm_back",
        [wide, low, gain_row],
        low_part,
        high_part,
        low_from_x,
        high_from_x,
        residual,
        gain_two[None, :],
        branch_grad,
    )
    down_keep, down_send = step_on(down_keep, down_from_y)
    residual_low = after(residual_low, down_send)
    down_from_z = swap_dp(down_send, ffn_order[2])
    qkv_grad_rows, normed_part, attn_gain_part = call(
        functools.partial(attend_back_kernel, local_heads),
        "attend_back",
        [((row_total, qkv_width), jnp.bfloat16), wide, gain_row],
        residual_low,
        o_weight,
        qkv_across,
        turned,
        top_score,
        mass,
        cosine,
        sine_table,
        begins,
        tokens,
        scratch=[
            ((q_width, row_total), jnp.bfloat16),
            ((padded, row_total), jnp.float32),
            ((row_total, HD), jnp.float32),
            ((row_total, HD), jnp.float32),
        ],
    )
    gate_keep, gate_send = step_on(gate_keep, gate_from_y)
    gain_sums = jnp.concatenate([attn_gain_part + swap_tensor(attn_gain_part), ffn_gain_sum])
    normed_part = after(normed_part, gain_sums, low_down_x)
    gate_from_z = swap_dp(gate_send, ffn_order[2])
    normed_other = swap_tensor(normed_part)
    high_down_x = swap_tensor(after(high_down, normed_part))
    gain_columns = jnp.pad(gain_sums, ((0, -qkv_width % 128 - 2), (0, 0))).T
    attn_operands = (gain_columns, normed, residual_low, qkv_grad_rows, mixed_heads)
    gain_block = width // dp_size
    attn_sent = swap_dp(
        attn_sums(gain_block, after(attn_send, gate_send, down_from_z), *attn_operands), attn_order[0]
    )
    attn_part, attn_next = attn_sums(gain_block, attn_keep, *attn_operands, attn_sent)
    attn_from_z = swap_dp(attn_next, attn_order[1])
    up_keep, up_send = step_on(up_keep, after(up_from_y, attn_next))
    up_from_z = swap_dp(up_send, ffn_order[2])
    attn_part, attn_next = step_on(attn_part, after(attn_from_z, up_send, gate_from_z))
    attn_from_y = swap_dp(attn_next, attn_order[2])
    attn_part, attn_next = step_on(attn_part, attn_from_y)
    attn_from_z = swap_dp(after(attn_next, up_from_z), attn_order[3])
    attn_grad = close(attn_part, attn_from_z, attn_order[4:])
    (tokens_grad,) = call(
        tokens_back_kernel,
        "tokens_back",
        [low],
        tokens,
        normed_part,
        after(normed_other, attn_next),
        gain_one[None, :],
        residual_grad,
        out_grad,
        alive_rows,
    )
    block_out = residual + jnp.concatenate([low_down + low_down_x, high_down + high_down_x])
    o_start = -(-qkv_width // 128) * 128
    qkv_grad, o_grad = attn_grad[:gain_block, :qkv_width], attn_grad[:gain_block, o_start : o_start + q_width]
    attn_gain_grad, ffn_gain_grad = attn_grad[:gain_block, qkv_width], attn_grad[:gain_block, qkv_width + 1]
    bias_heads = attn_grad[gain_block, :qkv_width].reshape(local_heads + 2 * local_kv, HD)
    bias_block = HD // dp_size
    bias_own = lax.dynamic_slice_in_dim(bias_heads, own * bias_block, bias_block, axis=1)
    down_grad, gate_grad, up_grad = (
        close(keep, got, ffn_order[3:])
        for keep, got in ((down_keep, down_from_z), (gate_keep, gate_from_z), (up_keep, up_from_z))
    )
    layer_out = jnp.where(alive[:, None], block_out, inputs).astype(jnp.bfloat16)
    return (
        layer_out,
        tokens_grad,
        qkv_grad[:, :q_width],
        qkv_grad[:, q_width : q_width + k_width],
        qkv_grad[:, q_width + k_width :],
        bias_own[:local_heads],
        bias_heads[local_heads : local_heads + local_kv],
        bias_own[local_heads + local_kv :],
        o_grad.T,
        attn_gain_grad,
        ffn_gain_grad,
        gate_grad,
        up_grad,
        down_grad.T,
    )


def solution(mesh):
    return jax.shard_map(
        on_device,
        mesh=mesh,
        in_specs=(
            P("dp", None),
            P("dp", None),
            P("dp", None),
            P(None, "tensor"),
            P(None, "tensor"),
            P(None, "tensor"),
            P("tensor", None),
            P("tensor", None),
            P("tensor", None),
            P("tensor", None),
            P(),
            P(),
            P(None, "tensor"),
            P(None, "tensor"),
            P("tensor", None),
        ),
        out_specs=(
            P("dp", None),
            P("dp", None),
            P("dp", "tensor"),
            P("dp", "tensor"),
            P("dp", "tensor"),
            P("tensor", "dp"),
            P("tensor", None),
            P("tensor", "dp"),
            P("tensor", "dp"),
            P("dp"),
            P("dp"),
            P("dp", "tensor"),
            P("dp", "tensor"),
            P("tensor", "dp"),
        ),
        check_vma=False,
    )
```

```python
import functools
import math

import jax
import jax.numpy as jnp
from jax import lax
from jax.experimental import pallas as pl
from jax.experimental.pallas import tpu as pltpu
from jax.sharding import PartitionSpec as P

HD = 64


norm_eps = 1e-06
rope_base = 1000000.0


def layout(lengths, row_total):
    doc_ends = jnp.cumsum(lengths)
    places = jnp.arange(row_total, dtype=jnp.int32)
    passed = (places[:, None] >= doc_ends[None, :]).astype(jnp.int32)
    begins = jnp.sum(passed * lengths[None, :], axis=1)
    alive = places < doc_ends[-1]
    return (places - begins, alive)


def rotary(positions, width):
    half_width = width // 2
    inv_freq = jnp.exp(
        jnp.arange(half_width, dtype=jnp.float32) * (-2.0 * math.log(rope_base) / width)
    )
    angles = inv_freq[:, None] * positions.astype(jnp.float32)[None, :]
    return (jnp.cos(angles), jnp.sin(angles))


def norm_back(inputs, factor, gain, upstream):
    scaled = upstream * gain
    return factor * scaled - inputs * factor**3 * jnp.mean(scaled * inputs, axis=-1, keepdims=True)


def swap_tensor(rows):
    size = lax.axis_size("tensor")
    return lax.ppermute(rows, "tensor", [(i, i ^ 1) for i in range(size)])


def swap_dp(rows, bit):
    size = lax.axis_size("dp")
    return lax.ppermute(rows, "dp", [(i, i ^ (1 << bit)) for i in range(size)])


def after(value, *others):
    return lax.optimization_barrier((value, *others))[0]


def dest_columns(width, order, fixed=(), extra=0):
    steps = len(order)
    block = width >> (steps + len(fixed))
    whole = block + extra
    count = whole << steps
    own = lax.axis_index("dp")
    places = jnp.arange(count, dtype=jnp.int32)
    spot = places // whole
    flip = jnp.zeros_like(spot)
    for j, bit in enumerate(order):
        flip = flip + (((spot >> (steps - 1 - j)) & 1) << bit)
    within = places % whole
    source = jnp.where(within < block, (own ^ flip) * block + within, -1)
    chosen = (source[:, None] == jnp.arange(width, dtype=jnp.int32)[None, :]).astype(jnp.bfloat16)
    return chosen[: count // 2], chosen[count // 2 :]


def finish(keep, send, order):
    for bit in order[:-1]:
        sent = swap_dp(send, bit)
        half = sent.shape[0] // 2
        send = keep[half:] + sent[half:]
        keep = keep[:half] + sent[:half]
    return keep + swap_dp(send, order[-1])


def close(keep, sent, order):
    return finish(*step_on(keep, sent), order) if order else keep + sent


def step_on(keep, sent):
    half = sent.shape[0] // 2
    return keep[:half] + sent[:half], keep[half:] + sent[half:]


IN_VMEM = pl.BlockSpec(memory_space=pltpu.VMEM)
LIMIT = 16
EXTRA = 8
CUTS = 4
ATTN_CUTS = 4


def contract(left, right, left_dim, right_dim):
    return lax.dot_general(
        left, right, (((left_dim,), (right_dim,)), ((), ())), preferred_element_type=jnp.float32
    )


def over(total, size, step):
    count, rest = divmod(total, size)

    def turn(i, carry):
        step(pl.multiple_of(i * size, size), size)
        return carry

    lax.fori_loop(0, count, turn, 0)
    if rest:
        step(count * size, rest)


def call(kernel, name, shapes, *operands, scratch=()):
    return pl.pallas_call(
        kernel,
        in_specs=[IN_VMEM] * len(operands),
        out_specs=[IN_VMEM] * len(shapes),
        out_shape=[jax.ShapeDtypeStruct(shape, dtype) for shape, dtype in shapes],
        compiler_params=pltpu.CompilerParams(vmem_limit_bytes=LIMIT * 2**20),
        cost_estimate=pl.CostEstimate(flops=1000, bytes_accessed=1000, transcendentals=0),
        scratch_shapes=[pltpu.VMEM(shape, dtype) for shape, dtype in scratch],
        name=name,
    )(*operands)


def turn(pairs, cosine, sine_table):
    half = pairs.shape[0] // 2
    front, back = pairs[:half], pairs[half:]
    return jnp.concatenate([front * cosine - back * sine_table, back * cosine + front * sine_table], axis=0)


def blocks_of(begins_ref, row_total):
    size = row_total // 2
    for first in range(0, row_total, size):
        keys = first + size
        key_place = lax.broadcasted_iota(jnp.int32, (keys, size), 0)
        query_place = lax.broadcasted_iota(jnp.int32, (keys, size), 1) + first
        allowed = (key_place >= begins_ref[:, first:keys]) & (key_place <= query_place)
        yield slice(first, keys), keys, allowed


def attend_kernel(
    heads,
    tokens_ref,
    gain_ref,
    weight_ref,
    bias_ref,
    cosine_ref,
    sine_ref,
    begins_ref,
    normed_ref,
    turned_ref,
    mixed_ref,
    mixed_wide_ref,
    top_ref,
    mass_ref,
    pre_ref,
    mixed_across_ref,
):
    inputs = tokens_ref[...].astype(jnp.float32)
    factor = lax.rsqrt(jnp.mean(inputs * inputs, axis=-1, keepdims=True) + norm_eps)
    normed = (inputs * factor * gain_ref[...]).astype(jnp.bfloat16)
    normed_ref[...] = normed
    pre_ref[...] = contract(weight_ref[...], normed, 1, 1) + bias_ref[...]
    cosine, sine_table = cosine_ref[...], sine_ref[...]

    def rope(h, carry):
        r = pl.ds(pl.multiple_of(h * HD, HD), HD)
        turned_ref[r, :] = turn(pre_ref[r, :], cosine, sine_table).astype(jnp.bfloat16)
        return carry

    lax.fori_loop(0, heads + 1, rope, 0)
    value_rows = pre_ref[(heads + 1) * HD :, :].astype(jnp.bfloat16)
    turned_ref[(heads + 1) * HD :, :] = value_rows
    key_rows = turned_ref[heads * HD : (heads + 1) * HD, :].astype(jnp.float32).T.astype(jnp.bfloat16)
    blocks = list(blocks_of(begins_ref, inputs.shape[0]))

    def head(h, carry):
        r = pl.ds(pl.multiple_of(h * HD, HD), HD)
        for cols, keys, allowed in blocks:
            scores = contract(key_rows[:keys], turned_ref[r, cols], 1, 0) * HD ** (-0.5)
            scores = jnp.where(allowed, scores, -1e30)
            top = jnp.max(scores, axis=0, keepdims=True)
            exp_scores = jnp.exp(scores - top)
            mass = 1.0 / jnp.sum(exp_scores, axis=0, keepdims=True)
            low_probs = (exp_scores * mass).astype(jnp.bfloat16)
            mixed_across_ref[r, cols] = contract(value_rows[:, :keys], low_probs, 1, 0)
            top_ref[pl.ds(h, 1), cols] = top
            mass_ref[pl.ds(h, 1), cols] = mass
        return carry

    lax.fori_loop(0, heads, head, 0)
    mixed_wide_ref[...] = mixed_across_ref[: heads * HD, :].astype(jnp.bfloat16).astype(jnp.float32)
    mixed_ref[...] = mixed_across_ref[...].T[:, : heads * HD].astype(jnp.bfloat16)


def project_kernel(
    first_ref,
    tokens_ref,
    mixed_ref,
    other_ref,
    o_ref,
    same_ref,
    cross_ref,
    gain_ref,
    residual_ref,
    two_ref,
    low_ref,
    high_ref,
    o_other_ref,
):
    first = first_ref[...] == 0.0
    o_half = same_ref.shape[0]
    same, cross = same_ref[...], cross_ref[...]
    o_other_ref[:o_half, :] = jnp.where(first, same, cross).astype(jnp.bfloat16)
    o_other_ref[o_half:, :] = jnp.where(first, cross, same).astype(jnp.bfloat16)
    half = low_ref.shape[0]
    for rows, wide_ref in ((slice(0, half), low_ref), (slice(half, 2 * half), high_ref)):
        other = other_ref[:, rows].T.astype(jnp.bfloat16)
        residual = tokens_ref[rows, :].astype(jnp.float32) + (
            contract(mixed_ref[rows, :], o_ref[...], 1, 0) + contract(other, o_other_ref[...], 1, 0)
        )
        residual_ref[rows, :] = residual
        factor = lax.rsqrt(jnp.mean(residual * residual, axis=-1, keepdims=True) + norm_eps)
        two = (residual * factor * gain_ref[...]).astype(jnp.bfloat16)
        two_ref[rows, :] = two
        wide_ref[...] = two.astype(jnp.float32)


def norm_back_kernel(*refs):
    part_refs, x_refs = refs[:3], refs[3:6]
    residual_ref, gain_ref, branch_ref, grad_ref, grad_low_ref, gain_grad_ref = refs[6:]
    gain_grad = jnp.zeros(gain_grad_ref.shape, jnp.float32)
    first = 0
    for part_ref, x_ref in zip(part_refs, x_refs):
        rows = slice(first, first + part_ref.shape[0])
        first += part_ref.shape[0]
        residual = residual_ref[rows, :]
        upstream = part_ref[...] + x_ref[...]
        factor = lax.rsqrt(jnp.mean(residual * residual, axis=-1, keepdims=True) + norm_eps)
        gain_grad += jnp.sum(upstream * (residual * factor), axis=0, keepdims=True)
        grad = norm_back(residual, factor, gain_ref[...], upstream) + branch_ref[rows, :].astype(jnp.float32)
        grad_ref[rows, :] = grad
        grad_low_ref[rows, :] = grad.astype(jnp.bfloat16)
    gain_grad_ref[...] = gain_grad


def tokens_back_kernel(
    tokens_ref, low_ref, high_ref, low_x_ref, high_x_ref, gain_ref, residual_ref, out_grad_ref, alive_ref, grad_ref
):
    half = low_ref.shape[0]
    for first, part_ref, x_ref in ((0, low_ref, low_x_ref), (half, high_ref, high_x_ref)):
        rows = slice(first, first + half)
        inputs = tokens_ref[rows, :].astype(jnp.float32)
        factor = lax.rsqrt(jnp.mean(inputs * inputs, axis=-1, keepdims=True) + norm_eps)
        grad = norm_back(inputs, factor, gain_ref[...], part_ref[...] + x_ref[...])
        upstream = out_grad_ref[rows, :].astype(jnp.float32)
        total = upstream * (1.0 - alive_ref[rows, :]) + residual_ref[rows, :] + grad
        grad_ref[rows, :] = total.astype(jnp.bfloat16)


def attend_back_kernel(
    heads,
    residual_ref,
    o_ref,
    weight_ref,
    turned_ref,
    top_ref,
    mass_ref,
    cosine_ref,
    sine_ref,
    begins_ref,
    tokens_ref,
    rows_ref,
    low_ref,
    high_ref,
    gain_grad_ref,
    mixed_ref,
    across_ref,
    key_ref,
    value_ref,
):
    mixed_ref[...] = contract(o_ref[...], residual_ref[...], 1, 1).astype(jnp.bfloat16)
    cosine, sine_table = cosine_ref[...], -sine_ref[...]
    k, v = heads * HD, (heads + 1) * HD
    keys_across = turned_ref[k:v, :]
    key_rows = keys_across.astype(jnp.float32).T.astype(jnp.bfloat16)
    value_rows = turned_ref[v:, :].astype(jnp.float32).T.astype(jnp.bfloat16)
    blocks = list(blocks_of(begins_ref, residual_ref.shape[0]))
    key_ref[...] = jnp.zeros(key_ref.shape, jnp.float32)
    value_ref[...] = jnp.zeros(value_ref.shape, jnp.float32)

    def head(h, carry):
        r = pl.ds(pl.multiple_of(h * HD, HD), HD)
        for cols, keys, allowed in blocks:
            query, grad = turned_ref[r, cols], mixed_ref[r, cols]
            scores = contract(key_rows[:keys], query, 1, 0) * HD ** (-0.5)
            scores = jnp.where(allowed, scores, -1e30)
            probs = jnp.exp(scores - top_ref[pl.ds(h, 1), cols]) * mass_ref[pl.ds(h, 1), cols]
            prob_grad = contract(value_rows[:keys], grad, 1, 0)
            inner_sum = jnp.sum(probs * prob_grad, axis=0, keepdims=True)
            score_grad = (probs * (prob_grad - inner_sum)).astype(jnp.bfloat16)
            query_grad = contract(keys_across[:, :keys], score_grad, 1, 0) * HD ** (-0.5)
            across_ref[r, cols] = turn(query_grad, cosine[:, cols], sine_table[:, cols])
            key_ref[:keys, :] += contract(score_grad, query, 1, 1)
            value_ref[:keys, :] += contract(probs.astype(jnp.bfloat16), grad, 1, 1)
        return carry

    lax.fori_loop(0, heads, head, 0)
    across_ref[k:v, :] = turn(key_ref[...].T * HD ** (-0.5), cosine, sine_table)
    across_ref[v : v + HD, :] = value_ref[...].T
    rows_ref[...] = across_ref[...].T[:, : v + HD].astype(jnp.bfloat16)

    def step(start, size):
        c = pl.ds(start, size)
        part = contract(rows_ref[...], weight_ref[:, c], 1, 0)
        put((low_ref, high_ref), part, c)
        gain_grad_ref[:, c] = jnp.sum(part * (tokens_ref[:, c].astype(jnp.float32) * factor), axis=0, keepdims=True)

    inputs = tokens_ref[...].astype(jnp.float32)
    factor = lax.rsqrt(jnp.mean(inputs * inputs, axis=-1, keepdims=True) + norm_eps)
    over(low_ref.shape[1], 256, step)


def ffn_kernel(two_ref, branch_ref, gate_ref, up_ref, down_ref, hidden_ref, gate_rows_ref, up_rows_ref, *low_refs):
    if low_refs:
        for wide_ref, low_ref in zip((two_ref, branch_ref), low_refs):
            low_ref[...] = wide_ref[...].astype(jnp.bfloat16)
        two_ref, branch_ref = low_refs

    def step(start, size):
        c = pl.ds(start, size)
        gate = contract(two_ref[...], gate_ref[:, c], 1, 0)
        up = contract(two_ref[...], up_ref[:, c], 1, 0)
        hidden_grad = contract(branch_ref[...], down_ref[c, :], 1, 1)
        sigmoid_gate = 0.5 * jnp.tanh(0.5 * gate) + 0.5
        silu_gate = gate * sigmoid_gate
        hidden_ref[:, c] = (silu_gate * up).astype(jnp.bfloat16)
        gate_rows_ref[:, c] = (hidden_grad * up * (sigmoid_gate + silu_gate * (1.0 - sigmoid_gate))).astype(jnp.bfloat16)
        up_rows_ref[:, c] = (hidden_grad * silu_gate).astype(jnp.bfloat16)

    over(gate_ref.shape[1], 768, step)


def ffn_rows(rows, branch, gate_weight, up_weight, down_weight):
    wide = ((rows.shape[0], gate_weight.shape[1]), jnp.bfloat16)
    low = [(rows.shape, jnp.bfloat16)] * 2 if rows.dtype == jnp.float32 else []
    return call(ffn_kernel, "ffn_rows", [wide] * 3 + low, rows, branch, gate_weight, up_weight, down_weight)


def back_kernel(first, gate_rows_ref, up_rows_ref, gate_ref, up_ref, *part_refs):
    rows = pl.ds(first, len(part_refs) * part_refs[0].shape[0])

    def step(start, size):
        c = pl.ds(start, size)
        total = contract(gate_rows_ref[rows, :], gate_ref[c, :], 1, 1) + contract(
            up_rows_ref[rows, :], up_ref[c, :], 1, 1
        )
        put(part_refs, total, c)

    over(gate_ref.shape[0], 256, step)


def ffn_back(gate_rows, up_rows, gate_weight, up_weight, first, counts):
    shapes = [((count, gate_weight.shape[0]), jnp.float32) for count in counts]
    kernel = functools.partial(back_kernel, first)
    return call(kernel, "ffn_back", shapes, gate_rows, up_rows, gate_weight, up_weight)


def down_kernel(hidden_ref, down_ref, low_ref, high_ref):
    def step(start, size):
        c = pl.ds(start, size)
        put((low_ref, high_ref), contract(hidden_ref[...], down_ref[:, c], 1, 0), c)

    over(down_ref.shape[1], 256, step)


def ffn_down(hidden, down_weight):
    shape = ((hidden.shape[0] // 2, down_weight.shape[1]), jnp.float32)
    return call(down_kernel, "ffn_down", [shape] * 2, hidden, down_weight)


def sums_kernel(pieces, cuts, chosen_ref, *refs):
    rows_refs, feature_refs, refs = refs[:pieces], refs[pieces : 2 * pieces], refs[2 * pieces :]
    picked = [contract(chosen_ref[...], r[...], 1, 1).astype(jnp.bfloat16) for r in rows_refs]

    def step(start, size):
        c = pl.ds(start, size)
        total = sum(contract(p, f[:, c], 1, 0) for p, f in zip(picked, feature_refs))
        if len(refs) == cuts:
            put(refs, total, c)
        else:
            total = total + jnp.concatenate([r[:, c] for r in refs[:cuts]])
            put(refs[cuts:], total, c)

    over(feature_refs[0].shape[1], 640, step)


def put(refs, total, c):
    size = total.shape[0] // len(refs)
    for i, ref in enumerate(refs):
        ref[:, c] = total[i * size : (i + 1) * size]


def outer_sums(chosen, rows, features):
    shape = ((chosen.shape[0] // CUTS, features[0].shape[1]), jnp.float32)
    kernel = functools.partial(sums_kernel, len(rows), CUTS)
    return call(kernel, "outer_sums", [shape] * CUTS, chosen, *rows, *features)


def outer_fold(chosen, rows, features, arrived):
    shape = ((chosen.shape[0] // 2, features[0].shape[1]), jnp.float32)
    kernel = functools.partial(sums_kernel, len(rows), CUTS)
    return call(kernel, "outer_fold", [shape] * 2, chosen, *rows, *features, *arrived)


def swap_cuts(cuts, bit):
    return [swap_dp(cut, bit) for cut in cuts]


def attn_sums_kernel(block, chosen_ref, gains_ref, normed_ref, residual_ref, qkv_ref, mixed_ref, *refs):
    count = chosen_ref.shape[0]
    chosen = chosen_ref[...]
    qkv_width = qkv_ref.shape[1]
    o_start = qkv_width + gains_ref.shape[1]
    ones_row = lax.broadcasted_iota(jnp.int32, (count, normed_ref.shape[0]), 0) % (block + EXTRA) == block
    picked = contract(chosen, normed_ref[...], 1, 1)
    picked = jnp.where(ones_row, 1.0, picked).astype(jnp.bfloat16)
    gains = jnp.dot(
        chosen.astype(jnp.float32), gains_ref[...], preferred_element_type=jnp.float32, precision=lax.Precision.HIGHEST
    )
    picked_residual = contract(chosen, residual_ref[...], 1, 1).astype(jnp.bfloat16)
    total = jnp.concatenate(
        [
            contract(picked, qkv_ref[...], 1, 0),
            gains,
            contract(picked_residual, mixed_ref[...], 1, 0),
            jnp.zeros((count, -mixed_ref.shape[1] % 128), jnp.float32),
        ],
        axis=1,
    )
    if len(refs) == ATTN_CUTS:
        put(refs, total, slice(None))
    else:
        total = total + jnp.concatenate([r[...] for r in refs[:ATTN_CUTS]])
        put(refs[ATTN_CUTS:], total, slice(None))


def attn_sums(block, chosen, gains, normed, residual_low, qkv_rows, mixed, arrived=None):
    count = chosen.shape[0]
    features = qkv_rows.shape[1] + gains.shape[1] + -(-mixed.shape[1] // 128) * 128
    kernel = functools.partial(attn_sums_kernel, block)
    operands = (chosen, gains, normed, residual_low, qkv_rows, mixed)
    if arrived is None:
        return call(kernel, "attn_sums", [((count // ATTN_CUTS, features), jnp.float32)] * ATTN_CUTS, *operands)
    return call(kernel, "attn_fold", [((count // 2, features), jnp.float32)] * 2, *operands, *arrived)


def on_device(
    tokens,
    out_grad,
    doc_lengths,
    q_weight,
    k_weight,
    v_weight,
    q_bias,
    k_bias,
    v_bias,
    o_weight,
    attn_gain,
    ffn_gain,
    gate_weight,
    up_weight,
    down_weight,
):
    row_total, width = tokens.shape
    local_heads = q_weight.shape[1] // HD
    local_kv = k_weight.shape[1] // HD
    dp_size = lax.axis_size("dp")
    dp_bits = dp_size.bit_length() - 1
    pair_bit = 2
    ffn_order = (0, 1) + tuple(range(3, dp_bits))
    attn_order = (0, 1, pair_bit) + tuple(range(3, dp_bits))
    own = lax.axis_index("dp")
    positions, alive = layout(doc_lengths[0], row_total)
    cosine, sine_table = rotary(positions, HD)
    alive_rows = alive.astype(jnp.float32)[:, None]
    places = jnp.arange(row_total, dtype=jnp.int32)
    o_half = o_weight.shape[0] // 2
    o_first = own & 1
    upstream = out_grad.astype(jnp.float32)
    branch_wide = upstream * alive_rows
    o_mine = lax.dynamic_slice_in_dim(o_weight, o_first * o_half, o_half).astype(jnp.float32)
    o_same = swap_tensor(o_mine)
    half_rows = row_total // 2
    pair_branch = swap_dp(branch_wide, pair_bit)
    ffn_keep, ffn_send = dest_columns(width, ffn_order, (pair_bit,))
    attn_keep, attn_send = dest_columns(width, attn_order, extra=EXTRA)
    branch_grad = branch_wide.astype(jnp.bfloat16)
    inputs = tokens.astype(jnp.float32)
    gain_one = attn_gain.astype(jnp.float32)
    gain_two = ffn_gain.astype(jnp.float32)
    qkv_across = jnp.concatenate([q_weight.T, k_weight.T, v_weight.T])
    qkv_bias = jnp.concatenate([q_bias.reshape(-1), k_bias.reshape(-1), v_bias.reshape(-1)]).astype(jnp.float32)
    q_width = local_heads * HD
    k_width = local_kv * HD
    qkv_width = q_width + 2 * k_width
    begins = (places - positions)[None, :]
    padded = -(-qkv_width // 128) * 128
    row_stats = ((-(-local_heads // 8) * 8, row_total), jnp.float32)
    normed, turned, mixed_heads, mixed_wide, top_score, mass = call(
        functools.partial(attend_kernel, local_heads),
        "attend",
        [
            ((row_total, width), jnp.bfloat16),
            ((qkv_width, row_total), jnp.bfloat16),
            ((row_total, q_width), jnp.bfloat16),
            ((q_width, row_total), jnp.float32),
            row_stats,
            row_stats,
        ],
        tokens,
        gain_one[None, :],
        qkv_across,
        qkv_bias[:, None],
        cosine,
        sine_table,
        begins,
        scratch=[((qkv_width, row_total), jnp.float32), ((-(-q_width // 128) * 128, row_total), jnp.float32)],
    )
    mixed_other = swap_tensor(mixed_wide)
    o_same = after(o_same, mixed_heads)
    o_cross = swap_dp(o_same, 0)
    residual, normed_two, low_wide, high_wide = call(
        project_kernel,
        "project",
        [
            ((row_total, width), jnp.float32),
            ((row_total, width), jnp.bfloat16),
            ((half_rows, width), jnp.float32),
            ((half_rows, width), jnp.float32),
        ],
        jnp.broadcast_to(o_first.astype(jnp.float32), (1, width)),
        tokens,
        mixed_heads,
        after(mixed_other, o_cross, ffn_keep, ffn_send, attn_keep, attn_send, branch_grad),
        o_weight,
        o_same,
        o_cross,
        gain_two[None, :],
        scratch=[((q_width, width), jnp.bfloat16)],
    )
    low_two = swap_dp(low_wide, pair_bit)
    high_two = swap_dp(high_wide, pair_bit)
    ffn_weights = (gate_weight, up_weight, down_weight)

    hidden_act, gate_grad_rows, up_grad_rows = ffn_rows(normed_two, branch_grad, *ffn_weights)
    quarter = half_rows // 2
    backward = (up_grad_rows, gate_weight, up_weight)
    (low_part,) = ffn_back(after(gate_grad_rows, pair_branch), *backward, 0, [half_rows])
    low_from_x = swap_tensor(low_part)
    mid_part, high_part = ffn_back(after(gate_grad_rows, low_part), *backward, half_rows, [quarter] * 2)
    low_branch, high_branch = pair_branch[:half_rows], pair_branch[half_rows:]
    low_hidden, low_gate, low_up, low_two, low_branch = ffn_rows(after(low_two, high_part), low_branch, *ffn_weights)
    low_down, high_down = ffn_down(after(hidden_act, low_hidden), down_weight)
    mid_from_x = swap_tensor(after(mid_part, low_hidden))
    high_from_x = swap_tensor(after(high_part, low_hidden))
    high_hidden, high_gate, high_up, high_two, high_branch = ffn_rows(
        after(high_two, low_down, low_from_x), high_branch, *ffn_weights
    )
    branch_rows = (branch_grad, low_branch, high_branch)
    two_rows = (normed_two, low_two, high_two)
    down_sums = outer_sums(ffn_send, branch_rows, (hidden_act, low_hidden, high_hidden))
    down_sent = swap_cuts(down_sums, 0)
    gate_sums = outer_sums(after(ffn_send, mid_from_x, *down_sums), two_rows, (gate_grad_rows, low_gate, high_gate))
    gate_sent = swap_cuts(gate_sums, 0)
    up_sums = outer_sums(after(ffn_send, *gate_sums), two_rows, (up_grad_rows, low_up, high_up))
    up_sent = swap_cuts(up_sums, 0)
    down_keep, down_send = outer_fold(
        after(ffn_keep, high_from_x, *up_sums), branch_rows, (hidden_act, low_hidden, high_hidden), down_sent
    )
    gate_keep, gate_send = outer_fold(
        after(ffn_keep, down_send), two_rows, (gate_grad_rows, low_gate, high_gate), gate_sent
    )
    up_keep, up_send = outer_fold(after(ffn_keep, gate_send), two_rows, (up_grad_rows, low_up, high_up), up_sent)
    down_from_y, gate_from_y, up_from_y = (swap_dp(v, ffn_order[1]) for v in (down_send, gate_send, up_send))
    low_down_x = swap_tensor(after(low_down, high_from_x))
    wide, low = ((row_total, width), jnp.float32), ((row_total, width), jnp.bfloat16)
    gain_row = ((1, width), jnp.float32)
    residual_grad, residual_low, ffn_gain_sum = call(
        norm_back_kernel,
        "norm_back",
        [wide, low, gain_row],
        low_part,
        mid_part,
        high_part,
        low_from_x,
        mid_from_x,
        after(high_from_x, up_send),
        residual,
        gain_two[None, :],
        branch_grad,
    )
    down_keep, down_send = step_on(down_keep, down_from_y)
    down_from_z = swap_dp(down_send, ffn_order[2])
    half_wide = ((half_rows, width), jnp.float32)
    qkv_grad_rows, low_normed, high_normed, attn_gain_part = call(
        functools.partial(attend_back_kernel, local_heads),
        "attend_back",
        [((row_total, qkv_width), jnp.bfloat16), half_wide, half_wide, gain_row],
        residual_low,
        o_weight,
        qkv_across,
        turned,
        top_score,
        mass,
        cosine,
        sine_table,
        begins,
        tokens,
        scratch=[
            ((q_width, row_total), jnp.bfloat16),
            ((padded, row_total), jnp.float32),
            ((row_total, HD), jnp.float32),
            ((row_total, HD), jnp.float32),
        ],
    )
    gain_sums = jnp.concatenate([attn_gain_part + swap_tensor(attn_gain_part), ffn_gain_sum])
    low_other = swap_tensor(after(low_normed, gain_sums))
    high_other = swap_tensor(after(high_normed, gain_sums))
    gain_columns = jnp.pad(gain_sums, ((0, -qkv_width % 128 - 2), (0, 0))).T
    attn_operands = (gain_columns, normed, residual_low, qkv_grad_rows, mixed_heads)
    gain_block = width // dp_size
    attn_sent = swap_cuts(
        attn_sums(gain_block, after(attn_send, low_down_x), *attn_operands), attn_order[0]
    )
    gate_keep, gate_send = step_on(gate_keep, gate_from_y)
    gate_from_z = swap_dp(gate_send, ffn_order[2])
    attn_part, attn_next = attn_sums(
        gain_block, after(attn_keep, gate_send, down_from_z), *attn_operands, attn_sent
    )
    attn_from_z = swap_dp(attn_next, attn_order[1])
    high_down_x = swap_tensor(after(high_down, attn_next))
    up_keep, up_send = step_on(up_keep, after(up_from_y, attn_next, low_other))
    up_from_z = swap_dp(up_send, ffn_order[2])
    attn_part, attn_next = step_on(attn_part, after(attn_from_z, up_send))
    attn_from_y = swap_dp(attn_next, attn_order[2])
    attn_part, attn_next = step_on(attn_part, after(attn_from_y, gate_from_z))
    attn_from_z = swap_dp(after(attn_next, up_from_z), attn_order[3])
    attn_grad = close(attn_part, attn_from_z, attn_order[4:])
    (tokens_grad,) = call(
        tokens_back_kernel,
        "tokens_back",
        [low],
        tokens,
        low_normed,
        high_normed,
        low_other,
        after(high_other, up_send),
        gain_one[None, :],
        residual_grad,
        out_grad,
        alive_rows,
    )
    block_out = residual + jnp.concatenate([low_down + low_down_x, high_down + high_down_x])
    o_start = -(-qkv_width // 128) * 128
    qkv_grad, o_grad = attn_grad[:gain_block, :qkv_width], attn_grad[:gain_block, o_start : o_start + q_width]
    attn_gain_grad, ffn_gain_grad = attn_grad[:gain_block, qkv_width], attn_grad[:gain_block, qkv_width + 1]
    bias_heads = attn_grad[gain_block, :qkv_width].reshape(local_heads + 2 * local_kv, HD)
    bias_block = HD // dp_size
    bias_own = lax.dynamic_slice_in_dim(bias_heads, own * bias_block, bias_block, axis=1)
    down_grad, gate_grad, up_grad = (
        close(keep, got, ffn_order[3:])
        for keep, got in ((down_keep, down_from_z), (gate_keep, gate_from_z), (up_keep, up_from_z))
    )
    layer_out = jnp.where(alive[:, None], block_out, inputs).astype(jnp.bfloat16)
    return (
        layer_out,
        tokens_grad,
        qkv_grad[:, :q_width],
        qkv_grad[:, q_width : q_width + k_width],
        qkv_grad[:, q_width + k_width :],
        bias_own[:local_heads],
        bias_heads[local_heads : local_heads + local_kv],
        bias_own[local_heads + local_kv :],
        o_grad.T,
        attn_gain_grad,
        ffn_gain_grad,
        gate_grad,
        up_grad,
        down_grad.T,
    )


def solution(mesh):
    return jax.shard_map(
        on_device,
        mesh=mesh,
        in_specs=(
            P("dp", None),
            P("dp", None),
            P("dp", None),
            P(None, "tensor"),
            P(None, "tensor"),
            P(None, "tensor"),
            P("tensor", None),
            P("tensor", None),
            P("tensor", None),
            P("tensor", None),
            P(),
            P(),
            P(None, "tensor"),
            P(None, "tensor"),
            P("tensor", None),
        ),
        out_specs=(
            P("dp", None),
            P("dp", None),
            P("dp", "tensor"),
            P("dp", "tensor"),
            P("dp", "tensor"),
            P("tensor", "dp"),
            P("tensor", None),
            P("tensor", "dp"),
            P("tensor", "dp"),
            P("dp"),
            P("dp"),
            P("dp", "tensor"),
            P("dp", "tensor"),
            P("tensor", "dp"),
        ),
        check_vma=False,
    )
```

```python
import functools
import math

import jax
import jax.numpy as jnp
from jax import lax
from jax.experimental import pallas as pl
from jax.experimental.pallas import tpu as pltpu
from jax.sharding import PartitionSpec as P

HD = 64


norm_eps = 1e-06
rope_base = 1000000.0


def layout(lengths, row_total):
    doc_ends = jnp.cumsum(lengths)
    places = jnp.arange(row_total, dtype=jnp.int32)
    passed = (places[:, None] >= doc_ends[None, :]).astype(jnp.int32)
    begins = jnp.sum(passed * lengths[None, :], axis=1)
    alive = places < doc_ends[-1]
    return (places - begins, alive)


def rotary(positions, width):
    half_width = width // 2
    inv_freq = jnp.exp(
        jnp.arange(half_width, dtype=jnp.float32) * (-2.0 * math.log(rope_base) / width)
    )
    angles = inv_freq[:, None] * positions.astype(jnp.float32)[None, :]
    return (jnp.cos(angles), jnp.sin(angles))


def norm_back(inputs, factor, gain, upstream):
    scaled = upstream * gain
    return factor * scaled - inputs * factor**3 * jnp.mean(scaled * inputs, axis=-1, keepdims=True)


def swap_tensor(rows):
    size = lax.axis_size("tensor")
    return lax.ppermute(rows, "tensor", [(i, i ^ 1) for i in range(size)])


def swap_dp(rows, bit):
    size = lax.axis_size("dp")
    return lax.ppermute(rows, "dp", [(i, i ^ (1 << bit)) for i in range(size)])


def after(value, *others):
    return lax.optimization_barrier((value, *others))[0]


def dest_columns(width, order, fixed=(), extra=0):
    steps = len(order)
    block = width >> (steps + len(fixed))
    whole = block + extra
    count = whole << steps
    own = lax.axis_index("dp")
    places = jnp.arange(count, dtype=jnp.int32)
    spot = places // whole
    flip = jnp.zeros_like(spot)
    for j, bit in enumerate(order):
        flip = flip + (((spot >> (steps - 1 - j)) & 1) << bit)
    within = places % whole
    source = jnp.where(within < block, (own ^ flip) * block + within, -1)
    chosen = (source[:, None] == jnp.arange(width, dtype=jnp.int32)[None, :]).astype(jnp.bfloat16)
    return chosen[: count // 2], chosen[count // 2 :]


def finish(keep, send, order):
    for bit in order[:-1]:
        sent = swap_dp(send, bit)
        half = sent.shape[0] // 2
        send = keep[half:] + sent[half:]
        keep = keep[:half] + sent[:half]
    return keep + swap_dp(send, order[-1])


def close(keep, sent, order):
    return finish(*step_on(keep, sent), order) if order else keep + sent


def step_on(keep, sent):
    half = sent.shape[0] // 2
    return keep[:half] + sent[:half], keep[half:] + sent[half:]


IN_VMEM = pl.BlockSpec(memory_space=pltpu.VMEM)
LIMIT = 16
EXTRA = 8
ROWS = 64
CUTS = 4
ATTN_CUTS = 4


def contract(left, right, left_dim, right_dim):
    return lax.dot_general(
        left, right, (((left_dim,), (right_dim,)), ((), ())), preferred_element_type=jnp.float32
    )


def over(total, size, step):
    count, rest = divmod(total, size)

    def turn(i, carry):
        step(pl.multiple_of(i * size, size), size)
        return carry

    lax.fori_loop(0, count, turn, 0)
    if rest:
        step(count * size, rest)


def call(kernel, name, shapes, *operands, scratch=()):
    return pl.pallas_call(
        kernel,
        in_specs=[IN_VMEM] * len(operands),
        out_specs=[IN_VMEM] * len(shapes),
        out_shape=[jax.ShapeDtypeStruct(shape, dtype) for shape, dtype in shapes],
        compiler_params=pltpu.CompilerParams(vmem_limit_bytes=LIMIT * 2**20),
        cost_estimate=pl.CostEstimate(flops=1000, bytes_accessed=1000, transcendentals=0),
        scratch_shapes=[pltpu.VMEM(shape, dtype) for shape, dtype in scratch],
        name=name,
    )(*operands)


def turn(pairs, cosine, sine_table):
    half = pairs.shape[0] // 2
    front, back = pairs[:half], pairs[half:]
    return jnp.concatenate([front * cosine - back * sine_table, back * cosine + front * sine_table], axis=0)


def blocks_of(begins_ref, row_total):
    size = row_total // 2
    for first in range(0, row_total, size):
        keys = first + size
        key_place = lax.broadcasted_iota(jnp.int32, (keys, size), 0)
        query_place = lax.broadcasted_iota(jnp.int32, (keys, size), 1) + first
        allowed = (key_place >= begins_ref[:, first:keys]) & (key_place <= query_place)
        yield slice(first, keys), keys, allowed


def attend_kernel(
    heads,
    tokens_ref,
    gain_ref,
    weight_ref,
    bias_ref,
    cosine_ref,
    sine_ref,
    begins_ref,
    normed_ref,
    turned_ref,
    mixed_ref,
    mixed_wide_ref,
    top_ref,
    mass_ref,
    pre_ref,
    mixed_across_ref,
):

    def norm(start):
        rows = pl.ds(start, ROWS)
        inputs = tokens_ref[rows, :].astype(jnp.float32)
        factor = lax.rsqrt(jnp.mean(inputs * inputs, axis=-1, keepdims=True) + norm_eps)
        normed_ref[rows, :] = (inputs * factor * gain_ref[...]).astype(jnp.bfloat16)

    row_blocks(tokens_ref.shape[0], norm)
    pre_ref[...] = contract(weight_ref[...], normed_ref[...], 1, 1) + bias_ref[...]
    cosine, sine_table = cosine_ref[...], sine_ref[...]

    def rope(h, carry):
        r = pl.ds(pl.multiple_of(h * HD, HD), HD)
        turned_ref[r, :] = turn(pre_ref[r, :], cosine, sine_table).astype(jnp.bfloat16)
        return carry

    lax.fori_loop(0, heads + 1, rope, 0)
    value_rows = pre_ref[(heads + 1) * HD :, :].astype(jnp.bfloat16)
    turned_ref[(heads + 1) * HD :, :] = value_rows
    key_rows = turned_ref[heads * HD : (heads + 1) * HD, :].astype(jnp.float32).T.astype(jnp.bfloat16)
    blocks = list(blocks_of(begins_ref, tokens_ref.shape[0]))

    def head(h, carry):
        r = pl.ds(pl.multiple_of(h * HD, HD), HD)
        for cols, keys, allowed in blocks:
            scores = contract(key_rows[:keys], turned_ref[r, cols], 1, 0) * HD ** (-0.5)
            scores = jnp.where(allowed, scores, -1e30)
            top = jnp.max(scores, axis=0, keepdims=True)
            exp_scores = jnp.exp(scores - top)
            mass = 1.0 / jnp.sum(exp_scores, axis=0, keepdims=True)
            low_probs = (exp_scores * mass).astype(jnp.bfloat16)
            mixed_across_ref[r, cols] = contract(value_rows[:, :keys], low_probs, 1, 0)
            top_ref[pl.ds(h, 1), cols] = top
            mass_ref[pl.ds(h, 1), cols] = mass
        return carry

    lax.fori_loop(0, heads, head, 0)
    mixed_wide_ref[...] = mixed_across_ref[: heads * HD, :].astype(jnp.bfloat16).astype(jnp.float32)
    mixed_ref[...] = mixed_across_ref[...].T[:, : heads * HD].astype(jnp.bfloat16)


def project_kernel(
    first_ref,
    tokens_ref,
    mixed_ref,
    other_ref,
    o_ref,
    same_ref,
    cross_ref,
    gain_ref,
    residual_ref,
    two_ref,
    low_ref,
    high_ref,
    o_other_ref,
):
    first = first_ref[...] == 0.0
    o_half = same_ref.shape[0]
    same, cross = same_ref[...], cross_ref[...]
    o_other_ref[:o_half, :] = jnp.where(first, same, cross).astype(jnp.bfloat16)
    o_other_ref[o_half:, :] = jnp.where(first, cross, same).astype(jnp.bfloat16)
    half = low_ref.shape[0]
    for rows, wide_ref in ((slice(0, half), low_ref), (slice(half, 2 * half), high_ref)):
        other = other_ref[:, rows].T.astype(jnp.bfloat16)
        residual = tokens_ref[rows, :].astype(jnp.float32) + (
            contract(mixed_ref[rows, :], o_ref[...], 1, 0) + contract(other, o_other_ref[...], 1, 0)
        )
        residual_ref[rows, :] = residual
        factor = lax.rsqrt(jnp.mean(residual * residual, axis=-1, keepdims=True) + norm_eps)
        two = (residual * factor * gain_ref[...]).astype(jnp.bfloat16)
        two_ref[rows, :] = two
        wide_ref[...] = two.astype(jnp.float32)


def row_blocks(count, step):
    def turn_on(i, carry):
        step(pl.multiple_of(i * ROWS, ROWS))
        return carry

    lax.fori_loop(0, count // ROWS, turn_on, 0)


def norm_back_kernel(*refs):
    part_refs, x_refs = refs[:2], refs[2:4]
    residual_ref, gain_ref, branch_ref, grad_ref, grad_low_ref, gain_grad_ref = refs[4:]
    gain_grad_ref[...] = jnp.zeros(gain_grad_ref.shape, jnp.float32)
    first = 0
    for part_ref, x_ref in zip(part_refs, x_refs):

        def step(start, part_ref=part_ref, x_ref=x_ref, first=first):
            here, rows = pl.ds(start, ROWS), pl.ds(first + start, ROWS)
            residual = residual_ref[rows, :]
            upstream = part_ref[here, :] + x_ref[here, :]
            factor = lax.rsqrt(jnp.mean(residual * residual, axis=-1, keepdims=True) + norm_eps)
            gain_grad_ref[...] += jnp.sum(upstream * (residual * factor), axis=0, keepdims=True)
            grad = norm_back(residual, factor, gain_ref[...], upstream) + branch_ref[rows, :].astype(jnp.float32)
            grad_ref[rows, :] = grad
            grad_low_ref[rows, :] = grad.astype(jnp.bfloat16)

        row_blocks(part_ref.shape[0], step)
        first += part_ref.shape[0]


def tokens_back_kernel(
    tokens_ref, low_ref, high_ref, low_x_ref, high_x_ref, gain_ref, residual_ref, out_grad_ref, alive_ref, grad_ref
):
    half = low_ref.shape[0]
    for first, part_ref, x_ref in ((0, low_ref, low_x_ref), (half, high_ref, high_x_ref)):

        def step(start, part_ref=part_ref, x_ref=x_ref, first=first):
            here, rows = pl.ds(start, ROWS), pl.ds(first + start, ROWS)
            inputs = tokens_ref[rows, :].astype(jnp.float32)
            factor = lax.rsqrt(jnp.mean(inputs * inputs, axis=-1, keepdims=True) + norm_eps)
            grad = norm_back(inputs, factor, gain_ref[...], part_ref[here, :] + x_ref[here, :])
            upstream = out_grad_ref[rows, :].astype(jnp.float32)
            total = upstream * (1.0 - alive_ref[rows, :]) + residual_ref[rows, :] + grad
            grad_ref[rows, :] = total.astype(jnp.bfloat16)

        row_blocks(half, step)


def attend_back_kernel(
    heads,
    residual_ref,
    o_ref,
    weight_ref,
    turned_ref,
    top_ref,
    mass_ref,
    cosine_ref,
    sine_ref,
    begins_ref,
    tokens_ref,
    rows_ref,
    low_ref,
    high_ref,
    gain_grad_ref,
    mixed_ref,
    across_ref,
    key_ref,
    value_ref,
):
    mixed_ref[...] = contract(o_ref[...], residual_ref[...], 1, 1).astype(jnp.bfloat16)
    cosine, sine_table = cosine_ref[...], -sine_ref[...]
    k, v = heads * HD, (heads + 1) * HD
    keys_across = turned_ref[k:v, :]
    key_rows = keys_across.astype(jnp.float32).T.astype(jnp.bfloat16)
    value_rows = turned_ref[v:, :].astype(jnp.float32).T.astype(jnp.bfloat16)
    blocks = list(blocks_of(begins_ref, residual_ref.shape[0]))
    key_ref[...] = jnp.zeros(key_ref.shape, jnp.float32)
    value_ref[...] = jnp.zeros(value_ref.shape, jnp.float32)

    def head(h, carry):
        r = pl.ds(pl.multiple_of(h * HD, HD), HD)
        for cols, keys, allowed in blocks:
            query, grad = turned_ref[r, cols], mixed_ref[r, cols]
            scores = contract(key_rows[:keys], query, 1, 0) * HD ** (-0.5)
            scores = jnp.where(allowed, scores, -1e30)
            probs = jnp.exp(scores - top_ref[pl.ds(h, 1), cols]) * mass_ref[pl.ds(h, 1), cols]
            prob_grad = contract(value_rows[:keys], grad, 1, 0)
            inner_sum = jnp.sum(probs * prob_grad, axis=0, keepdims=True)
            score_grad = (probs * (prob_grad - inner_sum)).astype(jnp.bfloat16)
            query_grad = contract(keys_across[:, :keys], score_grad, 1, 0) * HD ** (-0.5)
            across_ref[r, cols] = turn(query_grad, cosine[:, cols], sine_table[:, cols])
            key_ref[:keys, :] += contract(score_grad, query, 1, 1)
            value_ref[:keys, :] += contract(probs.astype(jnp.bfloat16), grad, 1, 1)
        return carry

    lax.fori_loop(0, heads, head, 0)
    across_ref[k:v, :] = turn(key_ref[...].T * HD ** (-0.5), cosine, sine_table)
    across_ref[v : v + HD, :] = value_ref[...].T
    rows_ref[...] = across_ref[...].T[:, : v + HD].astype(jnp.bfloat16)

    def step(start, size):
        c = pl.ds(start, size)
        part = contract(rows_ref[...], weight_ref[:, c], 1, 0)
        put((low_ref, high_ref), part, c)
        gain_grad_ref[:, c] = jnp.sum(part * (tokens_ref[:, c].astype(jnp.float32) * factor), axis=0, keepdims=True)

    inputs = tokens_ref[...].astype(jnp.float32)
    factor = lax.rsqrt(jnp.mean(inputs * inputs, axis=-1, keepdims=True) + norm_eps)
    over(low_ref.shape[1], 256, step)


def ffn_kernel(*refs):
    if len(refs) == 12:
        side_ref, mine_ref, other_ref, branch_ref, *refs, two_ref, branch_low_ref = refs
        gate_ref, up_ref, down_ref, hidden_ref, gate_rows_ref, up_rows_ref = refs
        half = mine_ref.shape[0]
        first = side_ref[...] == 0.0
        mine, other = mine_ref[...], other_ref[...]
        two_ref[:half, :] = jnp.where(first, mine, other).astype(jnp.bfloat16)
        two_ref[half:, :] = jnp.where(first, other, mine).astype(jnp.bfloat16)
        branch_low_ref[...] = branch_ref[...].astype(jnp.bfloat16)
        low_refs, branch_ref = (), branch_low_ref
    else:
        two_ref, branch_ref, gate_ref, up_ref, down_ref, hidden_ref, gate_rows_ref, up_rows_ref, *low_refs = refs
    if low_refs:
        for wide_ref, low_ref in zip((two_ref, branch_ref), low_refs):
            low_ref[...] = wide_ref[...].astype(jnp.bfloat16)
        two_ref, branch_ref = low_refs

    def step(start, size):
        c = pl.ds(start, size)
        gate = contract(two_ref[...], gate_ref[:, c], 1, 0)
        up = contract(two_ref[...], up_ref[:, c], 1, 0)
        hidden_grad = contract(branch_ref[...], down_ref[c, :], 1, 1)
        sigmoid_gate = 0.5 * jnp.tanh(0.5 * gate) + 0.5
        silu_gate = gate * sigmoid_gate
        hidden_ref[:, c] = (silu_gate * up).astype(jnp.bfloat16)
        gate_rows_ref[:, c] = (hidden_grad * up * (sigmoid_gate + silu_gate * (1.0 - sigmoid_gate))).astype(jnp.bfloat16)
        up_rows_ref[:, c] = (hidden_grad * silu_gate).astype(jnp.bfloat16)

    over(gate_ref.shape[1], 768, step)


def ffn_rows(rows, branch, *weights):
    wide = ((branch.shape[0], weights[0].shape[1]), jnp.bfloat16)
    low = [(branch.shape, jnp.bfloat16)] * 2 if branch.dtype == jnp.float32 else []
    return call(ffn_kernel, "ffn_rows", [wide] * 3 + low, *rows, branch, *weights)


def back_kernel(first, gate_rows_ref, up_rows_ref, gate_ref, up_ref, *part_refs):
    rows = pl.ds(first, len(part_refs) * part_refs[0].shape[0])

    def step(start, size):
        c = pl.ds(start, size)
        total = contract(gate_rows_ref[rows, :], gate_ref[c, :], 1, 1) + contract(
            up_rows_ref[rows, :], up_ref[c, :], 1, 1
        )
        put(part_refs, total, c)

    over(gate_ref.shape[0], 256, step)


def ffn_back(gate_rows, up_rows, gate_weight, up_weight, first, counts):
    shapes = [((count, gate_weight.shape[0]), jnp.float32) for count in counts]
    kernel = functools.partial(back_kernel, first)
    return call(kernel, "ffn_back", shapes, gate_rows, up_rows, gate_weight, up_weight)


def down_kernel(hidden_ref, down_ref, low_ref, high_ref):
    def step(start, size):
        c = pl.ds(start, size)
        put((low_ref, high_ref), contract(hidden_ref[...], down_ref[:, c], 1, 0), c)

    over(down_ref.shape[1], 256, step)


def ffn_down(hidden, down_weight):
    shape = ((hidden.shape[0] // 2, down_weight.shape[1]), jnp.float32)
    return call(down_kernel, "ffn_down", [shape] * 2, hidden, down_weight)


def sums_kernel(pieces, cuts, chosen_ref, *refs):
    rows_refs, feature_refs, refs = refs[:pieces], refs[pieces : 2 * pieces], refs[2 * pieces :]
    picked = [contract(chosen_ref[...], r[...], 1, 1).astype(jnp.bfloat16) for r in rows_refs]

    def step(start, size):
        c = pl.ds(start, size)
        total = sum(contract(p, f[:, c], 1, 0) for p, f in zip(picked, feature_refs))
        if len(refs) == cuts:
            put(refs, total, c)
        else:
            total = total + jnp.concatenate([r[:, c] for r in refs[:cuts]])
            put(refs[cuts:], total, c)

    over(feature_refs[0].shape[1], 640, step)


def put(refs, total, c):
    size = total.shape[0] // len(refs)
    for i, ref in enumerate(refs):
        ref[:, c] = total[i * size : (i + 1) * size]


def outer_sums(chosen, rows, features):
    shape = ((chosen.shape[0] // CUTS, features[0].shape[1]), jnp.float32)
    kernel = functools.partial(sums_kernel, len(rows), CUTS)
    return call(kernel, "outer_sums", [shape] * CUTS, chosen, *rows, *features)


def outer_fold(chosen, rows, features, arrived):
    shape = ((chosen.shape[0] // 2, features[0].shape[1]), jnp.float32)
    kernel = functools.partial(sums_kernel, len(rows), CUTS)
    return call(kernel, "outer_fold", [shape] * 2, chosen, *rows, *features, *arrived)


def swap_cuts(cuts, bit):
    return [swap_dp(cut, bit) for cut in cuts]


def attn_sums_kernel(block, chosen_ref, gains_ref, normed_ref, residual_ref, qkv_ref, mixed_ref, *refs):
    count = chosen_ref.shape[0]
    chosen = chosen_ref[...]
    qkv_width = qkv_ref.shape[1]
    o_start = qkv_width + gains_ref.shape[1]
    ones_row = lax.broadcasted_iota(jnp.int32, (count, normed_ref.shape[0]), 0) % (block + EXTRA) == block
    picked = contract(chosen, normed_ref[...], 1, 1)
    picked = jnp.where(ones_row, 1.0, picked).astype(jnp.bfloat16)
    gains = jnp.dot(
        chosen.astype(jnp.float32), gains_ref[...], preferred_element_type=jnp.float32, precision=lax.Precision.HIGHEST
    )
    picked_residual = contract(chosen, residual_ref[...], 1, 1).astype(jnp.bfloat16)
    total = jnp.concatenate(
        [
            contract(picked, qkv_ref[...], 1, 0),
            gains,
            contract(picked_residual, mixed_ref[...], 1, 0),
            jnp.zeros((count, -mixed_ref.shape[1] % 128), jnp.float32),
        ],
        axis=1,
    )
    if len(refs) == ATTN_CUTS:
        put(refs, total, slice(None))
    else:
        total = total + jnp.concatenate([r[...] for r in refs[:ATTN_CUTS]])
        put(refs[ATTN_CUTS:], total, slice(None))


def attn_sums(block, chosen, gains, normed, residual_low, qkv_rows, mixed, arrived=None):
    count = chosen.shape[0]
    features = qkv_rows.shape[1] + gains.shape[1] + -(-mixed.shape[1] // 128) * 128
    kernel = functools.partial(attn_sums_kernel, block)
    operands = (chosen, gains, normed, residual_low, qkv_rows, mixed)
    if arrived is None:
        return call(kernel, "attn_sums", [((count // ATTN_CUTS, features), jnp.float32)] * ATTN_CUTS, *operands)
    return call(kernel, "attn_fold", [((count // 2, features), jnp.float32)] * 2, *operands, *arrived)


def on_device(
    tokens,
    out_grad,
    doc_lengths,
    q_weight,
    k_weight,
    v_weight,
    q_bias,
    k_bias,
    v_bias,
    o_weight,
    attn_gain,
    ffn_gain,
    gate_weight,
    up_weight,
    down_weight,
):
    row_total, width = tokens.shape
    local_heads = q_weight.shape[1] // HD
    local_kv = k_weight.shape[1] // HD
    dp_size = lax.axis_size("dp")
    dp_bits = dp_size.bit_length() - 1
    pair_bit = 2
    ffn_order = (0, 1) + tuple(range(3, dp_bits))
    attn_order = (0, 1, pair_bit) + tuple(range(3, dp_bits))
    own = lax.axis_index("dp")
    positions, alive = layout(doc_lengths[0], row_total)
    cosine, sine_table = rotary(positions, HD)
    alive_rows = alive.astype(jnp.float32)[:, None]
    places = jnp.arange(row_total, dtype=jnp.int32)
    o_half = o_weight.shape[0] // 2
    o_first = own & 1
    upstream = out_grad.astype(jnp.float32)
    branch_wide = upstream * alive_rows
    o_mine = lax.dynamic_slice_in_dim(o_weight, o_first * o_half, o_half).astype(jnp.float32)
    o_same = swap_tensor(o_mine)
    half_rows = row_total // 2
    pair_branch = swap_dp(branch_wide, pair_bit)
    ffn_keep, ffn_send = dest_columns(width, ffn_order, (pair_bit,))
    attn_keep, attn_send = dest_columns(width, attn_order, extra=EXTRA)
    branch_grad = branch_wide.astype(jnp.bfloat16)
    inputs = tokens.astype(jnp.float32)
    gain_one = attn_gain.astype(jnp.float32)
    gain_two = ffn_gain.astype(jnp.float32)
    qkv_across = jnp.concatenate([q_weight.T, k_weight.T, v_weight.T])
    qkv_bias = jnp.concatenate([q_bias.reshape(-1), k_bias.reshape(-1), v_bias.reshape(-1)]).astype(jnp.float32)
    q_width = local_heads * HD
    k_width = local_kv * HD
    qkv_width = q_width + 2 * k_width
    begins = (places - positions)[None, :]
    padded = -(-qkv_width // 128) * 128
    row_stats = ((-(-local_heads // 8) * 8, row_total), jnp.float32)
    normed, turned, mixed_heads, mixed_wide, top_score, mass = call(
        functools.partial(attend_kernel, local_heads),
        "attend",
        [
            ((row_total, width), jnp.bfloat16),
            ((qkv_width, row_total), jnp.bfloat16),
            ((row_total, q_width), jnp.bfloat16),
            ((q_width, row_total), jnp.float32),
            row_stats,
            row_stats,
        ],
        tokens,
        gain_one[None, :],
        qkv_across,
        qkv_bias[:, None],
        cosine,
        sine_table,
        begins,
        scratch=[((qkv_width, row_total), jnp.float32), ((-(-q_width // 128) * 128, row_total), jnp.float32)],
    )
    mixed_other = swap_tensor(after(mixed_wide, o_same))
    o_same = after(o_same, mixed_heads)
    o_cross = swap_dp(o_same, 0)
    residual, normed_two, low_wide, high_wide = call(
        project_kernel,
        "project",
        [
            ((row_total, width), jnp.float32),
            ((row_total, width), jnp.bfloat16),
            ((half_rows, width), jnp.float32),
            ((half_rows, width), jnp.float32),
        ],
        jnp.broadcast_to(o_first.astype(jnp.float32), (1, width)),
        tokens,
        mixed_heads,
        after(mixed_other, o_cross, ffn_keep, ffn_send, attn_keep, attn_send, branch_grad),
        o_weight,
        o_same,
        o_cross,
        gain_two[None, :],
        scratch=[((q_width, width), jnp.bfloat16)],
    )
    side = jnp.broadcast_to(lax.axis_index("tensor").astype(jnp.float32), (1, width))
    quarter = half_rows // 2
    mine = jnp.where(side == 0.0, low_wide[:quarter], low_wide[quarter:])
    low_mine = swap_dp(mine, pair_bit)
    high_two = swap_dp(high_wide, pair_bit)
    ffn_weights = (gate_weight, up_weight, down_weight)

    hidden_act, gate_grad_rows, up_grad_rows = ffn_rows([normed_two], branch_grad, *ffn_weights)
    backward = (up_grad_rows, gate_weight, up_weight)
    (low_part,) = ffn_back(after(gate_grad_rows, pair_branch, low_mine), *backward, 0, [half_rows])
    low_swapped = swap_tensor(after(low_mine, gate_grad_rows))
    (high_part,) = ffn_back(after(gate_grad_rows, low_part), *backward, half_rows, [half_rows])
    low_from_x = swap_tensor(after(low_part, low_swapped, high_part))
    low_branch, high_branch = pair_branch[:half_rows], pair_branch[half_rows:]
    low_hidden, low_gate, low_up, low_two, low_branch = ffn_rows(
        [side, low_mine, after(low_swapped, high_part)], low_branch, *ffn_weights
    )
    high_from_x = swap_tensor(after(high_part, low_from_x))
    high_hidden, high_gate, high_up, high_two, high_branch = ffn_rows(
        [after(high_two, low_hidden)], high_branch, *ffn_weights
    )
    branch_rows = (branch_grad, low_branch, high_branch)
    two_rows = (normed_two, low_two, high_two)
    down_sums = outer_sums(ffn_send, branch_rows, (hidden_act, low_hidden, high_hidden))
    down_sent = swap_cuts(down_sums, 0)
    low_down, high_down = ffn_down(after(hidden_act, *down_sums), down_weight)
    gate_sums = outer_sums(after(ffn_send, low_from_x, low_down), two_rows, (gate_grad_rows, low_gate, high_gate))
    gate_sent = swap_cuts(gate_sums, 0)
    up_sums = outer_sums(after(ffn_send, *gate_sums), two_rows, (up_grad_rows, low_up, high_up))
    up_sent = swap_cuts(up_sums, 0)
    down_keep, down_send = outer_fold(
        after(ffn_keep, *up_sums), branch_rows, (hidden_act, low_hidden, high_hidden), down_sent
    )
    gate_keep, gate_send = outer_fold(
        after(ffn_keep, down_send), two_rows, (gate_grad_rows, low_gate, high_gate), gate_sent
    )
    up_keep, up_send = outer_fold(after(ffn_keep, gate_send), two_rows, (up_grad_rows, low_up, high_up), up_sent)
    down_from_y, gate_from_y, up_from_y = (swap_dp(v, ffn_order[1]) for v in (down_send, gate_send, up_send))
    wide, low = ((row_total, width), jnp.float32), ((row_total, width), jnp.bfloat16)
    gain_row = ((1, width), jnp.float32)
    residual_grad, residual_low, ffn_gain_sum = call(
        norm_back_kernel,
        "norm_back",
        [wide, low, gain_row],
        low_part,
        high_part,
        low_from_x,
        after(high_from_x, up_send),
        residual,
        gain_two[None, :],
        branch_grad,
    )
    down_keep, down_send = step_on(down_keep, after(down_from_y, residual_low))
    residual_low = after(residual_low, down_send)
    down_from_z = swap_dp(down_send, ffn_order[2])
    half_wide = ((half_rows, width), jnp.float32)
    qkv_grad_rows, low_normed, high_normed, attn_gain_part = call(
        functools.partial(attend_back_kernel, local_heads),
        "attend_back",
        [((row_total, qkv_width), jnp.bfloat16), half_wide, half_wide, gain_row],
        residual_low,
        o_weight,
        qkv_across,
        turned,
        top_score,
        mass,
        cosine,
        sine_table,
        begins,
        tokens,
        scratch=[
            ((q_width, row_total), jnp.bfloat16),
            ((padded, row_total), jnp.float32),
            ((row_total, HD), jnp.float32),
            ((row_total, HD), jnp.float32),
        ],
    )
    gain_sums = jnp.concatenate([attn_gain_part + swap_tensor(attn_gain_part), ffn_gain_sum])
    low_other = swap_tensor(after(low_normed, gain_sums))
    high_other = swap_tensor(after(high_normed, gain_sums))
    gain_columns = jnp.pad(gain_sums, ((0, -qkv_width % 128 - 2), (0, 0))).T
    attn_operands = (gain_columns, normed, residual_low, qkv_grad_rows, mixed_heads)
    gain_block = width // dp_size
    attn_sent = swap_cuts(
        attn_sums(gain_block, after(attn_send, down_from_z), *attn_operands), attn_order[0]
    )
    gate_keep, gate_send = step_on(gate_keep, gate_from_y)
    gate_from_z = swap_dp(gate_send, ffn_order[2])
    attn_part, attn_next = attn_sums(
        gain_block, after(attn_keep, gate_send, low_other), *attn_operands, attn_sent
    )
    attn_from_z = swap_dp(attn_next, attn_order[1])
    low_down_x = swap_tensor(after(low_down, attn_next))
    high_down_x = swap_tensor(after(high_down, attn_next))
    up_keep, up_send = step_on(up_keep, after(up_from_y, attn_next, low_other))
    up_from_z = swap_dp(up_send, ffn_order[2])
    attn_part, attn_next = step_on(attn_part, after(attn_from_z, up_send))
    attn_from_y = swap_dp(attn_next, attn_order[2])
    attn_part, attn_next = step_on(attn_part, after(attn_from_y, gate_from_z))
    attn_from_z = swap_dp(after(attn_next, up_from_z), attn_order[3])
    attn_grad = close(attn_part, attn_from_z, attn_order[4:])
    (tokens_grad,) = call(
        tokens_back_kernel,
        "tokens_back",
        [low],
        tokens,
        low_normed,
        high_normed,
        low_other,
        after(high_other, up_send),
        gain_one[None, :],
        residual_grad,
        out_grad,
        alive_rows,
    )
    high_down_x = after(high_down_x, attn_next)
    block_out = residual + jnp.concatenate([low_down + low_down_x, high_down + high_down_x])
    o_start = -(-qkv_width // 128) * 128
    qkv_grad, o_grad = attn_grad[:gain_block, :qkv_width], attn_grad[:gain_block, o_start : o_start + q_width]
    attn_gain_grad, ffn_gain_grad = attn_grad[:gain_block, qkv_width], attn_grad[:gain_block, qkv_width + 1]
    bias_heads = attn_grad[gain_block, :qkv_width].reshape(local_heads + 2 * local_kv, HD)
    bias_block = HD // dp_size
    bias_own = lax.dynamic_slice_in_dim(bias_heads, own * bias_block, bias_block, axis=1)
    down_grad, gate_grad, up_grad = (
        close(keep, got, ffn_order[3:])
        for keep, got in ((down_keep, down_from_z), (gate_keep, gate_from_z), (up_keep, up_from_z))
    )
    layer_out = jnp.where(alive[:, None], block_out, inputs).astype(jnp.bfloat16)
    return (
        layer_out,
        tokens_grad,
        qkv_grad[:, :q_width],
        qkv_grad[:, q_width : q_width + k_width],
        qkv_grad[:, q_width + k_width :],
        bias_own[:local_heads],
        bias_heads[local_heads : local_heads + local_kv],
        bias_own[local_heads + local_kv :],
        o_grad.T,
        attn_gain_grad,
        ffn_gain_grad,
        gate_grad,
        up_grad,
        down_grad.T,
    )


def solution(mesh):
    return jax.shard_map(
        on_device,
        mesh=mesh,
        in_specs=(
            P("dp", None),
            P("dp", None),
            P("dp", None),
            P(None, "tensor"),
            P(None, "tensor"),
            P(None, "tensor"),
            P("tensor", None),
            P("tensor", None),
            P("tensor", None),
            P("tensor", None),
            P(),
            P(),
            P(None, "tensor"),
            P(None, "tensor"),
            P("tensor", None),
        ),
        out_specs=(
            P("dp", None),
            P("dp", None),
            P("dp", "tensor"),
            P("dp", "tensor"),
            P("dp", "tensor"),
            P("tensor", "dp"),
            P("tensor", None),
            P("tensor", "dp"),
            P("tensor", "dp"),
            P("dp"),
            P("dp"),
            P("dp", "tensor"),
            P("dp", "tensor"),
            P("tensor", "dp"),
        ),
        check_vma=False,
    )
```

```python
import functools
import math

import jax
import jax.numpy as jnp
from jax import lax
from jax.experimental import pallas as pl
from jax.experimental.pallas import tpu as pltpu
from jax.sharding import PartitionSpec as P

HD = 64


norm_eps = 1e-06
rope_base = 1000000.0


def layout(lengths, row_total):
    doc_ends = jnp.cumsum(lengths)
    places = jnp.arange(row_total, dtype=jnp.int32)
    passed = (places[:, None] >= doc_ends[None, :]).astype(jnp.int32)
    begins = jnp.sum(passed * lengths[None, :], axis=1)
    alive = places < doc_ends[-1]
    return (places - begins, alive)


def rotary(positions, width):
    half_width = width // 2
    inv_freq = jnp.exp(
        jnp.arange(half_width, dtype=jnp.float32) * (-2.0 * math.log(rope_base) / width)
    )
    angles = inv_freq[:, None] * positions.astype(jnp.float32)[None, :]
    return (jnp.cos(angles), jnp.sin(angles))


def norm_back(inputs, factor, gain, upstream):
    scaled = upstream * gain
    return factor * scaled - inputs * factor**3 * jnp.mean(scaled * inputs, axis=-1, keepdims=True)


def swap_tensor(rows):
    size = lax.axis_size("tensor")
    return lax.ppermute(rows, "tensor", [(i, i ^ 1) for i in range(size)])


def swap_dp(rows, bit):
    size = lax.axis_size("dp")
    return lax.ppermute(rows, "dp", [(i, i ^ (1 << bit)) for i in range(size)])


def after(value, *others):
    return lax.optimization_barrier((value, *others))[0]


def dest_columns(width, order, fixed=(), extra=0):
    steps = len(order)
    block = width >> (steps + len(fixed))
    whole = block + extra
    count = whole << steps
    own = lax.axis_index("dp")
    places = jnp.arange(count, dtype=jnp.int32)
    spot = places // whole
    flip = jnp.zeros_like(spot)
    for j, bit in enumerate(order):
        flip = flip + (((spot >> (steps - 1 - j)) & 1) << bit)
    within = places % whole
    source = jnp.where(within < block, (own ^ flip) * block + within, -1)
    chosen = (source[:, None] == jnp.arange(width, dtype=jnp.int32)[None, :]).astype(jnp.bfloat16)
    return chosen[: count // 2], chosen[count // 2 :]


def finish(keep, send, order):
    for bit in order[:-1]:
        sent = swap_dp(send, bit)
        half = sent.shape[0] // 2
        send = keep[half:] + sent[half:]
        keep = keep[:half] + sent[:half]
    return keep + swap_dp(send, order[-1])


def close(keep, sent, order):
    return finish(*step_on(keep, sent), order) if order else keep + sent


def step_on(keep, sent):
    half = sent.shape[0] // 2
    return keep[:half] + sent[:half], keep[half:] + sent[half:]


IN_VMEM = pl.BlockSpec(memory_space=pltpu.VMEM)
LIMIT = 11
EXTRA = 8
ROWS = 64
CUTS = 4
ATTN_CUTS = 4


def contract(left, right, left_dim, right_dim):
    return lax.dot_general(
        left, right, (((left_dim,), (right_dim,)), ((), ())), preferred_element_type=jnp.float32
    )


def over(total, size, step):
    count, rest = divmod(total, size)

    def turn(i, carry):
        step(pl.multiple_of(i * size, size), size)
        return carry

    lax.fori_loop(0, count, turn, 0)
    if rest:
        step(count * size, rest)


def call(kernel, name, shapes, *operands, scratch=()):
    return pl.pallas_call(
        kernel,
        in_specs=[IN_VMEM] * len(operands),
        out_specs=[IN_VMEM] * len(shapes),
        out_shape=[jax.ShapeDtypeStruct(shape, dtype) for shape, dtype in shapes],
        compiler_params=pltpu.CompilerParams(vmem_limit_bytes=LIMIT * 2**20),
        cost_estimate=pl.CostEstimate(flops=1000, bytes_accessed=1000, transcendentals=0),
        scratch_shapes=[pltpu.VMEM(shape, dtype) for shape, dtype in scratch],
        name=name,
    )(*operands)


def turn(pairs, cosine, sine_table):
    half = pairs.shape[0] // 2
    front, back = pairs[:half], pairs[half:]
    return jnp.concatenate([front * cosine - back * sine_table, back * cosine + front * sine_table], axis=0)


def blocks_of(begins_ref, row_total):
    size = row_total // 2
    for first in range(0, row_total, size):
        keys = first + size
        key_place = lax.broadcasted_iota(jnp.int32, (keys, size), 0)
        query_place = lax.broadcasted_iota(jnp.int32, (keys, size), 1) + first
        allowed = (key_place >= begins_ref[:, first:keys]) & (key_place <= query_place)
        yield slice(first, keys), keys, allowed


def attend_kernel(
    heads,
    tokens_ref,
    gain_ref,
    weight_ref,
    bias_ref,
    cosine_ref,
    sine_ref,
    begins_ref,
    normed_ref,
    turned_ref,
    mixed_ref,
    mixed_wide_ref,
    top_ref,
    mass_ref,
    pre_ref,
    mixed_across_ref,
):

    def norm(start):
        rows = pl.ds(start, ROWS)
        inputs = tokens_ref[rows, :].astype(jnp.float32)
        factor = lax.rsqrt(jnp.mean(inputs * inputs, axis=-1, keepdims=True) + norm_eps)
        normed_ref[rows, :] = (inputs * factor * gain_ref[...]).astype(jnp.bfloat16)

    row_blocks(tokens_ref.shape[0], norm)
    pre_ref[...] = contract(weight_ref[...], normed_ref[...], 1, 1) + bias_ref[...]
    cosine, sine_table = cosine_ref[...], sine_ref[...]

    def rope(h, carry):
        r = pl.ds(pl.multiple_of(h * HD, HD), HD)
        turned_ref[r, :] = turn(pre_ref[r, :], cosine, sine_table).astype(jnp.bfloat16)
        return carry

    lax.fori_loop(0, heads + 1, rope, 0)
    value_rows = pre_ref[(heads + 1) * HD :, :].astype(jnp.bfloat16)
    turned_ref[(heads + 1) * HD :, :] = value_rows
    key_rows = turned_ref[heads * HD : (heads + 1) * HD, :].astype(jnp.float32).T.astype(jnp.bfloat16)
    blocks = list(blocks_of(begins_ref, tokens_ref.shape[0]))

    def head(h, carry):
        r = pl.ds(pl.multiple_of(h * HD, HD), HD)
        for cols, keys, allowed in blocks:
            scores = contract(key_rows[:keys], turned_ref[r, cols], 1, 0) * HD ** (-0.5)
            scores = jnp.where(allowed, scores, -1e30)
            top = jnp.max(scores, axis=0, keepdims=True)
            exp_scores = jnp.exp(scores - top)
            mass = 1.0 / jnp.sum(exp_scores, axis=0, keepdims=True)
            low_probs = (exp_scores * mass).astype(jnp.bfloat16)
            mixed_across_ref[r, cols] = contract(value_rows[:, :keys], low_probs, 1, 0)
            top_ref[pl.ds(h, 1), cols] = top
            mass_ref[pl.ds(h, 1), cols] = mass
        return carry

    lax.fori_loop(0, heads, head, 0)
    mixed_wide_ref[...] = mixed_across_ref[: heads * HD, :].astype(jnp.bfloat16).astype(jnp.float32)
    mixed_ref[...] = mixed_across_ref[...].T[:, : heads * HD].astype(jnp.bfloat16)


def project_kernel(
    first_ref,
    tokens_ref,
    mixed_ref,
    other_ref,
    o_ref,
    same_ref,
    cross_ref,
    gain_ref,
    residual_ref,
    two_ref,
    low_ref,
    high_ref,
    o_other_ref,
):
    first = first_ref[...] == 0.0
    o_half = same_ref.shape[0]
    same, cross = same_ref[...], cross_ref[...]
    o_other_ref[:o_half, :] = jnp.where(first, same, cross).astype(jnp.bfloat16)
    o_other_ref[o_half:, :] = jnp.where(first, cross, same).astype(jnp.bfloat16)
    half = low_ref.shape[0]
    for rows, wide_ref in ((slice(0, half), low_ref), (slice(half, 2 * half), high_ref)):
        other = other_ref[:, rows].T.astype(jnp.bfloat16)
        residual = tokens_ref[rows, :].astype(jnp.float32) + (
            contract(mixed_ref[rows, :], o_ref[...], 1, 0) + contract(other, o_other_ref[...], 1, 0)
        )
        residual_ref[rows, :] = residual
        factor = lax.rsqrt(jnp.mean(residual * residual, axis=-1, keepdims=True) + norm_eps)
        two = (residual * factor * gain_ref[...]).astype(jnp.bfloat16)
        two_ref[rows, :] = two
        wide_ref[...] = two.astype(jnp.float32)


def row_blocks(count, step):
    def turn_on(i, carry):
        step(pl.multiple_of(i * ROWS, ROWS))
        return carry

    lax.fori_loop(0, count // ROWS, turn_on, 0)


def norm_back_kernel(*refs):
    part_refs, x_refs = refs[:2], refs[2:4]
    residual_ref, gain_ref, branch_ref, grad_ref, grad_low_ref, gain_grad_ref = refs[4:]
    gain_grad_ref[...] = jnp.zeros(gain_grad_ref.shape, jnp.float32)
    first = 0
    for part_ref, x_ref in zip(part_refs, x_refs):

        def step(start, part_ref=part_ref, x_ref=x_ref, first=first):
            here, rows = pl.ds(start, ROWS), pl.ds(first + start, ROWS)
            residual = residual_ref[rows, :]
            upstream = part_ref[here, :] + x_ref[here, :]
            factor = lax.rsqrt(jnp.mean(residual * residual, axis=-1, keepdims=True) + norm_eps)
            gain_grad_ref[...] += jnp.sum(upstream * (residual * factor), axis=0, keepdims=True)
            grad = norm_back(residual, factor, gain_ref[...], upstream) + branch_ref[rows, :].astype(jnp.float32)
            grad_ref[rows, :] = grad
            grad_low_ref[rows, :] = grad.astype(jnp.bfloat16)

        row_blocks(part_ref.shape[0], step)
        first += part_ref.shape[0]


def tokens_back_kernel(
    tokens_ref, low_ref, high_ref, low_x_ref, high_x_ref, gain_ref, residual_ref, out_grad_ref, alive_ref, grad_ref
):
    half = low_ref.shape[0]
    for first, part_ref, x_ref in ((0, low_ref, low_x_ref), (half, high_ref, high_x_ref)):

        def step(start, part_ref=part_ref, x_ref=x_ref, first=first):
            here, rows = pl.ds(start, ROWS), pl.ds(first + start, ROWS)
            inputs = tokens_ref[rows, :].astype(jnp.float32)
            factor = lax.rsqrt(jnp.mean(inputs * inputs, axis=-1, keepdims=True) + norm_eps)
            grad = norm_back(inputs, factor, gain_ref[...], part_ref[here, :] + x_ref[here, :])
            upstream = out_grad_ref[rows, :].astype(jnp.float32)
            total = upstream * (1.0 - alive_ref[rows, :]) + residual_ref[rows, :] + grad
            grad_ref[rows, :] = total.astype(jnp.bfloat16)

        row_blocks(half, step)


def attend_back_kernel(
    heads,
    residual_ref,
    o_ref,
    weight_ref,
    turned_ref,
    top_ref,
    mass_ref,
    cosine_ref,
    sine_ref,
    begins_ref,
    tokens_ref,
    rows_ref,
    low_ref,
    high_ref,
    gain_grad_ref,
    mixed_ref,
    across_ref,
    key_ref,
    value_ref,
):
    mixed_ref[...] = contract(o_ref[...], residual_ref[...], 1, 1).astype(jnp.bfloat16)
    cosine, sine_table = cosine_ref[...], -sine_ref[...]
    k, v = heads * HD, (heads + 1) * HD
    keys_across = turned_ref[k:v, :]
    key_rows = keys_across.astype(jnp.float32).T.astype(jnp.bfloat16)
    value_rows = turned_ref[v:, :].astype(jnp.float32).T.astype(jnp.bfloat16)
    blocks = list(blocks_of(begins_ref, residual_ref.shape[0]))
    key_ref[...] = jnp.zeros(key_ref.shape, jnp.float32)
    value_ref[...] = jnp.zeros(value_ref.shape, jnp.float32)

    def head(h, carry):
        r = pl.ds(pl.multiple_of(h * HD, HD), HD)
        for cols, keys, allowed in blocks:
            query, grad = turned_ref[r, cols], mixed_ref[r, cols]
            scores = contract(key_rows[:keys], query, 1, 0) * HD ** (-0.5)
            scores = jnp.where(allowed, scores, -1e30)
            probs = jnp.exp(scores - top_ref[pl.ds(h, 1), cols]) * mass_ref[pl.ds(h, 1), cols]
            prob_grad = contract(value_rows[:keys], grad, 1, 0)
            inner_sum = jnp.sum(probs * prob_grad, axis=0, keepdims=True)
            score_grad = (probs * (prob_grad - inner_sum)).astype(jnp.bfloat16)
            query_grad = contract(keys_across[:, :keys], score_grad, 1, 0) * HD ** (-0.5)
            across_ref[r, cols] = turn(query_grad, cosine[:, cols], sine_table[:, cols])
            key_ref[:keys, :] += contract(score_grad, query, 1, 1)
            value_ref[:keys, :] += contract(probs.astype(jnp.bfloat16), grad, 1, 1)
        return carry

    lax.fori_loop(0, heads, head, 0)
    across_ref[k:v, :] = turn(key_ref[...].T * HD ** (-0.5), cosine, sine_table)
    across_ref[v : v + HD, :] = value_ref[...].T
    rows_ref[...] = across_ref[...].T[:, : v + HD].astype(jnp.bfloat16)

    def step(start, size):
        c = pl.ds(start, size)
        part = contract(rows_ref[...], weight_ref[:, c], 1, 0)
        put((low_ref, high_ref), part, c)
        gain_grad_ref[:, c] = jnp.sum(part * (tokens_ref[:, c].astype(jnp.float32) * factor), axis=0, keepdims=True)

    inputs = tokens_ref[...].astype(jnp.float32)
    factor = lax.rsqrt(jnp.mean(inputs * inputs, axis=-1, keepdims=True) + norm_eps)
    over(low_ref.shape[1], 256, step)


def ffn_kernel(*refs):
    if len(refs) == 12:
        side_ref, mine_ref, other_ref, branch_ref, *refs, two_ref, branch_low_ref = refs
        gate_ref, up_ref, down_ref, hidden_ref, gate_rows_ref, up_rows_ref = refs
        half = mine_ref.shape[0]
        first = side_ref[...] == 0.0
        mine, other = mine_ref[...], other_ref[...]
        two_ref[:half, :] = jnp.where(first, mine, other).astype(jnp.bfloat16)
        two_ref[half:, :] = jnp.where(first, other, mine).astype(jnp.bfloat16)
        branch_low_ref[...] = branch_ref[...].astype(jnp.bfloat16)
        low_refs, branch_ref = (), branch_low_ref
    else:
        two_ref, branch_ref, gate_ref, up_ref, down_ref, hidden_ref, gate_rows_ref, up_rows_ref, *low_refs = refs
    if low_refs:
        for wide_ref, low_ref in zip((two_ref, branch_ref), low_refs):
            low_ref[...] = wide_ref[...].astype(jnp.bfloat16)
        two_ref, branch_ref = low_refs

    def step(start, size):
        c = pl.ds(start, size)
        gate = contract(two_ref[...], gate_ref[:, c], 1, 0)
        up = contract(two_ref[...], up_ref[:, c], 1, 0)
        hidden_grad = contract(branch_ref[...], down_ref[c, :], 1, 1)
        sigmoid_gate = 0.5 * jnp.tanh(0.5 * gate) + 0.5
        silu_gate = gate * sigmoid_gate
        hidden_ref[:, c] = (silu_gate * up).astype(jnp.bfloat16)
        gate_rows_ref[:, c] = (hidden_grad * up * (sigmoid_gate + silu_gate * (1.0 - sigmoid_gate))).astype(jnp.bfloat16)
        up_rows_ref[:, c] = (hidden_grad * silu_gate).astype(jnp.bfloat16)

    over(gate_ref.shape[1], 768, step)


def ffn_rows(rows, branch, *weights):
    wide = ((branch.shape[0], weights[0].shape[1]), jnp.bfloat16)
    low = [(branch.shape, jnp.bfloat16)] * 2 if branch.dtype == jnp.float32 else []
    return call(ffn_kernel, "ffn_rows", [wide] * 3 + low, *rows, branch, *weights)


def back_kernel(first, gate_rows_ref, up_rows_ref, gate_ref, up_ref, *part_refs):
    rows = pl.ds(first, len(part_refs) * part_refs[0].shape[0])

    def step(start, size):
        c = pl.ds(start, size)
        total = contract(gate_rows_ref[rows, :], gate_ref[c, :], 1, 1) + contract(
            up_rows_ref[rows, :], up_ref[c, :], 1, 1
        )
        put(part_refs, total, c)

    over(gate_ref.shape[0], 256, step)


def ffn_back(gate_rows, up_rows, gate_weight, up_weight, first, counts):
    shapes = [((count, gate_weight.shape[0]), jnp.float32) for count in counts]
    kernel = functools.partial(back_kernel, first)
    return call(kernel, "ffn_back", shapes, gate_rows, up_rows, gate_weight, up_weight)


def down_kernel(hidden_ref, down_ref, low_ref, high_ref):
    def step(start, size):
        c = pl.ds(start, size)
        put((low_ref, high_ref), contract(hidden_ref[...], down_ref[:, c], 1, 0), c)

    over(down_ref.shape[1], 256, step)


def ffn_down(hidden, down_weight):
    shape = ((hidden.shape[0] // 2, down_weight.shape[1]), jnp.float32)
    return call(down_kernel, "ffn_down", [shape] * 2, hidden, down_weight)


def sums_kernel(pieces, cuts, chosen_ref, *refs):
    rows_refs, feature_refs, refs = refs[:pieces], refs[pieces : 2 * pieces], refs[2 * pieces :]
    picked = [contract(chosen_ref[...], r[...], 1, 1).astype(jnp.bfloat16) for r in rows_refs]

    def step(start, size):
        c = pl.ds(start, size)
        total = sum(contract(p, f[:, c], 1, 0) for p, f in zip(picked, feature_refs))
        if len(refs) == cuts:
            put(refs, total, c)
        else:
            total = total + jnp.concatenate([r[:, c] for r in refs[:cuts]])
            put(refs[cuts:], total, c)

    over(feature_refs[0].shape[1], 640, step)


def put(refs, total, c):
    size = total.shape[0] // len(refs)
    for i, ref in enumerate(refs):
        ref[:, c] = total[i * size : (i + 1) * size]


def outer_sums(chosen, rows, features):
    shape = ((chosen.shape[0] // CUTS, features[0].shape[1]), jnp.float32)
    kernel = functools.partial(sums_kernel, len(rows), CUTS)
    return call(kernel, "outer_sums", [shape] * CUTS, chosen, *rows, *features)


def outer_fold(chosen, rows, features, arrived):
    shape = ((chosen.shape[0] // 2, features[0].shape[1]), jnp.float32)
    kernel = functools.partial(sums_kernel, len(rows), CUTS)
    return call(kernel, "outer_fold", [shape] * 2, chosen, *rows, *features, *arrived)


def swap_cuts(cuts, bit):
    return [swap_dp(cut, bit) for cut in cuts]


def attn_sums_kernel(block, chosen_ref, gains_ref, normed_ref, residual_ref, qkv_ref, mixed_ref, *refs):
    count = chosen_ref.shape[0]
    chosen = chosen_ref[...]
    qkv_width = qkv_ref.shape[1]
    o_start = qkv_width + gains_ref.shape[1]
    ones_row = lax.broadcasted_iota(jnp.int32, (count, normed_ref.shape[0]), 0) % (block + EXTRA) == block
    picked = contract(chosen, normed_ref[...], 1, 1)
    picked = jnp.where(ones_row, 1.0, picked).astype(jnp.bfloat16)
    gains = jnp.dot(
        chosen.astype(jnp.float32), gains_ref[...], preferred_element_type=jnp.float32, precision=lax.Precision.HIGHEST
    )
    picked_residual = contract(chosen, residual_ref[...], 1, 1).astype(jnp.bfloat16)
    total = jnp.concatenate(
        [
            contract(picked, qkv_ref[...], 1, 0),
            gains,
            contract(picked_residual, mixed_ref[...], 1, 0),
            jnp.zeros((count, -mixed_ref.shape[1] % 128), jnp.float32),
        ],
        axis=1,
    )
    if len(refs) == ATTN_CUTS:
        put(refs, total, slice(None))
    else:
        total = total + jnp.concatenate([r[...] for r in refs[:ATTN_CUTS]])
        put(refs[ATTN_CUTS:], total, slice(None))


def attn_sums(block, chosen, gains, normed, residual_low, qkv_rows, mixed, arrived=None):
    count = chosen.shape[0]
    features = qkv_rows.shape[1] + gains.shape[1] + -(-mixed.shape[1] // 128) * 128
    kernel = functools.partial(attn_sums_kernel, block)
    operands = (chosen, gains, normed, residual_low, qkv_rows, mixed)
    if arrived is None:
        return call(kernel, "attn_sums", [((count // ATTN_CUTS, features), jnp.float32)] * ATTN_CUTS, *operands)
    return call(kernel, "attn_fold", [((count // 2, features), jnp.float32)] * 2, *operands, *arrived)


def on_device(
    tokens,
    out_grad,
    doc_lengths,
    q_weight,
    k_weight,
    v_weight,
    q_bias,
    k_bias,
    v_bias,
    o_weight,
    attn_gain,
    ffn_gain,
    gate_weight,
    up_weight,
    down_weight,
):
    row_total, width = tokens.shape
    local_heads = q_weight.shape[1] // HD
    local_kv = k_weight.shape[1] // HD
    dp_size = lax.axis_size("dp")
    dp_bits = dp_size.bit_length() - 1
    pair_bit = 2
    ffn_order = (0, 1) + tuple(range(3, dp_bits))
    attn_order = (0, 1, pair_bit) + tuple(range(3, dp_bits))
    own = lax.axis_index("dp")
    positions, alive = layout(doc_lengths[0], row_total)
    cosine, sine_table = rotary(positions, HD)
    alive_rows = alive.astype(jnp.float32)[:, None]
    places = jnp.arange(row_total, dtype=jnp.int32)
    o_half = o_weight.shape[0] // 2
    o_first = own & 1
    upstream = out_grad.astype(jnp.float32)
    branch_wide = upstream * alive_rows
    o_mine = lax.dynamic_slice_in_dim(o_weight, o_first * o_half, o_half).astype(jnp.float32)
    o_same = swap_tensor(o_mine)
    half_rows = row_total // 2
    pair_branch = swap_dp(branch_wide, pair_bit)
    ffn_keep, ffn_send = dest_columns(width, ffn_order, (pair_bit,))
    attn_keep, attn_send = dest_columns(width, attn_order, extra=EXTRA)
    branch_grad = branch_wide.astype(jnp.bfloat16)
    inputs = tokens.astype(jnp.float32)
    gain_one = attn_gain.astype(jnp.float32)
    gain_two = ffn_gain.astype(jnp.float32)
    qkv_across = jnp.concatenate([q_weight.T, k_weight.T, v_weight.T])
    qkv_bias = jnp.concatenate([q_bias.reshape(-1), k_bias.reshape(-1), v_bias.reshape(-1)]).astype(jnp.float32)
    q_width = local_heads * HD
    k_width = local_kv * HD
    qkv_width = q_width + 2 * k_width
    begins = (places - positions)[None, :]
    padded = -(-qkv_width // 128) * 128
    row_stats = ((-(-local_heads // 8) * 8, row_total), jnp.float32)
    normed, turned, mixed_heads, mixed_wide, top_score, mass = call(
        functools.partial(attend_kernel, local_heads),
        "attend",
        [
            ((row_total, width), jnp.bfloat16),
            ((qkv_width, row_total), jnp.bfloat16),
            ((row_total, q_width), jnp.bfloat16),
            ((q_width, row_total), jnp.float32),
            row_stats,
            row_stats,
        ],
        tokens,
        gain_one[None, :],
        qkv_across,
        qkv_bias[:, None],
        cosine,
        sine_table,
        begins,
        scratch=[((qkv_width, row_total), jnp.float32), ((-(-q_width // 128) * 128, row_total), jnp.float32)],
    )
    mixed_other = swap_tensor(after(mixed_wide, o_same))
    o_same = after(o_same, mixed_heads)
    o_cross = swap_dp(o_same, 0)
    residual, normed_two, low_wide, high_wide = call(
        project_kernel,
        "project",
        [
            ((row_total, width), jnp.float32),
            ((row_total, width), jnp.bfloat16),
            ((half_rows, width), jnp.float32),
            ((half_rows, width), jnp.float32),
        ],
        jnp.broadcast_to(o_first.astype(jnp.float32), (1, width)),
        tokens,
        mixed_heads,
        after(mixed_other, o_cross, ffn_keep, ffn_send, attn_keep, attn_send, branch_grad),
        o_weight,
        o_same,
        o_cross,
        gain_two[None, :],
        scratch=[((q_width, width), jnp.bfloat16)],
    )
    side = jnp.broadcast_to(lax.axis_index("tensor").astype(jnp.float32), (1, width))
    quarter = half_rows // 2
    mine = jnp.where(side == 0.0, low_wide[:quarter], low_wide[quarter:])
    low_mine = swap_dp(mine, pair_bit)
    high_two = swap_dp(high_wide, pair_bit)
    ffn_weights = (gate_weight, up_weight, down_weight)

    hidden_act, gate_grad_rows, up_grad_rows = ffn_rows([normed_two], branch_grad, *ffn_weights)
    backward = (up_grad_rows, gate_weight, up_weight)
    (low_part,) = ffn_back(after(gate_grad_rows, pair_branch, low_mine), *backward, 0, [half_rows])
    low_swapped = swap_tensor(after(low_mine, gate_grad_rows))
    (high_part,) = ffn_back(after(gate_grad_rows, low_part), *backward, half_rows, [half_rows])
    low_from_x = swap_tensor(after(low_part, low_swapped, high_part))
    low_branch, high_branch = pair_branch[:half_rows], pair_branch[half_rows:]
    low_hidden, low_gate, low_up, low_two, low_branch = ffn_rows(
        [side, low_mine, after(low_swapped, high_part)], low_branch, *ffn_weights
    )
    high_from_x = swap_tensor(after(high_part, low_from_x))
    high_hidden, high_gate, high_up, high_two, high_branch = ffn_rows(
        [after(high_two, low_hidden)], high_branch, *ffn_weights
    )
    branch_rows = (branch_grad, low_branch, high_branch)
    two_rows = (normed_two, low_two, high_two)
    down_sums = outer_sums(ffn_send, branch_rows, (hidden_act, low_hidden, high_hidden))
    down_sent = swap_cuts(down_sums, 0)
    low_down, high_down = ffn_down(after(hidden_act, *down_sums), down_weight)
    gate_sums = outer_sums(after(ffn_send, low_from_x, low_down), two_rows, (gate_grad_rows, low_gate, high_gate))
    gate_sent = swap_cuts(gate_sums, 0)
    up_sums = outer_sums(after(ffn_send, *gate_sums), two_rows, (up_grad_rows, low_up, high_up))
    up_sent = swap_cuts(up_sums, 0)
    down_keep, down_send = outer_fold(
        after(ffn_keep, *up_sums), branch_rows, (hidden_act, low_hidden, high_hidden), down_sent
    )
    gate_keep, gate_send = outer_fold(
        after(ffn_keep, down_send), two_rows, (gate_grad_rows, low_gate, high_gate), gate_sent
    )
    up_keep, up_send = outer_fold(after(ffn_keep, gate_send), two_rows, (up_grad_rows, low_up, high_up), up_sent)
    down_from_y, gate_from_y, up_from_y = (swap_dp(v, ffn_order[1]) for v in (down_send, gate_send, up_send))
    wide, low = ((row_total, width), jnp.float32), ((row_total, width), jnp.bfloat16)
    gain_row = ((1, width), jnp.float32)
    residual_grad, residual_low, ffn_gain_sum = call(
        norm_back_kernel,
        "norm_back",
        [wide, low, gain_row],
        low_part,
        high_part,
        low_from_x,
        after(high_from_x, up_send),
        residual,
        gain_two[None, :],
        branch_grad,
    )
    down_keep, down_send = step_on(down_keep, after(down_from_y, residual_low))
    residual_low = after(residual_low, down_send)
    down_from_z = swap_dp(down_send, ffn_order[2])
    half_wide = ((half_rows, width), jnp.float32)
    qkv_grad_rows, low_normed, high_normed, attn_gain_part = call(
        functools.partial(attend_back_kernel, local_heads),
        "attend_back",
        [((row_total, qkv_width), jnp.bfloat16), half_wide, half_wide, gain_row],
        residual_low,
        o_weight,
        qkv_across,
        turned,
        top_score,
        mass,
        cosine,
        sine_table,
        begins,
        tokens,
        scratch=[
            ((q_width, row_total), jnp.bfloat16),
            ((padded, row_total), jnp.float32),
            ((row_total, HD), jnp.float32),
            ((row_total, HD), jnp.float32),
        ],
    )
    gain_sums = jnp.concatenate([attn_gain_part + swap_tensor(attn_gain_part), ffn_gain_sum])
    low_other = swap_tensor(after(low_normed, gain_sums))
    high_other = swap_tensor(after(high_normed, gain_sums))
    gain_columns = jnp.pad(gain_sums, ((0, -qkv_width % 128 - 2), (0, 0))).T
    attn_operands = (gain_columns, normed, residual_low, qkv_grad_rows, mixed_heads)
    gain_block = width // dp_size
    attn_sent = swap_cuts(
        attn_sums(gain_block, after(attn_send, down_from_z), *attn_operands), attn_order[0]
    )
    gate_keep, gate_send = step_on(gate_keep, gate_from_y)
    gate_from_z = swap_dp(gate_send, ffn_order[2])
    attn_part, attn_next = attn_sums(
        gain_block, after(attn_keep, gate_send, low_other), *attn_operands, attn_sent
    )
    attn_from_z = swap_dp(attn_next, attn_order[1])
    low_down_x = swap_tensor(after(low_down, attn_next))
    high_down_x = swap_tensor(after(high_down, attn_next))
    up_keep, up_send = step_on(up_keep, after(up_from_y, attn_next, low_other))
    up_from_z = swap_dp(up_send, ffn_order[2])
    attn_part, attn_next = step_on(attn_part, after(attn_from_z, up_send))
    attn_from_y = swap_dp(attn_next, attn_order[2])
    attn_part, attn_next = step_on(attn_part, after(attn_from_y, gate_from_z))
    attn_from_z = swap_dp(after(attn_next, up_from_z), attn_order[3])
    attn_grad = close(attn_part, attn_from_z, attn_order[4:])
    (tokens_grad,) = call(
        tokens_back_kernel,
        "tokens_back",
        [low],
        tokens,
        low_normed,
        high_normed,
        low_other,
        after(high_other, up_send),
        gain_one[None, :],
        residual_grad,
        out_grad,
        alive_rows,
    )
    high_down_x = after(high_down_x, attn_next)
    block_out = residual + jnp.concatenate([low_down + low_down_x, high_down + high_down_x])
    o_start = -(-qkv_width // 128) * 128
    qkv_grad, o_grad = attn_grad[:gain_block, :qkv_width], attn_grad[:gain_block, o_start : o_start + q_width]
    attn_gain_grad, ffn_gain_grad = attn_grad[:gain_block, qkv_width], attn_grad[:gain_block, qkv_width + 1]
    bias_heads = attn_grad[gain_block, :qkv_width].reshape(local_heads + 2 * local_kv, HD)
    bias_block = HD // dp_size
    bias_own = lax.dynamic_slice_in_dim(bias_heads, own * bias_block, bias_block, axis=1)
    down_grad, gate_grad, up_grad = (
        close(keep, got, ffn_order[3:])
        for keep, got in ((down_keep, down_from_z), (gate_keep, gate_from_z), (up_keep, up_from_z))
    )
    layer_out = jnp.where(alive[:, None], block_out, inputs).astype(jnp.bfloat16)
    return (
        layer_out,
        tokens_grad,
        qkv_grad[:, :q_width],
        qkv_grad[:, q_width : q_width + k_width],
        qkv_grad[:, q_width + k_width :],
        bias_own[:local_heads],
        bias_heads[local_heads : local_heads + local_kv],
        bias_own[local_heads + local_kv :],
        o_grad.T,
        attn_gain_grad,
        ffn_gain_grad,
        gate_grad,
        up_grad,
        down_grad.T,
    )


def solution(mesh):
    return jax.shard_map(
        on_device,
        mesh=mesh,
        in_specs=(
            P("dp", None),
            P("dp", None),
            P("dp", None),
            P(None, "tensor"),
            P(None, "tensor"),
            P(None, "tensor"),
            P("tensor", None),
            P("tensor", None),
            P("tensor", None),
            P("tensor", None),
            P(),
            P(),
            P(None, "tensor"),
            P(None, "tensor"),
            P("tensor", None),
        ),
        out_specs=(
            P("dp", None),
            P("dp", None),
            P("dp", "tensor"),
            P("dp", "tensor"),
            P("dp", "tensor"),
            P("tensor", "dp"),
            P("tensor", None),
            P("tensor", "dp"),
            P("tensor", "dp"),
            P("dp"),
            P("dp"),
            P("dp", "tensor"),
            P("dp", "tensor"),
            P("tensor", "dp"),
        ),
        check_vma=False,
    )
```

```python
import functools
import math

import jax
import jax.numpy as jnp
from jax import lax
from jax.experimental import pallas as pl
from jax.experimental.pallas import tpu as pltpu
from jax.sharding import PartitionSpec as P

HD = 64


norm_eps = 1e-06
rope_base = 1000000.0


def layout(lengths, row_total):
    doc_ends = jnp.cumsum(lengths)
    places = jnp.arange(row_total, dtype=jnp.int32)
    passed = (places[:, None] >= doc_ends[None, :]).astype(jnp.int32)
    begins = jnp.sum(passed * lengths[None, :], axis=1)
    alive = places < doc_ends[-1]
    return (places - begins, alive)


def rotary(positions, width):
    half_width = width // 2
    inv_freq = jnp.exp(
        jnp.arange(half_width, dtype=jnp.float32) * (-2.0 * math.log(rope_base) / width)
    )
    angles = inv_freq[:, None] * positions.astype(jnp.float32)[None, :]
    return (jnp.cos(angles), jnp.sin(angles))


def norm_back(inputs, factor, gain, upstream):
    scaled = upstream * gain
    return factor * scaled - inputs * factor**3 * jnp.mean(scaled * inputs, axis=-1, keepdims=True)


def swap_tensor(rows):
    size = lax.axis_size("tensor")
    return lax.ppermute(rows, "tensor", [(i, i ^ 1) for i in range(size)])


def swap_dp(rows, bit):
    size = lax.axis_size("dp")
    return lax.ppermute(rows, "dp", [(i, i ^ (1 << bit)) for i in range(size)])


def after(value, *others):
    return lax.optimization_barrier((value, *others))[0]


def dest_columns(width, order, fixed=(), extra=0):
    steps = len(order)
    block = width >> (steps + len(fixed))
    whole = block + extra
    count = whole << steps
    own = lax.axis_index("dp")
    places = jnp.arange(count, dtype=jnp.int32)
    spot = places // whole
    flip = jnp.zeros_like(spot)
    for j, bit in enumerate(order):
        flip = flip + (((spot >> (steps - 1 - j)) & 1) << bit)
    within = places % whole
    source = jnp.where(within < block, (own ^ flip) * block + within, -1)
    chosen = (source[:, None] == jnp.arange(width, dtype=jnp.int32)[None, :]).astype(jnp.bfloat16)
    return chosen[: count // 2], chosen[count // 2 :]


def finish(keep, send, order):
    for bit in order[:-1]:
        sent = swap_dp(send, bit)
        half = sent.shape[0] // 2
        send = keep[half:] + sent[half:]
        keep = keep[:half] + sent[:half]
    return keep + swap_dp(send, order[-1])


def close(keep, sent, order):
    return finish(*step_on(keep, sent), order) if order else keep + sent


def step_on(keep, sent):
    half = sent.shape[0] // 2
    return keep[:half] + sent[:half], keep[half:] + sent[half:]


IN_VMEM = pl.BlockSpec(memory_space=pltpu.VMEM)
LIMIT = 11
EXTRA = 8
ROWS = 128
CUTS = 4
ATTN_CUTS = 4


def contract(left, right, left_dim, right_dim):
    return lax.dot_general(
        left, right, (((left_dim,), (right_dim,)), ((), ())), preferred_element_type=jnp.float32
    )


def over(total, size, step):
    count, rest = divmod(total, size)

    def turn(i, carry):
        step(pl.multiple_of(i * size, size), size)
        return carry

    lax.fori_loop(0, count, turn, 0)
    if rest:
        step(count * size, rest)


def call(kernel, name, shapes, *operands, scratch=()):
    return pl.pallas_call(
        kernel,
        in_specs=[IN_VMEM] * len(operands),
        out_specs=[IN_VMEM] * len(shapes),
        out_shape=[jax.ShapeDtypeStruct(shape, dtype) for shape, dtype in shapes],
        compiler_params=pltpu.CompilerParams(vmem_limit_bytes=LIMIT * 2**20),
        cost_estimate=pl.CostEstimate(flops=1000, bytes_accessed=1000, transcendentals=0),
        scratch_shapes=[pltpu.VMEM(shape, dtype) for shape, dtype in scratch],
        name=name,
    )(*operands)


def turn(pairs, cosine, sine_table):
    half = pairs.shape[0] // 2
    front, back = pairs[:half], pairs[half:]
    return jnp.concatenate([front * cosine - back * sine_table, back * cosine + front * sine_table], axis=0)


def blocks_of(begins_ref, row_total):
    size = row_total // 2
    for first in range(0, row_total, size):
        keys = first + size
        key_place = lax.broadcasted_iota(jnp.int32, (keys, size), 0)
        query_place = lax.broadcasted_iota(jnp.int32, (keys, size), 1) + first
        allowed = (key_place >= begins_ref[:, first:keys]) & (key_place <= query_place)
        yield slice(first, keys), keys, allowed


def attend_kernel(
    heads,
    tokens_ref,
    gain_ref,
    weight_ref,
    bias_ref,
    cosine_ref,
    sine_ref,
    begins_ref,
    normed_ref,
    turned_ref,
    mixed_ref,
    mixed_wide_ref,
    top_ref,
    mass_ref,
    pre_ref,
    mixed_across_ref,
):

    def norm(start):
        rows = pl.ds(start, ROWS)
        inputs = tokens_ref[rows, :].astype(jnp.float32)
        factor = lax.rsqrt(jnp.mean(inputs * inputs, axis=-1, keepdims=True) + norm_eps)
        normed_ref[rows, :] = (inputs * factor * gain_ref[...]).astype(jnp.bfloat16)

    row_blocks(tokens_ref.shape[0], norm)
    pre_ref[...] = contract(weight_ref[...], normed_ref[...], 1, 1) + bias_ref[...]
    cosine, sine_table = cosine_ref[...], sine_ref[...]

    def rope(h, carry):
        r = pl.ds(pl.multiple_of(h * HD, HD), HD)
        turned_ref[r, :] = turn(pre_ref[r, :], cosine, sine_table).astype(jnp.bfloat16)
        return carry

    lax.fori_loop(0, heads + 1, rope, 0)
    value_rows = pre_ref[(heads + 1) * HD :, :].astype(jnp.bfloat16)
    turned_ref[(heads + 1) * HD :, :] = value_rows
    key_rows = turned_ref[heads * HD : (heads + 1) * HD, :].astype(jnp.float32).T.astype(jnp.bfloat16)
    blocks = list(blocks_of(begins_ref, tokens_ref.shape[0]))

    def head(h, carry):
        r = pl.ds(pl.multiple_of(h * HD, HD), HD)
        for cols, keys, allowed in blocks:
            scores = contract(key_rows[:keys], turned_ref[r, cols], 1, 0) * HD ** (-0.5)
            scores = jnp.where(allowed, scores, -1e30)
            top = jnp.max(scores, axis=0, keepdims=True)
            exp_scores = jnp.exp(scores - top)
            mass = 1.0 / jnp.sum(exp_scores, axis=0, keepdims=True)
            low_probs = (exp_scores * mass).astype(jnp.bfloat16)
            mixed_across_ref[r, cols] = contract(value_rows[:, :keys], low_probs, 1, 0)
            top_ref[pl.ds(h, 1), cols] = top
            mass_ref[pl.ds(h, 1), cols] = mass
        return carry

    lax.fori_loop(0, heads, head, 0)
    mixed_wide_ref[...] = mixed_across_ref[: heads * HD, :].astype(jnp.bfloat16).astype(jnp.float32)
    mixed_ref[...] = mixed_across_ref[...].T[:, : heads * HD].astype(jnp.bfloat16)


def project_kernel(
    first_ref,
    tokens_ref,
    mixed_ref,
    other_ref,
    o_ref,
    same_ref,
    cross_ref,
    gain_ref,
    residual_ref,
    two_ref,
    low_ref,
    high_ref,
    o_other_ref,
):
    first = first_ref[...] == 0.0
    o_half = same_ref.shape[0]
    same, cross = same_ref[...], cross_ref[...]
    o_other_ref[:o_half, :] = jnp.where(first, same, cross).astype(jnp.bfloat16)
    o_other_ref[o_half:, :] = jnp.where(first, cross, same).astype(jnp.bfloat16)
    half = low_ref.shape[0]
    for rows, wide_ref in ((slice(0, half), low_ref), (slice(half, 2 * half), high_ref)):
        other = other_ref[:, rows].T.astype(jnp.bfloat16)
        residual = tokens_ref[rows, :].astype(jnp.float32) + (
            contract(mixed_ref[rows, :], o_ref[...], 1, 0) + contract(other, o_other_ref[...], 1, 0)
        )
        residual_ref[rows, :] = residual
        factor = lax.rsqrt(jnp.mean(residual * residual, axis=-1, keepdims=True) + norm_eps)
        two = (residual * factor * gain_ref[...]).astype(jnp.bfloat16)
        two_ref[rows, :] = two
        wide_ref[...] = two.astype(jnp.float32)


def row_blocks(count, step):
    def turn_on(i, carry):
        step(pl.multiple_of(i * ROWS, ROWS))
        return carry

    lax.fori_loop(0, count // ROWS, turn_on, 0)


def norm_back_kernel(*refs):
    part_refs, x_refs = refs[:2], refs[2:4]
    residual_ref, gain_ref, branch_ref, grad_ref, grad_low_ref, gain_grad_ref = refs[4:]
    gain_grad_ref[...] = jnp.zeros(gain_grad_ref.shape, jnp.float32)
    first = 0
    for part_ref, x_ref in zip(part_refs, x_refs):

        def step(start, part_ref=part_ref, x_ref=x_ref, first=first):
            here, rows = pl.ds(start, ROWS), pl.ds(first + start, ROWS)
            residual = residual_ref[rows, :]
            upstream = part_ref[here, :] + x_ref[here, :]
            factor = lax.rsqrt(jnp.mean(residual * residual, axis=-1, keepdims=True) + norm_eps)
            gain_grad_ref[...] += jnp.sum(upstream * (residual * factor), axis=0, keepdims=True)
            grad = norm_back(residual, factor, gain_ref[...], upstream) + branch_ref[rows, :].astype(jnp.float32)
            grad_ref[rows, :] = grad
            grad_low_ref[rows, :] = grad.astype(jnp.bfloat16)

        row_blocks(part_ref.shape[0], step)
        first += part_ref.shape[0]


def tokens_back_kernel(
    tokens_ref, low_ref, high_ref, low_x_ref, high_x_ref, gain_ref, residual_ref, out_grad_ref, alive_ref, grad_ref
):
    half = low_ref.shape[0]
    for first, part_ref, x_ref in ((0, low_ref, low_x_ref), (half, high_ref, high_x_ref)):

        def step(start, part_ref=part_ref, x_ref=x_ref, first=first):
            here, rows = pl.ds(start, ROWS), pl.ds(first + start, ROWS)
            inputs = tokens_ref[rows, :].astype(jnp.float32)
            factor = lax.rsqrt(jnp.mean(inputs * inputs, axis=-1, keepdims=True) + norm_eps)
            grad = norm_back(inputs, factor, gain_ref[...], part_ref[here, :] + x_ref[here, :])
            upstream = out_grad_ref[rows, :].astype(jnp.float32)
            total = upstream * (1.0 - alive_ref[rows, :]) + residual_ref[rows, :] + grad
            grad_ref[rows, :] = total.astype(jnp.bfloat16)

        row_blocks(half, step)


def attend_back_kernel(
    heads,
    residual_ref,
    o_ref,
    weight_ref,
    turned_ref,
    top_ref,
    mass_ref,
    cosine_ref,
    sine_ref,
    begins_ref,
    tokens_ref,
    rows_ref,
    low_ref,
    high_ref,
    gain_grad_ref,
    mixed_ref,
    across_ref,
    key_ref,
    value_ref,
):
    mixed_ref[...] = contract(o_ref[...], residual_ref[...], 1, 1).astype(jnp.bfloat16)
    cosine, sine_table = cosine_ref[...], -sine_ref[...]
    k, v = heads * HD, (heads + 1) * HD
    keys_across = turned_ref[k:v, :]
    key_rows = keys_across.astype(jnp.float32).T.astype(jnp.bfloat16)
    value_rows = turned_ref[v:, :].astype(jnp.float32).T.astype(jnp.bfloat16)
    blocks = list(blocks_of(begins_ref, residual_ref.shape[0]))
    key_ref[...] = jnp.zeros(key_ref.shape, jnp.float32)
    value_ref[...] = jnp.zeros(value_ref.shape, jnp.float32)

    def head(h, carry):
        r = pl.ds(pl.multiple_of(h * HD, HD), HD)
        for cols, keys, allowed in blocks:
            query, grad = turned_ref[r, cols], mixed_ref[r, cols]
            scores = contract(key_rows[:keys], query, 1, 0) * HD ** (-0.5)
            scores = jnp.where(allowed, scores, -1e30)
            probs = jnp.exp(scores - top_ref[pl.ds(h, 1), cols]) * mass_ref[pl.ds(h, 1), cols]
            prob_grad = contract(value_rows[:keys], grad, 1, 0)
            inner_sum = jnp.sum(probs * prob_grad, axis=0, keepdims=True)
            score_grad = (probs * (prob_grad - inner_sum)).astype(jnp.bfloat16)
            query_grad = contract(keys_across[:, :keys], score_grad, 1, 0) * HD ** (-0.5)
            across_ref[r, cols] = turn(query_grad, cosine[:, cols], sine_table[:, cols])
            key_ref[:keys, :] += contract(score_grad, query, 1, 1)
            value_ref[:keys, :] += contract(probs.astype(jnp.bfloat16), grad, 1, 1)
        return carry

    lax.fori_loop(0, heads, head, 0)
    across_ref[k:v, :] = turn(key_ref[...].T * HD ** (-0.5), cosine, sine_table)
    across_ref[v : v + HD, :] = value_ref[...].T
    rows_ref[...] = across_ref[...].T[:, : v + HD].astype(jnp.bfloat16)

    def step(start, size):
        c = pl.ds(start, size)
        part = contract(rows_ref[...], weight_ref[:, c], 1, 0)
        put((low_ref, high_ref), part, c)
        gain_grad_ref[:, c] = jnp.sum(part * (tokens_ref[:, c].astype(jnp.float32) * factor), axis=0, keepdims=True)

    inputs = tokens_ref[...].astype(jnp.float32)
    factor = lax.rsqrt(jnp.mean(inputs * inputs, axis=-1, keepdims=True) + norm_eps)
    over(low_ref.shape[1], 256, step)


def ffn_kernel(*refs):
    if len(refs) == 12:
        side_ref, mine_ref, other_ref, branch_ref, *refs, two_ref, branch_low_ref = refs
        gate_ref, up_ref, down_ref, hidden_ref, gate_rows_ref, up_rows_ref = refs
        half = mine_ref.shape[0]
        first = side_ref[...] == 0.0
        mine, other = mine_ref[...], other_ref[...]
        two_ref[:half, :] = jnp.where(first, mine, other).astype(jnp.bfloat16)
        two_ref[half:, :] = jnp.where(first, other, mine).astype(jnp.bfloat16)
        branch_low_ref[...] = branch_ref[...].astype(jnp.bfloat16)
        low_refs, branch_ref = (), branch_low_ref
    else:
        two_ref, branch_ref, gate_ref, up_ref, down_ref, hidden_ref, gate_rows_ref, up_rows_ref, *low_refs = refs
    if low_refs:
        for wide_ref, low_ref in zip((two_ref, branch_ref), low_refs):
            low_ref[...] = wide_ref[...].astype(jnp.bfloat16)
        two_ref, branch_ref = low_refs

    def step(start, size):
        c = pl.ds(start, size)
        gate = contract(two_ref[...], gate_ref[:, c], 1, 0)
        up = contract(two_ref[...], up_ref[:, c], 1, 0)
        hidden_grad = contract(branch_ref[...], down_ref[c, :], 1, 1)
        sigmoid_gate = 0.5 * jnp.tanh(0.5 * gate) + 0.5
        silu_gate = gate * sigmoid_gate
        hidden_ref[:, c] = (silu_gate * up).astype(jnp.bfloat16)
        gate_rows_ref[:, c] = (hidden_grad * up * (sigmoid_gate + silu_gate * (1.0 - sigmoid_gate))).astype(jnp.bfloat16)
        up_rows_ref[:, c] = (hidden_grad * silu_gate).astype(jnp.bfloat16)

    over(gate_ref.shape[1], 768, step)


def ffn_rows(rows, branch, *weights):
    wide = ((branch.shape[0], weights[0].shape[1]), jnp.bfloat16)
    low = [(branch.shape, jnp.bfloat16)] * 2 if branch.dtype == jnp.float32 else []
    return call(ffn_kernel, "ffn_rows", [wide] * 3 + low, *rows, branch, *weights)


def back_kernel(first, gate_rows_ref, up_rows_ref, gate_ref, up_ref, *part_refs):
    rows = pl.ds(first, len(part_refs) * part_refs[0].shape[0])

    def step(start, size):
        c = pl.ds(start, size)
        total = contract(gate_rows_ref[rows, :], gate_ref[c, :], 1, 1) + contract(
            up_rows_ref[rows, :], up_ref[c, :], 1, 1
        )
        put(part_refs, total, c)

    over(gate_ref.shape[0], 256, step)


def ffn_back(gate_rows, up_rows, gate_weight, up_weight, first, counts):
    shapes = [((count, gate_weight.shape[0]), jnp.float32) for count in counts]
    kernel = functools.partial(back_kernel, first)
    return call(kernel, "ffn_back", shapes, gate_rows, up_rows, gate_weight, up_weight)


def down_kernel(hidden_ref, down_ref, low_ref, high_ref):
    def step(start, size):
        c = pl.ds(start, size)
        put((low_ref, high_ref), contract(hidden_ref[...], down_ref[:, c], 1, 0), c)

    over(down_ref.shape[1], 256, step)


def ffn_down(hidden, down_weight):
    shape = ((hidden.shape[0] // 2, down_weight.shape[1]), jnp.float32)
    return call(down_kernel, "ffn_down", [shape] * 2, hidden, down_weight)


def sums_kernel(pieces, cuts, chosen_ref, *refs):
    rows_refs, feature_refs, refs = refs[:pieces], refs[pieces : 2 * pieces], refs[2 * pieces :]
    picked = [contract(chosen_ref[...], r[...], 1, 1).astype(jnp.bfloat16) for r in rows_refs]

    def step(start, size):
        c = pl.ds(start, size)
        total = sum(contract(p, f[:, c], 1, 0) for p, f in zip(picked, feature_refs))
        if len(refs) == cuts:
            put(refs, total, c)
        else:
            total = total + jnp.concatenate([r[:, c] for r in refs[:cuts]])
            put(refs[cuts:], total, c)

    over(feature_refs[0].shape[1], 640, step)


def put(refs, total, c):
    size = total.shape[0] // len(refs)
    for i, ref in enumerate(refs):
        ref[:, c] = total[i * size : (i + 1) * size]


def outer_sums(chosen, rows, features):
    shape = ((chosen.shape[0] // CUTS, features[0].shape[1]), jnp.float32)
    kernel = functools.partial(sums_kernel, len(rows), CUTS)
    return call(kernel, "outer_sums", [shape] * CUTS, chosen, *rows, *features)


def outer_fold(chosen, rows, features, arrived):
    shape = ((chosen.shape[0] // 2, features[0].shape[1]), jnp.float32)
    kernel = functools.partial(sums_kernel, len(rows), CUTS)
    return call(kernel, "outer_fold", [shape] * 2, chosen, *rows, *features, *arrived)


def swap_cuts(cuts, bit):
    return [swap_dp(cut, bit) for cut in cuts]


def attn_sums_kernel(block, chosen_ref, gains_ref, normed_ref, residual_ref, qkv_ref, mixed_ref, *refs):
    count = chosen_ref.shape[0]
    chosen = chosen_ref[...]
    qkv_width = qkv_ref.shape[1]
    o_start = qkv_width + gains_ref.shape[1]
    ones_row = lax.broadcasted_iota(jnp.int32, (count, normed_ref.shape[0]), 0) % (block + EXTRA) == block
    picked = contract(chosen, normed_ref[...], 1, 1)
    picked = jnp.where(ones_row, 1.0, picked).astype(jnp.bfloat16)
    gains = jnp.dot(
        chosen.astype(jnp.float32), gains_ref[...], preferred_element_type=jnp.float32, precision=lax.Precision.HIGHEST
    )
    picked_residual = contract(chosen, residual_ref[...], 1, 1).astype(jnp.bfloat16)
    total = jnp.concatenate(
        [
            contract(picked, qkv_ref[...], 1, 0),
            gains,
            contract(picked_residual, mixed_ref[...], 1, 0),
            jnp.zeros((count, -mixed_ref.shape[1] % 128), jnp.float32),
        ],
        axis=1,
    )
    if len(refs) == ATTN_CUTS:
        put(refs, total, slice(None))
    else:
        total = total + jnp.concatenate([r[...] for r in refs[:ATTN_CUTS]])
        put(refs[ATTN_CUTS:], total, slice(None))


def attn_sums(block, chosen, gains, normed, residual_low, qkv_rows, mixed, arrived=None):
    count = chosen.shape[0]
    features = qkv_rows.shape[1] + gains.shape[1] + -(-mixed.shape[1] // 128) * 128
    kernel = functools.partial(attn_sums_kernel, block)
    operands = (chosen, gains, normed, residual_low, qkv_rows, mixed)
    if arrived is None:
        return call(kernel, "attn_sums", [((count // ATTN_CUTS, features), jnp.float32)] * ATTN_CUTS, *operands)
    return call(kernel, "attn_fold", [((count // 2, features), jnp.float32)] * 2, *operands, *arrived)


def on_device(
    tokens,
    out_grad,
    doc_lengths,
    q_weight,
    k_weight,
    v_weight,
    q_bias,
    k_bias,
    v_bias,
    o_weight,
    attn_gain,
    ffn_gain,
    gate_weight,
    up_weight,
    down_weight,
):
    row_total, width = tokens.shape
    local_heads = q_weight.shape[1] // HD
    local_kv = k_weight.shape[1] // HD
    dp_size = lax.axis_size("dp")
    dp_bits = dp_size.bit_length() - 1
    pair_bit = 2
    ffn_order = (0, 1) + tuple(range(3, dp_bits))
    attn_order = (0, 1, pair_bit) + tuple(range(3, dp_bits))
    own = lax.axis_index("dp")
    positions, alive = layout(doc_lengths[0], row_total)
    cosine, sine_table = rotary(positions, HD)
    alive_rows = alive.astype(jnp.float32)[:, None]
    places = jnp.arange(row_total, dtype=jnp.int32)
    o_half = o_weight.shape[0] // 2
    o_first = own & 1
    upstream = out_grad.astype(jnp.float32)
    branch_wide = upstream * alive_rows
    o_mine = lax.dynamic_slice_in_dim(o_weight, o_first * o_half, o_half).astype(jnp.float32)
    o_same = swap_tensor(o_mine)
    half_rows = row_total // 2
    pair_branch = swap_dp(branch_wide, pair_bit)
    ffn_keep, ffn_send = dest_columns(width, ffn_order, (pair_bit,))
    attn_keep, attn_send = dest_columns(width, attn_order, extra=EXTRA)
    branch_grad = branch_wide.astype(jnp.bfloat16)
    inputs = tokens.astype(jnp.float32)
    gain_one = attn_gain.astype(jnp.float32)
    gain_two = ffn_gain.astype(jnp.float32)
    qkv_across = jnp.concatenate([q_weight.T, k_weight.T, v_weight.T])
    qkv_bias = jnp.concatenate([q_bias.reshape(-1), k_bias.reshape(-1), v_bias.reshape(-1)]).astype(jnp.float32)
    q_width = local_heads * HD
    k_width = local_kv * HD
    qkv_width = q_width + 2 * k_width
    begins = (places - positions)[None, :]
    padded = -(-qkv_width // 128) * 128
    row_stats = ((-(-local_heads // 8) * 8, row_total), jnp.float32)
    normed, turned, mixed_heads, mixed_wide, top_score, mass = call(
        functools.partial(attend_kernel, local_heads),
        "attend",
        [
            ((row_total, width), jnp.bfloat16),
            ((qkv_width, row_total), jnp.bfloat16),
            ((row_total, q_width), jnp.bfloat16),
            ((q_width, row_total), jnp.float32),
            row_stats,
            row_stats,
        ],
        tokens,
        gain_one[None, :],
        qkv_across,
        qkv_bias[:, None],
        cosine,
        sine_table,
        begins,
        scratch=[((qkv_width, row_total), jnp.float32), ((-(-q_width // 128) * 128, row_total), jnp.float32)],
    )
    mixed_other = swap_tensor(after(mixed_wide, o_same))
    o_same = after(o_same, mixed_heads)
    o_cross = swap_dp(o_same, 0)
    residual, normed_two, low_wide, high_wide = call(
        project_kernel,
        "project",
        [
            ((row_total, width), jnp.float32),
            ((row_total, width), jnp.bfloat16),
            ((half_rows, width), jnp.float32),
            ((half_rows, width), jnp.float32),
        ],
        jnp.broadcast_to(o_first.astype(jnp.float32), (1, width)),
        tokens,
        mixed_heads,
        after(mixed_other, o_cross, ffn_keep, ffn_send, attn_keep, attn_send, branch_grad),
        o_weight,
        o_same,
        o_cross,
        gain_two[None, :],
        scratch=[((q_width, width), jnp.bfloat16)],
    )
    side = jnp.broadcast_to(lax.axis_index("tensor").astype(jnp.float32), (1, width))
    quarter = half_rows // 2
    mine = jnp.where(side == 0.0, low_wide[:quarter], low_wide[quarter:])
    low_mine = swap_dp(mine, pair_bit)
    high_two = swap_dp(high_wide, pair_bit)
    ffn_weights = (gate_weight, up_weight, down_weight)

    hidden_act, gate_grad_rows, up_grad_rows = ffn_rows([normed_two], branch_grad, *ffn_weights)
    backward = (up_grad_rows, gate_weight, up_weight)
    (low_part,) = ffn_back(after(gate_grad_rows, pair_branch, low_mine), *backward, 0, [half_rows])
    low_swapped = swap_tensor(after(low_mine, gate_grad_rows))
    (high_part,) = ffn_back(after(gate_grad_rows, low_part), *backward, half_rows, [half_rows])
    low_from_x = swap_tensor(after(low_part, low_swapped, high_part))
    low_branch, high_branch = pair_branch[:half_rows], pair_branch[half_rows:]
    low_hidden, low_gate, low_up, low_two, low_branch = ffn_rows(
        [side, low_mine, after(low_swapped, high_part)], low_branch, *ffn_weights
    )
    high_from_x = swap_tensor(after(high_part, low_from_x))
    high_hidden, high_gate, high_up, high_two, high_branch = ffn_rows(
        [after(high_two, low_hidden)], high_branch, *ffn_weights
    )
    branch_rows = (branch_grad, low_branch, high_branch)
    two_rows = (normed_two, low_two, high_two)
    down_sums = outer_sums(ffn_send, branch_rows, (hidden_act, low_hidden, high_hidden))
    down_sent = swap_cuts(down_sums, 0)
    low_down, high_down = ffn_down(after(hidden_act, *down_sums), down_weight)
    gate_sums = outer_sums(after(ffn_send, low_from_x, low_down), two_rows, (gate_grad_rows, low_gate, high_gate))
    gate_sent = swap_cuts(gate_sums, 0)
    up_sums = outer_sums(after(ffn_send, *gate_sums), two_rows, (up_grad_rows, low_up, high_up))
    up_sent = swap_cuts(up_sums, 0)
    down_keep, down_send = outer_fold(
        after(ffn_keep, *up_sums), branch_rows, (hidden_act, low_hidden, high_hidden), down_sent
    )
    gate_keep, gate_send = outer_fold(
        after(ffn_keep, down_send), two_rows, (gate_grad_rows, low_gate, high_gate), gate_sent
    )
    up_keep, up_send = outer_fold(after(ffn_keep, gate_send), two_rows, (up_grad_rows, low_up, high_up), up_sent)
    down_from_y, gate_from_y, up_from_y = (swap_dp(v, ffn_order[1]) for v in (down_send, gate_send, up_send))
    wide, low = ((row_total, width), jnp.float32), ((row_total, width), jnp.bfloat16)
    gain_row = ((1, width), jnp.float32)
    residual_grad, residual_low, ffn_gain_sum = call(
        norm_back_kernel,
        "norm_back",
        [wide, low, gain_row],
        low_part,
        high_part,
        low_from_x,
        after(high_from_x, up_send),
        residual,
        gain_two[None, :],
        branch_grad,
    )
    down_keep, down_send = step_on(down_keep, after(down_from_y, residual_low))
    residual_low = after(residual_low, down_send)
    down_from_z = swap_dp(down_send, ffn_order[2])
    half_wide = ((half_rows, width), jnp.float32)
    qkv_grad_rows, low_normed, high_normed, attn_gain_part = call(
        functools.partial(attend_back_kernel, local_heads),
        "attend_back",
        [((row_total, qkv_width), jnp.bfloat16), half_wide, half_wide, gain_row],
        residual_low,
        o_weight,
        qkv_across,
        turned,
        top_score,
        mass,
        cosine,
        sine_table,
        begins,
        tokens,
        scratch=[
            ((q_width, row_total), jnp.bfloat16),
            ((padded, row_total), jnp.float32),
            ((row_total, HD), jnp.float32),
            ((row_total, HD), jnp.float32),
        ],
    )
    gain_sums = jnp.concatenate([attn_gain_part + swap_tensor(attn_gain_part), ffn_gain_sum])
    low_other = swap_tensor(after(low_normed, gain_sums))
    high_other = swap_tensor(after(high_normed, gain_sums))
    gain_columns = jnp.pad(gain_sums, ((0, -qkv_width % 128 - 2), (0, 0))).T
    attn_operands = (gain_columns, normed, residual_low, qkv_grad_rows, mixed_heads)
    gain_block = width // dp_size
    attn_sent = swap_cuts(
        attn_sums(gain_block, after(attn_send, down_from_z), *attn_operands), attn_order[0]
    )
    gate_keep, gate_send = step_on(gate_keep, gate_from_y)
    gate_from_z = swap_dp(gate_send, ffn_order[2])
    attn_part, attn_next = attn_sums(
        gain_block, after(attn_keep, gate_send, low_other), *attn_operands, attn_sent
    )
    attn_from_z = swap_dp(attn_next, attn_order[1])
    low_down_x = swap_tensor(after(low_down, attn_next))
    high_down_x = swap_tensor(after(high_down, attn_next))
    up_keep, up_send = step_on(up_keep, after(up_from_y, attn_next, low_other))
    up_from_z = swap_dp(up_send, ffn_order[2])
    attn_part, attn_next = step_on(attn_part, after(attn_from_z, up_send))
    attn_from_y = swap_dp(attn_next, attn_order[2])
    attn_part, attn_next = step_on(attn_part, after(attn_from_y, gate_from_z))
    attn_from_z = swap_dp(after(attn_next, up_from_z), attn_order[3])
    attn_grad = close(attn_part, attn_from_z, attn_order[4:])
    (tokens_grad,) = call(
        tokens_back_kernel,
        "tokens_back",
        [low],
        tokens,
        low_normed,
        high_normed,
        low_other,
        after(high_other, up_send),
        gain_one[None, :],
        residual_grad,
        out_grad,
        alive_rows,
    )
    high_down_x = after(high_down_x, attn_next)
    block_out = residual + jnp.concatenate([low_down + low_down_x, high_down + high_down_x])
    o_start = -(-qkv_width // 128) * 128
    qkv_grad, o_grad = attn_grad[:gain_block, :qkv_width], attn_grad[:gain_block, o_start : o_start + q_width]
    attn_gain_grad, ffn_gain_grad = attn_grad[:gain_block, qkv_width], attn_grad[:gain_block, qkv_width + 1]
    bias_heads = attn_grad[gain_block, :qkv_width].reshape(local_heads + 2 * local_kv, HD)
    bias_block = HD // dp_size
    bias_own = lax.dynamic_slice_in_dim(bias_heads, own * bias_block, bias_block, axis=1)
    down_grad, gate_grad, up_grad = (
        close(keep, got, ffn_order[3:])
        for keep, got in ((down_keep, down_from_z), (gate_keep, gate_from_z), (up_keep, up_from_z))
    )
    layer_out = jnp.where(alive[:, None], block_out, inputs).astype(jnp.bfloat16)
    return (
        layer_out,
        tokens_grad,
        qkv_grad[:, :q_width],
        qkv_grad[:, q_width : q_width + k_width],
        qkv_grad[:, q_width + k_width :],
        bias_own[:local_heads],
        bias_heads[local_heads : local_heads + local_kv],
        bias_own[local_heads + local_kv :],
        o_grad.T,
        attn_gain_grad,
        ffn_gain_grad,
        gate_grad,
        up_grad,
        down_grad.T,
    )


def solution(mesh):
    return jax.shard_map(
        on_device,
        mesh=mesh,
        in_specs=(
            P("dp", None),
            P("dp", None),
            P("dp", None),
            P(None, "tensor"),
            P(None, "tensor"),
            P(None, "tensor"),
            P("tensor", None),
            P("tensor", None),
            P("tensor", None),
            P("tensor", None),
            P(),
            P(),
            P(None, "tensor"),
            P(None, "tensor"),
            P("tensor", None),
        ),
        out_specs=(
            P("dp", None),
            P("dp", None),
            P("dp", "tensor"),
            P("dp", "tensor"),
            P("dp", "tensor"),
            P("tensor", "dp"),
            P("tensor", None),
            P("tensor", "dp"),
            P("tensor", "dp"),
            P("dp"),
            P("dp"),
            P("dp", "tensor"),
            P("dp", "tensor"),
            P("tensor", "dp"),
        ),
        check_vma=False,
    )
```
